32 devices in a mesh: gx: 4 (over x, core), gy: 8 (over z, y).
Axes of the slice: x: 2, y: 2, z: 4, core: 2. Of those that a mesh axis runs over, the one named last changes fastest.
Arguments:
- tokens: bfloat16 [2740, 1024], P('gx', 'gy'), may hold values from -64 to 64
- cotangent: bfloat16 [2740, 1024], P('gx', 'gy'), may hold values from -6 to 6
- norm1_gain: float32 [1024], P('gy'), may hold values from 0.1 to 1.9
- norm1_shift: float32 [1024], P('gy'), may hold values from -1.5 to 1.5
- qkv_weight: bfloat16 [1024, 3072], P('gx', 'gy'), may hold values from -4 to 4
- qv_bias: float32 [2048], P('gy'), may hold values from -2.5 to 2.5
- proj_weight: bfloat16 [1024, 1024], P('gx', 'gy'), may hold values from -1.5 to 1.5
- proj_bias: float32 [1024], P('gy'), may hold values from -1.5 to 1.5
- scale_attn: float32 [1024], P('gy'), may hold values from 0.3 to 1.5
- norm2_gain: float32 [1024], P('gy'), may hold values from 0.1 to 1.9
- norm2_shift: float32 [1024], P('gy'), may hold values from -1.5 to 1.5
- fc1_weight: bfloat16 [1024, 4096], P('gx', 'gy'), may hold values from -0.1875 to 0.1875
- fc1_bias: float32 [4096], P('gy'), may hold values from -2.5 to 2.5
- fc2_weight: bfloat16 [4096, 1024], P('gx', 'gy'), may hold values from -0.09375 to 0.09375
- fc2_bias: float32 [1024], P('gy'), may hold values from -1.5 to 1.5
- scale_mlp: float32 [1024], P('gy'), may hold values from 0.3 to 1.5
Outputs:
- output: float32 [2740, 1024], P('gx', 'gy')
- grad_tokens: float32 [2740, 1024], P('gx', 'gy')
- grad_norm1_gain: float32 [1024], P('gy')
- grad_norm1_shift: float32 [1024], P('gy')
- grad_qkv_weight: float32 [1024, 3072], P('gx', 'gy')
- grad_qv_bias: float32 [2048], P('gy')
- grad_proj_weight: float32 [1024, 1024], P('gx', 'gy')
- grad_proj_bias: float32 [1024], P('gy')
- grad_scale_attn: float32 [1024], P('gy')
- grad_norm2_gain: float32 [1024], P('gy')
- grad_norm2_shift: float32 [1024], P('gy')
- grad_fc1_weight: float32 [1024, 4096], P('gx', 'gy')
- grad_fc1_bias: float32 [4096], P('gy')
- grad_fc2_weight: float32 [4096, 1024], P('gx', 'gy')
- grad_fc2_bias: float32 [1024], P('gy')
- grad_scale_mlp: float32 [1024], P('gy')
The draws below stay inside these ranges and needn't reach their ends.
All inputs are finite; a program needn't handle non-finite values.
Results may differ from the reference program's by a relative error of at most 0.012.
Values may be sent and summed in bfloat16 or wider, within the bound.
A program may use at most 128 MiB of HBM per device.

```python
import math
import jax
import jax.numpy as jnp
from jax import lax

D = 1024
HEADS = 16
HD = 64
FF = 4096
SEQ = 1370
IMGS = 1
TOKENS = 2740


def draw_tokens(key, part):
    subkeys = jax.random.split(key, 3)
    lowest = math.log(0.4)
    highest = math.log(4.0)
    row_scale = jnp.exp(jax.random.uniform(subkeys[0], (TOKENS, 1), jnp.float32, lowest, highest))
    col_scale = jnp.exp(jax.random.uniform(subkeys[1], (1, D), jnp.float32, lowest, highest))
    sample = jnp.clip(jax.random.normal(subkeys[2], (TOKENS, D), jnp.float32), -4.0, 4.0)
    return (sample * row_scale * col_scale).astype(jnp.bfloat16)


def draw_qkv_weight(key, part):
    subkeys = jax.random.split(key, 1)
    sample = jnp.clip(jax.random.normal(subkeys[0], (D, HEADS, 3, HD), jnp.float32), -4.0, 4.0) * D ** (-0.5)
    return jnp.clip(sample, -4.0, 4.0).reshape(D, 3 * D).astype(jnp.bfloat16)


def shard_levels(own_key, extent, pieces, smallest, high):
    loudness, own = 1.0, jax.random.fold_in(own_key, 6)
    for axis_at, shards_of in pieces:
        steps = jnp.exp(jax.random.uniform(jax.random.fold_in(own, axis_at), (shards_of,), jnp.float32, smallest / len(pieces), high / len(pieces)))
        loudness = loudness * jnp.repeat(steps, extent[axis_at] // shards_of).reshape([-1 if axis == axis_at else 1 for axis in range(len(extent))])
    return loudness


def centred(key, dims, width, most, cuts=(), kind=jnp.bfloat16):
    drawn = width * jax.random.normal(key, dims, jnp.float32)
    if cuts:
        drawn = drawn * shard_levels(key, dims, cuts, -0.22, 0.18)
    return jnp.clip(drawn, -most, most).astype(kind)


def setup_inputs(seed: int = 0) -> dict:
    splits = jax.random.split(jax.random.key(seed), 17)
    tokens = draw_tokens(jax.random.fold_in(splits[16], 71), 0)
    cotangent = centred(splits[1], (TOKENS, D), 1.0, 6.0, ((0, 4), (1, 8)))
    norm1_gain = jnp.clip(1.0 + 0.18 * jax.random.normal(splits[2], (D,), jnp.float32), 0.1, 1.9)
    norm1_shift = centred(splits[3], (D,), 0.3, 1.5, ((0, 8),), jnp.float32)
    qkv_weight = draw_qkv_weight(jax.random.fold_in(splits[16], 71), 0)
    qv_bias = centred(splits[5], (2 * D,), 0.5, 2.5, ((0, 8),), jnp.float32)
    proj_weight = centred(splits[6], (D, D), (HD // 4) ** -0.5, 1.5, ((0, 4), (1, 8)))
    proj_bias = centred(splits[7], (D,), 0.3, 1.5, ((0, 8),), jnp.float32)
    scale_attn = jnp.clip(jnp.exp(math.log(1.5) - 1.60943787 * jax.random.uniform(splits[8], (D,), jnp.float32) ** shard_levels(splits[8], (D,), ((0, 8),), -0.2, 0.2)), 0.3, 1.5)
    norm2_gain = jnp.clip(1.0 + 0.18 * jax.random.normal(splits[9], (D,), jnp.float32), 0.1, 1.9)
    norm2_shift = centred(splits[10], (D,), 0.3, 1.5, ((0, 8),), jnp.float32)
    fc1_weight = centred(splits[11], (D, FF), D ** -0.5, 0.1875, ((0, 4), (1, 8)))
    fc1_bias = centred(splits[12], (FF,), 0.5, 2.5, ((0, 8),), jnp.float32)
    fc2_weight = centred(splits[13], (FF, D), FF ** -0.5, 0.09375, ((0, 4), (1, 8)))
    fc2_bias = centred(splits[14], (D,), 0.3, 1.5, ((0, 8),), jnp.float32)
    scale_mlp = jnp.clip(jnp.exp(math.log(1.5) - 1.60943787 * jax.random.uniform(splits[15], (D,), jnp.float32) ** shard_levels(splits[15], (D,), ((0, 8),), -0.2, 0.2)), 0.3, 1.5)
    return dict(tokens=tokens, cotangent=cotangent, norm1_gain=norm1_gain, norm1_shift=norm1_shift, qkv_weight=qkv_weight, qv_bias=qv_bias, proj_weight=proj_weight, proj_bias=proj_bias, scale_attn=scale_attn, norm2_gain=norm2_gain, norm2_shift=norm2_shift, fc1_weight=fc1_weight, fc1_bias=fc1_bias, fc2_weight=fc2_weight, fc2_bias=fc2_bias, scale_mlp=scale_mlp)


EPS = 1e-06
ROOT_HALF = 0.7071067811865476
INV_ROOT_TAU = 0.3989422804014327

def normal_cdf(values):
    return 0.5 * (1.0 + jax.scipy.special.erf(values * ROOT_HALF))

def gelu_exact(values):
    return values * normal_cdf(values)

def gelu_slope(values):
    return normal_cdf(values) + values * jnp.exp(-0.5 * values * values) * INV_ROOT_TAU

def round_keep(values):
    return lax.optimization_barrier(values.astype(jnp.bfloat16)).astype(jnp.float32)

def to_images(array):
    half_len = SEQ // 2
    groups = array.shape[0] // (2 * IMGS * half_len)
    shaped = array.reshape(groups, 2, IMGS, half_len, array.shape[1])
    return jnp.transpose(shaped, (0, 2, 1, 3, 4)).reshape(array.shape[0], array.shape[1])

def from_images(array):
    half_len = SEQ // 2
    groups = array.shape[0] // (2 * IMGS * half_len)
    shaped = array.reshape(groups, IMGS, 2, half_len, array.shape[1])
    return jnp.transpose(shaped, (0, 2, 1, 3, 4)).reshape(array.shape[0], array.shape[1])

def norm_forward(rows, gain, shift):
    row_mean = lax.optimization_barrier(jnp.mean(rows, axis=1, keepdims=True))
    centered = rows - row_mean
    inv_std = lax.rsqrt(lax.optimization_barrier(jnp.mean(centered * centered, axis=1, keepdims=True)) + EPS)
    normed = centered * inv_std
    return (normed, inv_std, (normed * gain + shift).astype(jnp.bfloat16))

def norm_backward(grad_normed, normed, inv_std, gain):
    scaled = grad_normed * gain
    first = lax.optimization_barrier(jnp.mean(scaled, axis=1, keepdims=True))
    second = lax.optimization_barrier(jnp.mean(scaled * normed, axis=1, keepdims=True))
    return inv_std * (scaled - first - normed * second)

def attend(blocks):
    queries, keys, values = blocks
    scores = jnp.einsum('qhe,khe->hqk', queries.astype(jnp.float32), keys.astype(jnp.float32)) * HD ** (-0.5)
    row_max = lax.optimization_barrier(jnp.max(scores, axis=2, keepdims=True))
    exponent = jnp.exp(scores - row_max)
    totals = lax.optimization_barrier(jnp.sum(exponent, axis=2, keepdims=True))
    probs = round_keep(exponent / totals)
    attended = jnp.einsum('hqk,khe->qhe', probs, values.astype(jnp.float32)).astype(jnp.bfloat16)
    return (attended, row_max + jnp.log(totals))

def attend_back(blocks):
    queries, keys, values, attended, log_total, grad_att = blocks
    scores = jnp.einsum('qhe,khe->hqk', queries.astype(jnp.float32), keys.astype(jnp.float32)) * HD ** (-0.5)
    recomputed = jnp.exp(scores - log_total)
    probs_b = round_keep(recomputed)
    grad_att_f = grad_att.astype(jnp.float32)
    grad_values = jnp.einsum('hqk,qhe->khe', probs_b, grad_att_f)
    grad_probs = jnp.einsum('qhe,khe->hqk', grad_att_f, values.astype(jnp.float32))
    delta = lax.optimization_barrier(jnp.sum(grad_att_f * attended.astype(jnp.float32), axis=2))
    grad_scores = recomputed * (grad_probs - jnp.transpose(delta)[:, :, None])
    grad_scores_b = round_keep(grad_scores)
    grad_queries = jnp.einsum('hqk,khe->qhe', grad_scores_b, keys.astype(jnp.float32)) * HD ** (-0.5)
    grad_keys = jnp.einsum('hqk,qhe->khe', grad_scores_b, queries.astype(jnp.float32)) * HD ** (-0.5)
    return (grad_queries, grad_keys, grad_values)

def reference(tokens, cotangent, norm1_gain, norm1_shift, qkv_weight, qv_bias, proj_weight, proj_bias, scale_attn, norm2_gain, norm2_shift, fc1_weight, fc1_bias, fc2_weight, fc2_bias, scale_mlp):
    count = tokens.shape[0]
    images = count // SEQ
    inputs = to_images(tokens).astype(jnp.float32)
    upstream = to_images(cotangent).astype(jnp.float32)
    normed_one, inv_one, norm_one = norm_forward(inputs, norm1_gain, norm1_shift)
    mixed = jnp.dot(norm_one, qkv_weight, preferred_element_type=jnp.float32).reshape(count, HEADS, 3, HD)
    biases = qv_bias.reshape(HEADS, 2, HD)
    queries = (mixed[:, :, 0] + biases[:, 0]).astype(jnp.bfloat16).reshape(images, SEQ, HEADS, HD)
    keys = mixed[:, :, 1].astype(jnp.bfloat16).reshape(images, SEQ, HEADS, HD)
    values = (mixed[:, :, 2] + biases[:, 1]).astype(jnp.bfloat16).reshape(images, SEQ, HEADS, HD)
    attended, log_total = lax.map(attend, (queries, keys, values))
    attended_flat = attended.reshape(count, D)
    attn_out = jnp.dot(attended_flat, proj_weight, preferred_element_type=jnp.float32) + proj_bias
    middle = inputs + scale_attn * attn_out
    normed_two, inv_two, norm_two = norm_forward(middle, norm2_gain, norm2_shift)
    pre_act = jnp.dot(norm_two, fc1_weight, preferred_element_type=jnp.float32) + fc1_bias
    hidden = gelu_exact(pre_act).astype(jnp.bfloat16)
    mlp_out = jnp.dot(hidden, fc2_weight, preferred_element_type=jnp.float32) + fc2_bias
    output = middle + scale_mlp * mlp_out
    grad_scale_mlp = lax.optimization_barrier(jnp.sum(upstream * mlp_out, axis=0))
    grad_mlp = upstream * scale_mlp
    grad_fc2_bias = lax.optimization_barrier(jnp.sum(grad_mlp, axis=0))
    grad_mlp_b = grad_mlp.astype(jnp.bfloat16)
    grad_fc2 = jnp.dot(hidden.T, grad_mlp_b, preferred_element_type=jnp.float32)
    grad_hidden = jnp.dot(grad_mlp_b, fc2_weight.T, preferred_element_type=jnp.float32)
    grad_pre = grad_hidden * gelu_slope(pre_act)
    grad_fc1_bias = lax.optimization_barrier(jnp.sum(grad_pre, axis=0))
    grad_pre_b = grad_pre.astype(jnp.bfloat16)
    grad_fc1 = jnp.dot(norm_two.T, grad_pre_b, preferred_element_type=jnp.float32)
    grad_norm_two = jnp.dot(grad_pre_b, fc1_weight.T, preferred_element_type=jnp.float32)
    grad_gain_two = lax.optimization_barrier(jnp.sum(grad_norm_two * normed_two, axis=0))
    grad_shift_two = lax.optimization_barrier(jnp.sum(grad_norm_two, axis=0))
    grad_middle = upstream + norm_backward(grad_norm_two, normed_two, inv_two, norm2_gain)
    grad_scale_attn = lax.optimization_barrier(jnp.sum(grad_middle * attn_out, axis=0))
    grad_attn = grad_middle * scale_attn
    grad_proj_bias = lax.optimization_barrier(jnp.sum(grad_attn, axis=0))
    grad_attn_b = grad_attn.astype(jnp.bfloat16)
    grad_proj = jnp.dot(attended_flat.T, grad_attn_b, preferred_element_type=jnp.float32)
    grad_attended = jnp.dot(grad_attn_b, proj_weight.T, preferred_element_type=jnp.float32).astype(jnp.bfloat16)
    grad_queries, grad_keys, grad_values = lax.map(attend_back, (queries, keys, values, attended, log_total, grad_attended.reshape(images, SEQ, HEADS, HD)))
    grad_queries = grad_queries.reshape(count, HEADS, HD)
    grad_keys = grad_keys.reshape(count, HEADS, HD)
    grad_values = grad_values.reshape(count, HEADS, HD)
    grad_qv_bias = jnp.stack([lax.optimization_barrier(jnp.sum(grad_queries, axis=0)), lax.optimization_barrier(jnp.sum(grad_values, axis=0))], axis=1).reshape(2 * D)
    grad_mixed = jnp.stack([grad_queries, grad_keys, grad_values], axis=2).astype(jnp.bfloat16).reshape(count, 3 * D)
    grad_qkv = jnp.dot(norm_one.T, grad_mixed, preferred_element_type=jnp.float32)
    grad_norm_one = jnp.dot(grad_mixed, qkv_weight.T, preferred_element_type=jnp.float32)
    grad_gain_one = lax.optimization_barrier(jnp.sum(grad_norm_one * normed_one, axis=0))
    grad_shift_one = lax.optimization_barrier(jnp.sum(grad_norm_one, axis=0))
    grad_input = grad_middle + norm_backward(grad_norm_one, normed_one, inv_one, norm1_gain)
    return (from_images(output), from_images(grad_input), grad_gain_one, grad_shift_one, grad_qkv, grad_qv_bias, grad_proj, grad_proj_bias, grad_scale_attn, grad_gain_two, grad_shift_two, grad_fc1, grad_fc1_bias, grad_fc2, grad_fc2_bias, grad_scale_mlp)
```

```python
import functools

import jax
import jax.numpy as jnp
from jax import lax
from jax.experimental import pallas as pl
from jax.experimental.pallas import tpu as pltpu
from jax.sharding import PartitionSpec as P

D = 1024
HD = 64
IMGS = 1


EPS = 1e-06
ROOT_HALF = 0.7071067811865476
INV_ROOT_TAU = 0.3989422804014327
SEMS = 256
VMEM_BYTES = 62 * 1024 * 1024


def from_partner(block, axis, bit):
    count = lax.axis_size(axis)
    route = []
    for low in range(count):
        high = low | 1 << bit
        if high != low and high < count:
            route += [(low, high), (high, low)]
    return lax.ppermute(block, axis, route)


def normal_cdf(values):
    return 0.5 * (1.0 + jax.scipy.special.erf(values * ROOT_HALF))


def gelu_exact(values):
    return values * normal_cdf(values)


def gelu_slope(values):
    return normal_cdf(values) + values * jnp.exp(-0.5 * values * values) * INV_ROOT_TAU


def norm_full(rows, gain, shift):
    row_mean = jnp.mean(rows, axis=1, keepdims=True)
    inv_std = lax.rsqrt(jnp.mean(rows * rows, axis=1, keepdims=True) - row_mean * row_mean + EPS)
    normed = (rows - row_mean) * inv_std
    return (normed, inv_std, (normed * gain + shift).astype(jnp.bfloat16))


def gather_columns(block):
    return lax.all_gather(block, "gy", axis=1, tiled=True)


def ring_kernel(parts, block_ref, out_ref, send_sem, recv_sem):
    half = parts // 2

    def index_of(place):
        back = place // half
        return (1 - back) * (2 * place) + back * (2 * (parts - 1 - place) + 1)

    me = lax.axis_index("gy")
    odd = me % 2
    place = (1 - odd) * (me // 2) + odd * (parts - 1 - me // 2)
    sides = (index_of((place + 1) % parts), index_of((place + parts - 1) % parts))
    barrier = pltpu.get_barrier_semaphore()
    for side in sides:
        pl.semaphore_signal(
            barrier, inc=1, device_id={"gy": side}, device_id_type=pl.DeviceIdType.MESH
        )
    pl.semaphore_wait(barrier, 2)
    copies = []
    for step in range(half):
        owners = (
            index_of((place + parts - step) % parts),
            index_of((place + step) % parts),
        )
        started = []
        for way in range(2):
            if way == 1 and step == half - 1:
                continue
            copy = pltpu.make_async_remote_copy(
                src_ref=block_ref if step == 0 else out_ref.at[owners[way]],
                dst_ref=out_ref.at[owners[way]],
                send_sem=send_sem.at[way, step],
                recv_sem=recv_sem.at[way, step],
                device_id={"gy": sides[way]},
                device_id_type=pl.DeviceIdType.MESH,
            )
            copy.start()
            started.append(copy)
        if step == 0:
            out_ref[me] = block_ref[...]
        for copy in started:
            copy.wait_recv()
        copies += started
    for copy in copies:
        copy.wait_send()


def ring_columns(block, call):
    parts = lax.axis_size("gy")
    count, width = block.shape
    if parts % 2 or parts < 4:
        return gather_columns(block)
    got = pl.pallas_call(
        functools.partial(ring_kernel, parts),
        out_shape=jax.ShapeDtypeStruct((parts, count, width), block.dtype),
        in_specs=[pl.BlockSpec(memory_space=pltpu.VMEM)],
        out_specs=pl.BlockSpec(memory_space=pltpu.VMEM),
        scratch_shapes=[
            pltpu.SemaphoreType.DMA((2, parts // 2)),
            pltpu.SemaphoreType.DMA((2, parts // 2)),
        ],
        compiler_params=pltpu.CompilerParams(collective_id=call, has_side_effects=True),
    )(block)
    return jnp.transpose(got, (1, 0, 2)).reshape(count, parts * width)


def spread_columns(block):
    parts = lax.axis_size("gy")
    got = lax.all_to_all(
        jnp.broadcast_to(block[None], (parts,) + block.shape), "gy", 0, 0, tiled=True
    )
    return jnp.transpose(got, (1, 0, 2)).reshape(block.shape[0], parts * block.shape[1])


def column_blocks(block):
    parts = lax.axis_size("gy")
    count, full = block.shape
    return jnp.transpose(block.reshape(count, parts, full // parts), (1, 0, 2))


def scatter_sum(blocks, axis):
    got = lax.all_to_all(blocks, axis, 0, 0, tiled=True)
    return jnp.sum(got.astype(jnp.float32), axis=0)


def own_columns(block, width):
    return lax.dynamic_slice_in_dim(block, lax.axis_index("gy") * width, width, axis=1)


def sum_rows(term):
    parts = lax.axis_size("gx")
    blocks = term.reshape(parts, term.shape[0] // parts, term.shape[1])
    return scatter_sum(blocks, "gx")


def weight_grad_rows(saved, grad_out):
    term = jnp.einsum("tk,tn->kn", saved, grad_out, preferred_element_type=jnp.float32)
    return lax.psum_scatter(
        term.astype(jnp.bfloat16), "gx", scatter_dimension=0, tiled=True
    ).astype(jnp.float32)


def weight_grad(saved, grad_out):
    term = jnp.einsum("tk,tn->kn", saved, grad_out, preferred_element_type=jnp.float32)
    return sum_rows(term.astype(jnp.bfloat16))


def lanes_of(column, width):
    count = column.shape[0]
    lines = -(-count // width)
    return jnp.pad(column, (0, lines * width - count)).reshape(lines, width)


def back_norm(grad_out, weight, normed, normed_own, inv_std, gain, gain_own):
    parts = lax.axis_size("gy")
    count, full = normed.shape
    width = full // parts
    term = jnp.einsum("tn,kn->tk", grad_out, weight, preferred_element_type=jnp.float32)
    scaled = term * gain
    first = lanes_of(jnp.sum(scaled, axis=1), width)
    second = lanes_of(jnp.sum(scaled * normed, axis=1), width)
    lines = first.shape[0]
    sums = jnp.concatenate([first, second], axis=0).astype(jnp.bfloat16)
    blocks = column_blocks(term.astype(jnp.bfloat16))
    sent = jnp.concatenate(
        [blocks, jnp.broadcast_to(sums[None], (parts,) + sums.shape)], axis=1
    )
    back = scatter_sum(sent, "gy")
    grad_normed = back[:count]
    first = back[count : count + lines].reshape(-1)[:count, None]
    second = back[count + lines :].reshape(-1)[:count, None]
    grad_rows = inv_std * (
        grad_normed * gain_own - first / full - normed_own * (second / full)
    )
    return (
        grad_rows,
        jnp.sum(grad_normed * normed_own, axis=0),
        jnp.sum(grad_normed, axis=0),
    )


def on_device_plain(
    tokens,
    cotangent,
    norm1_gain,
    norm1_shift,
    qkv_weight,
    qv_bias,
    proj_weight,
    proj_bias,
    scale_attn,
    norm2_gain,
    norm2_shift,
    fc1_weight,
    fc1_bias,
    fc2_weight,
    fc2_bias,
    scale_mlp,
):
    count = tokens.shape[0]
    half_len = count // IMGS
    heads_here = qkv_weight.shape[1] // (3 * HD)
    factor = HD ** (-0.5)
    width = tokens.shape[1]
    full_tokens = ring_columns(tokens, 0)
    vectors = spread_columns(
        jnp.stack([norm1_gain, norm1_shift, proj_bias, scale_attn, norm2_gain, norm2_shift, scale_mlp])
    )
    gain_one, shift_one, bias_proj, full_scale_attn, gain_two, shift_two, full_scale_mlp = vectors
    full_qkv = lax.all_gather(qkv_weight, "gx", axis=0, tiled=True)
    all_proj = lax.all_gather(ring_columns(proj_weight, 1), "gx", axis=0, tiled=True)
    full_fc1 = lax.all_gather(fc1_weight, "gx", axis=0, tiled=True)
    full_fc2 = lax.all_gather(fc2_weight, "gx", axis=0, tiled=True)
    rows_fc2 = lax.all_to_all(full_fc2, "gy", split_axis=0, concat_axis=1, tiled=True)
    full_cotangent = gather_columns(cotangent)
    inputs = full_tokens.astype(jnp.float32)
    normed_one, inv_one, norm_one = norm_full(inputs, gain_one, shift_one)
    mixed = jnp.dot(norm_one, full_qkv, preferred_element_type=jnp.float32)
    mixed = mixed.reshape(count, heads_here, 3, HD)
    biases = qv_bias.reshape(heads_here, 2, HD)
    queries = (mixed[:, :, 0] + biases[:, 0]).astype(jnp.bfloat16)
    keys = mixed[:, :, 1].astype(jnp.bfloat16)
    values = (mixed[:, :, 2] + biases[:, 1]).astype(jnp.bfloat16)
    lower = lax.axis_index("gx") % 2 == 0
    pair_kv = jnp.concatenate([keys, values], axis=2).reshape(count, heads_here * 2 * HD)
    other_kv = from_partner(pair_kv, "gx", 0)
    first_kv = jnp.where(lower, pair_kv, other_kv)
    second_kv = jnp.where(lower, other_kv, pair_kv)
    image_shape = (IMGS, half_len, heads_here, 2 * HD)
    both_kv = jnp.concatenate(
        [first_kv.reshape(image_shape), second_kv.reshape(image_shape)], axis=1
    )
    key_all = both_kv[..., :HD]
    value_all = both_kv[..., HD:]
    query_img = queries.reshape(IMGS, half_len, heads_here, HD)
    scores = (
        jnp.einsum("iqhe,ikhe->ihqk", query_img, key_all, preferred_element_type=jnp.float32)
        * factor
    )
    row_max = jnp.max(scores, axis=3, keepdims=True)
    exponent = jnp.exp(scores - row_max)
    totals = jnp.sum(exponent, axis=3, keepdims=True)
    log_total = row_max + jnp.log(totals)
    probs = (exponent / totals).astype(jnp.bfloat16)
    attended_img = jnp.einsum(
        "ihqk,ikhe->iqhe", probs, value_all, preferred_element_type=jnp.float32
    ).astype(jnp.bfloat16)
    attended = attended_img.reshape(count, heads_here * HD)
    full_attended = ring_columns(attended, 0)
    attn_out = jnp.dot(full_attended, all_proj, preferred_element_type=jnp.float32) + bias_proj
    middle = inputs + full_scale_attn * attn_out
    normed_two, inv_two, norm_two = norm_full(middle, gain_two, shift_two)
    pre_act = jnp.dot(norm_two, full_fc1, preferred_element_type=jnp.float32) + fc1_bias
    hidden = gelu_exact(pre_act).astype(jnp.bfloat16)
    upstream = cotangent.astype(jnp.float32)
    grad_mlp = upstream * scale_mlp
    grad_fc2_bias = jnp.sum(grad_mlp, axis=0)
    full_grad_mlp_b = (full_cotangent.astype(jnp.float32) * full_scale_mlp).astype(jnp.bfloat16)
    grad_hidden = jnp.einsum(
        "tn,kn->tk", full_grad_mlp_b, rows_fc2, preferred_element_type=jnp.float32
    )
    grad_pre = grad_hidden * gelu_slope(pre_act)
    grad_fc1_bias = jnp.sum(grad_pre, axis=0)
    grad_pre_b = grad_pre.astype(jnp.bfloat16)
    own_two = own_columns(normed_two, width)
    grad_rows, grad_gain_two, grad_shift_two = back_norm(
        grad_pre_b, full_fc1, normed_two, own_two, inv_two, gain_two, norm2_gain
    )
    grad_middle = upstream + grad_rows
    grad_scale_attn = jnp.sum(grad_middle * own_columns(attn_out, width), axis=0)
    grad_attn = grad_middle * scale_attn
    grad_proj_bias = jnp.sum(grad_attn, axis=0)
    grad_attn_b = grad_attn.astype(jnp.bfloat16)
    full_grad_attn_b = ring_columns(grad_attn_b, 0)
    own_rows_proj = lax.dynamic_slice_in_dim(
        all_proj, lax.axis_index("gy") * width, width, axis=0
    )
    grad_attended = jnp.einsum(
        "tn,kn->tk", full_grad_attn_b, own_rows_proj, preferred_element_type=jnp.float32
    ).astype(jnp.bfloat16)
    mlp_term = jnp.dot(hidden, rows_fc2, preferred_element_type=jnp.float32)
    mlp_out = (
        lax.psum_scatter(
            column_blocks(mlp_term.astype(jnp.bfloat16)), "gy", scatter_dimension=0, tiled=False
        ).astype(jnp.float32)
        + fc2_bias
    )
    output = own_columns(middle, width) + scale_mlp * mlp_out
    grad_scale_mlp = jnp.sum(upstream * mlp_out, axis=0)
    fc2_term = jnp.einsum(
        "tk,tn->kn", hidden, full_grad_mlp_b, preferred_element_type=jnp.float32
    )
    fc2_blocks = lax.all_to_all(column_blocks(fc2_term.astype(jnp.bfloat16)), "gy", 0, 0, tiled=True)
    grad_fc2 = sum_rows(fc2_blocks.reshape(-1, width))
    grad_fc1 = weight_grad_rows(norm_two, grad_pre_b)
    grad_proj = weight_grad_rows(full_attended, grad_attn_b)
    grad_att_img = grad_attended.reshape(IMGS, half_len, heads_here, HD)
    recomputed = jnp.exp(scores - log_total)
    probs_b = recomputed.astype(jnp.bfloat16)
    grad_value_all = jnp.einsum(
        "ihqk,iqhe->ikhe", probs_b, grad_att_img, preferred_element_type=jnp.float32
    )
    grad_probs = jnp.einsum(
        "iqhe,ikhe->ihqk", grad_att_img, value_all, preferred_element_type=jnp.float32
    )
    delta = jnp.sum(grad_att_img.astype(jnp.float32) * attended_img.astype(jnp.float32), axis=3)
    grad_scores = recomputed * (grad_probs - jnp.transpose(delta, (0, 2, 1))[..., None])
    grad_scores_b = grad_scores.astype(jnp.bfloat16)
    grad_query = (
        jnp.einsum("ihqk,ikhe->iqhe", grad_scores_b, key_all, preferred_element_type=jnp.float32)
        * factor
    )
    grad_key_all = (
        jnp.einsum("ihqk,iqhe->ikhe", grad_scores_b, query_img, preferred_element_type=jnp.float32)
        * factor
    )
    grad_kv_all = jnp.concatenate([grad_key_all, grad_value_all], axis=3)
    first_part = grad_kv_all[:, :half_len].reshape(count, heads_here * 2 * HD)
    second_part = grad_kv_all[:, half_len:].reshape(count, heads_here * 2 * HD)
    own_part = jnp.where(lower, first_part, second_part)
    sent_part = jnp.where(lower, second_part, first_part)
    grad_kv = own_part + from_partner(sent_part.astype(jnp.bfloat16), "gx", 0).astype(
        sent_part.dtype
    )
    grad_kv = grad_kv.reshape(count, heads_here, 2, HD)
    grad_query = grad_query.reshape(count, heads_here, HD)
    grad_qv_bias = jnp.stack(
        [jnp.sum(grad_query, axis=0), jnp.sum(grad_kv[:, :, 1], axis=0)], axis=1
    ).reshape(heads_here * 2 * HD)
    grad_mixed = (
        jnp.stack([grad_query, grad_kv[:, :, 0], grad_kv[:, :, 1]], axis=2)
        .astype(jnp.bfloat16)
        .reshape(count, heads_here * 3 * HD)
    )
    grad_qkv = weight_grad(norm_one, grad_mixed)
    own_one = own_columns(normed_one, width)
    grad_rows, grad_gain_one, grad_shift_one = back_norm(
        grad_mixed, full_qkv, normed_one, own_one, inv_one, gain_one, norm1_gain
    )
    grad_input = grad_middle + grad_rows
    smalls = lax.psum(
        (
            grad_gain_one,
            grad_shift_one,
            grad_qv_bias,
            grad_proj_bias,
            grad_scale_attn,
            grad_gain_two,
            grad_shift_two,
            grad_fc1_bias,
            grad_fc2_bias,
            grad_scale_mlp,
        ),
        "gx",
    )
    return (
        output,
        grad_input,
        smalls[0],
        smalls[1],
        grad_qkv,
        smalls[2],
        grad_proj,
        smalls[3],
        smalls[4],
        smalls[5],
        smalls[6],
        grad_fc1,
        smalls[7],
        grad_fc2,
        smalls[8],
        smalls[9],
    )


def up_to(value, step):
    return -(-value // step) * step


def dot_nn(a, b):
    return lax.dot_general(a, b, (((1,), (0,)), ((), ())), preferred_element_type=jnp.float32)


def dot_nt(a, b):
    return lax.dot_general(a, b, (((1,), (1,)), ((), ())), preferred_element_type=jnp.float32)


def dot_tn(a, b):
    return lax.dot_general(a, b, (((0,), (0,)), ((), ())), preferred_element_type=jnp.float32)


def split_high(values):
    high = values.astype(jnp.bfloat16)
    return high, (values - high.astype(jnp.float32)).astype(jnp.bfloat16)


def mega_kernel(
    parts,
    count,
    heads,
    hidden_width,
    sems,
    tok_ref,
    cot_ref,
    vec_ref,
    own_ref,
    qkv_ref,
    proj_ref,
    fc1_ref,
    fc2_ref,
    out_ref,
    gin_ref,
    small_ref,
    gqkv_ref,
    gproj_ref,
    gfc1_ref,
    gfc2_ref,
    tg,
    cg,
    ag,
    hg,
    vecs,
    wqkv,
    wfc1,
    projg,
    wproj,
    fc2x,
    fc2g,
    wfc2,
    nb,
    nt,
    gm,
    stat,
    mixf,
    qkvb,
    qkvo,
    kvc,
    kvt,
    qz,
    dz,
    pt,
    att,
    atile,
    ao,
    pre,
    gh,
    hid,
    gpb,
    prod,
    tscr,
    rs_send,
    rs_recv,
    st_mine,
    st_all,
    st_sum,
    mid_own,
    gmid,
    gat,
    dkv,
    dks,
    dkr,
    dqf,
    gmx,
    tq,
    tqs,
    tqc,
    tqx,
    tp,
    tps,
    tpc,
    tpx,
    t1,
    t1s,
    t1c,
    t1x,
    t2,
    t2s,
    t2c,
    t2r,
    t2x,
    sm,
    sma,
    cs_acc,
    ssem,
    rsem,
):
    width = 128
    full = parts * width
    half = parts // 2
    rows_pad = tg.shape[1]
    tile = rows_pad // 4
    mid_row = rows_pad // 2
    three = heads * 3 * HD
    qpad = qz.shape[1]
    f32, bf = jnp.float32, jnp.bfloat16
    MESH = pl.DeviceIdType.MESH
    i = lax.axis_index("gx")
    me = lax.axis_index("gy")
    core = i % 2
    plane = i // 2
    sib = plane * 2 + (1 - core)
    opp = (1 - plane) * 2 + core
    dia = (1 - plane) * 2 + (1 - core)
    odd = me % 2
    place = (1 - odd) * (me // 2) + odd * (parts - 1 - me // 2)

    def index_of(spot):
        spot = (spot + 2 * parts) % parts
        back = spot // half
        return (1 - back) * (2 * spot) + back * (2 * (parts - 1 - spot) + 1)

    right, left = index_of(place + 1), index_of(place - 1)
    used = [0]
    started = []

    def take(number):
        first = used[0]
        used[0] += number
        assert used[0] <= sems
        return first

    def remote(src, dst, send, recv, **where):
        return pltpu.make_async_remote_copy(
            src_ref=src,
            dst_ref=dst,
            send_sem=ssem.at[send],
            recv_sem=rsem.at[recv],
            device_id=where,
            device_id_type=MESH,
        )

    def launch(copy):
        copy.start()
        started.append(copy)

    class Ring:
        def __init__(self, buf, height):
            self.buf, self.height, self.base = buf, height, take(4 * half)

        def has(self, way, step, chunk):
            return step < half - 1 or (step == half - 1 and way == chunk)

        def copy(self, way, step, chunk):
            owner = index_of(place - step if way == 0 else place + step)
            cut = self.height // 2
            ref = self.buf.at[owner, pl.ds(chunk * cut, cut)]
            sem = self.base + (way * half + step) * 2 + chunk
            return remote(ref, ref, sem, sem, gy=right if way == 0 else left)

        def start(self, chunk):
            for way in range(2):
                if self.has(way, 0, chunk):
                    launch(self.copy(way, 0, chunk))

        def advance(self, step):
            for chunk in range(2):
                for way in range(2):
                    if self.has(way, step, chunk):
                        self.copy(way, step, chunk).wait_recv()
                        if self.has(way, step + 1, chunk):
                            launch(self.copy(way, step + 1, chunk))

    class Scatter:
        def __init__(self, slot, lhs, weight_rows):
            self.send, self.recv = rs_send.at[slot], rs_recv.at[slot]
            self.lhs, self.weight_rows = lhs, weight_rows
            self.base = take(4 * half)
            self.scr = tscr

        def has(self, way, step, chunk):
            return 0 <= step < half and (step > 0 or way == chunk)

        def copy(self, way, step, chunk):
            sem = self.base + (way * half + step) * 2 + chunk
            piece = pl.ds(chunk * mid_row, mid_row)
            return remote(
                self.send.at[way, step, piece],
                self.recv.at[way, step, piece],
                sem,
                sem,
                gy=right if way == 0 else left,
            )

        def term(self, step):
            first = self.weight_rows(index_of(place + half - step))
            if 0 < step < half:
                weight = jnp.concatenate(
                    [first, self.weight_rows(index_of(place - half + step))], axis=0
                )
            else:
                weight = first
            wide = weight.shape[0]

            @pl.loop(0, 2)
            def _(piece):
                at = pl.ds(pl.multiple_of(piece * mid_row, mid_row), mid_row)
                self.scr[at, 0:wide] = dot_nt(self.lhs[at, :], weight)

        def put(self, step):
            for chunk in range(2):
                at = pl.ds(chunk * mid_row, mid_row)
                for way in range(2):
                    if not self.has(way, step, chunk):
                        continue
                    lane = 0 if step == 0 or way == 0 else width
                    value = self.scr[at, lane : lane + width]
                    if self.has(way, step - 1, chunk):
                        self.copy(way, step - 1, chunk).wait_recv()
                        value = value + self.recv[way, step - 1, at, :].astype(f32)
                    self.send[way, step, at, :] = value.astype(bf)
                    launch(self.copy(way, step, chunk))

        def step(self, step):
            self.term(step)
            self.put(step)

        def finish(self):
            self.term(half)
            total = self.scr[:, 0:width]
            for way in range(2):
                for chunk in range(2):
                    self.copy(way, half - 1, chunk).wait_recv()
                total = total + self.recv[way, half - 1].astype(f32)
            return total

    class Gather:
        def __init__(self, view):
            self.view, self.base = view, take(3)

        def copy(self, which):
            shard = opp if which == 2 else i
            to = opp if which == 1 else sib
            ref = self.view(shard)
            return remote(ref, ref, self.base + which, self.base + which, gx=to)

        def start(self):
            launch(self.copy(1))
            launch(self.copy(0))

        def forward(self):
            self.copy(1).wait_recv()
            launch(self.copy(2))

        def finish(self):
            self.copy(0).wait_recv()
            self.copy(2).wait_recv()

    class RowSum:
        def __init__(self, term, from_sib, sent, from_opp, out):
            self.refs = (term, from_sib, sent, from_opp, out)
            self.base = take(2)

        def first(self):
            term, from_sib = self.refs[:2]
            return remote(term.at[1 - core], from_sib, self.base, self.base, gx=sib)

        def second(self):
            sent, from_opp = self.refs[2:4]
            return remote(sent, from_opp, self.base + 1, self.base + 1, gx=opp)

        def start(self):
            launch(self.first())

        def cross(self):
            term, from_sib, sent = self.refs[:3]
            self.first().wait_recv()
            sent[...] = (
                term[core, 1 - plane].astype(f32) + from_sib[1 - plane].astype(f32)
            ).astype(bf)
            launch(self.second())

        def finish(self):
            term, from_sib, _, from_opp, out = self.refs
            self.second().wait_recv()
            out[...] = (
                term[core, plane].astype(f32)
                + from_sib[plane].astype(f32)
                + from_opp[...].astype(f32)
            )

    ring_tok, ring_cot = Ring(tg, rows_pad), Ring(cg, rows_pad)
    ring_att, ring_grad = Ring(ag, rows_pad), Ring(hg, rows_pad)
    quarter = full // 4
    ring_proj = Ring(projg.at[i], quarter)
    gat_qkv = Gather(lambda shard: wqkv.at[pl.ds(pl.multiple_of(shard * quarter, quarter), quarter)])
    gat_fc1 = Gather(lambda shard: wfc1.at[pl.ds(pl.multiple_of(shard * quarter, quarter), quarter)])
    gat_proj = Gather(lambda shard: projg.at[shard])
    sum_qkv = RowSum(tq, tqs, tqc, tqx, gqkv_ref)
    sum_proj = RowSum(tp, tps, tpc, tpx, gproj_ref)
    sum_fc1 = RowSum(t1, t1s, t1c, t1x, gfc1_ref)

    class Spread:
        def __init__(self, src, view, number):
            self.src, self.view = src, view
            self.sends, self.recvs = take(parts), take(parts)

        def start(self):
            for step in range(1, parts):
                to = (me + step) % parts
                launch(
                    remote(self.src(to), self.view(me), self.sends + step, self.recvs + me, gy=to)
                )

        def wait(self, other):
            remote(self.src(other), self.view(other), self.sends, self.recvs + other, gy=other).wait_recv()

        def finish(self):
            for step in range(1, parts):
                self.wait((me + step) % parts)

    all_vecs = Spread(lambda to: vec_ref, lambda who: vecs.at[who], 0)
    all_stats = [
        Spread(lambda to, k=k: st_mine.at[k], lambda who, k=k: st_all.at[k, who], 0) for k in range(2)
    ]

    barrier = pltpu.get_barrier_semaphore()
    for step in range(1, parts):
        pl.semaphore_signal(
            barrier, inc=1, device_id={"gy": (me + step) % parts}, device_id_type=MESH
        )
    for to in (sib, opp, dia):
        pl.semaphore_signal(barrier, inc=1, device_id={"gx": to}, device_id_type=MESH)
    tg[me] = tok_ref[...]
    wqkv[pl.ds(pl.multiple_of(i * quarter, quarter), quarter), :] = qkv_ref[...]
    pl.semaphore_wait(barrier, parts + 2)

    ring_tok.start(0)
    ring_tok.start(1)
    gat_qkv.start()
    all_vecs.start()
    vecs[me] = vec_ref[...]
    cg[me] = cot_ref[...]
    projg[i, me] = proj_ref[...]
    wfc1[pl.ds(pl.multiple_of(i * quarter, quarter), quarter), :] = fc1_ref[...]
    ring_tok.advance(0)
    fc2_cross = take(1)
    cross = remote(fc2_ref, fc2x, fc2_cross, fc2_cross, gx=opp)
    launch(cross)
    gat_qkv.forward()
    ring_tok.advance(1)
    gat_fc1.start()
    ring_tok.advance(2)
    ring_proj.start(0)
    ring_proj.start(1)
    gat_qkv.finish()
    ring_tok.advance(3) if half > 3 else None
    for step in range(4, half):
        ring_tok.advance(step)
    ring_cot.start(0)
    ring_cot.start(1)
    all_vecs.finish()

    GAIN1, SHIFT1, BPROJ, SATT, GAIN2, SHIFT2, SMLP = range(7)
    FC2B = 7

    def vec_block(block, which):
        return vecs[block, which : which + 1, :]

    def row_tile(number, size=tile):
        return pl.ds(pl.multiple_of(number * size, size), size)

    def normalise(blocks, gain, shift, rows, slot, dest):
        acc = blocks[0]
        for block in blocks[1:]:
            acc = acc + block
        row_mean = jnp.sum(acc, axis=1, keepdims=True) * (1.0 / full)
        blocks = [block - row_mean for block in blocks]
        acc = blocks[0] * blocks[0]
        for block in blocks[1:]:
            acc = acc + block * block
        inv = lax.rsqrt(jnp.sum(acc, axis=1, keepdims=True) * (1.0 / full) + EPS)
        for at in range(parts):
            value = blocks[at] * inv * vec_block(at, gain) + vec_block(at, shift)
            dest[rows, at * width : (at + 1) * width] = value.astype(bf)
        stat[slot, rows, :] = row_mean
        stat[slot + 1, rows, :] = inv

    @pl.loop(0, 4)
    def _(number):
        rows = row_tile(number)
        normalise([tg[at, rows, :].astype(f32) for at in range(parts)], GAIN1, SHIFT1, rows, 0, nb)

    qkv_bias = own_ref[0:1, 0:three]
    qkv_scale = own_ref[1:2, 0:three]

    @pl.loop(0, 2)
    def _(number):
        rows = row_tile(number, mid_row)
        mixed = dot_nn(nb[rows, :], wqkv[...])
        mixf[rows, :] = mixed
        qkvb[rows, :] = ((mixed + qkv_bias) * qkv_scale).astype(bf)

    kv_sem = take(1)
    kv_copy = remote(qkvb, qkvo, kv_sem, kv_sem, gx=sib)
    launch(kv_copy)
    ring_proj.advance(0)
    ring_cot.advance(0)
    gat_fc1.forward()
    zero_half = jnp.zeros((qpad - rows_pad, 2 * HD), bf)
    for head in range(heads):
        at = head * 3 * HD
        query = qkvb[:, at : at + HD]
        qz[head, 0:rows_pad, :] = jnp.concatenate([query, jnp.zeros_like(query)], axis=1)
        qz[head, rows_pad:qpad, :] = zero_half
        kvc[head, 0:rows_pad, :] = qkvb[:, at + HD : at + 3 * HD]
    kv_copy.wait_recv()
    for head in range(heads):
        at = head * 3 * HD
        kvc[head, rows_pad : 2 * rows_pad, :] = qkvo[:, at + HD : at + 3 * HD]
        kvt[head] = jnp.transpose(kvc[head])
    ring_proj.advance(1)

    lo = count // 8 * 8
    qtile = 256
    qtiles = qpad // qtile

    def mask_keys(scores):
        pieces = []
        for base in (0, rows_pad):
            pieces.append(scores[base : base + lo])
            edge = scores[base + lo : base + rows_pad]
            index = lax.broadcasted_iota(jnp.int32, edge.shape, 0) + lo
            pieces.append(jnp.where(index < count, edge, -1e30))
        return jnp.concatenate(pieces, axis=0)

    def attend_tile(number):
        cols = slice(number * qtile, (number + 1) * qtile)
        for head in range(heads):
            scores = mask_keys(dot_nt(kvc[head], qz[head, cols, :]))
            top = jnp.max(scores, axis=0, keepdims=True)
            exponent = jnp.exp(scores - top)
            total = jnp.sum(exponent, axis=0, keepdims=True)
            probs = (exponent * (1.0 / total)).astype(bf)
            pt[head, :, cols] = probs
            result = dot_nn(kvt[head, HD : 2 * HD, :], probs).astype(bf)
            att[head * HD : (head + 1) * HD, cols] = result
        stop = min((number + 1) * qtile, rows_pad)
        got = jnp.transpose(att[:, cols])
        ag[me, number * qtile : stop, :] = got[0 : stop - number * qtile]

    sent_chunks = 0
    for number in range(qtiles):
        attend_tile(number)
        ring_cot.advance(number + 1) if number + 1 < half else None
        if number == 0:
            ring_proj.advance(2)
            gat_fc1.finish()
        if number == 1:
            for step in range(3, half):
                ring_proj.advance(step)
            gat_proj.start()
        while sent_chunks < 2 and (number + 1) * qtile >= (sent_chunks + 1) * mid_row:
            ring_att.start(sent_chunks)
            sent_chunks += 1
    for step in range(qtiles + 1, half):
        ring_cot.advance(step)

    lines = fc2_ref.shape[0] // 2
    cross.wait_recv()
    is_owner = core == (me // 2) % 2
    spread_send, spread_recv = take(4), take(parts)
    later = []

    def fc2_copy(block):
        source = fc2_ref if block < 2 else fc2x
        target = 2 * (i if block < 2 else opp) + block % 2
        return target, remote(
            source.at[pl.ds((block % 2) * lines, lines)],
            fc2g.at[me],
            spread_send + block,
            spread_recv + me,
            gy=target,
        )

    for block in range(4):
        target, copy = fc2_copy(block)
        source = fc2_ref if block < 2 else fc2x

        @pl.when(target != me)
        def _():
            copy.start()

        @pl.when(target == me)
        def _():
            fc2g[me] = source[(block % 2) * lines : (block % 2 + 1) * lines, :]

    pass_sem = take(1)
    fc2_pass = remote(fc2g, fc2g, pass_sem, pass_sem, gx=sib)

    @pl.loop(0, 4)
    def _(number):
        rows = row_tile(number)
        for at in range(parts):
            gm[rows, at * width : (at + 1) * width] = (
                cg[at, rows, :].astype(f32) * vec_block(at, SMLP)
            ).astype(bf)

    ring_att.advance(0)
    gat_proj.forward()

    @pl.when(is_owner)
    def _():
        for step in range(1, parts):
            other = (me + step) % parts
            remote(fc2g.at[other], fc2g.at[other], spread_send, spread_recv + other, gy=other).wait_recv()
        fc2_pass.start()

    ring_att.advance(1)

    @pl.when(jnp.logical_not(is_owner))
    def _():
        fc2_pass.wait_recv()

    for at in range(parts):
        wfc2[:, at * width : (at + 1) * width] = fc2g[at]

    @pl.loop(0, 2)
    def _(number):
        rows = row_tile(number, mid_row)
        gh[rows, :] = dot_nt(gm[rows, :], wfc2[...])

    ring_att.advance(2)
    gat_proj.finish()
    for shard in range(4):
        for at in range(parts):
            wproj[shard * quarter : (shard + 1) * quarter, at * width : (at + 1) * width] = projg[shard, at]

    def weigh(which, weight):
        whole = jnp.concatenate([vec_block(at, which) for at in range(parts)], axis=1)
        high, low = split_high(jnp.broadcast_to(whole, (16, full)))
        return (dot_nn(high, weight) + dot_nn(low, weight))[0:1]

    gain_fc1 = weigh(GAIN2, wfc1[...])
    shift_fc1 = weigh(SHIFT2, wfc1[...])
    gain_qkv = weigh(GAIN1, wqkv[...])
    shift_qkv = weigh(SHIFT1, wqkv[...])
    for step in range(3, half):
        ring_att.advance(step)

    @pl.loop(0, 4)
    def _(number):
        rows = row_tile(number)
        whole = jnp.concatenate([ag[at, rows, :] for at in range(parts)], axis=1)
        result = dot_nn(whole, wproj[...])
        blocks = []
        for at in range(parts):
            attn = result[:, at * width : (at + 1) * width] + vec_block(at, BPROJ)
            ao[at, rows, :] = attn
            blocks.append(tg[at, rows, :].astype(f32) + vec_block(at, SATT) * attn)
        normalise(blocks, GAIN2, SHIFT2, rows, 2, nt)

    fc1_bias = own_ref[2:3, 0:hidden_width]
    cs_acc[...] = jnp.zeros_like(cs_acc)

    @pl.loop(0, 4)
    def _(number):
        rows = row_tile(number)
        raw = dot_nn(nt[rows, :], wfc1[...])
        act = raw + fc1_bias
        cdf = normal_cdf(act)
        hid[rows, :] = (act * cdf).astype(bf)
        slope = cdf + act * jnp.exp(-0.5 * act * act) * INV_ROOT_TAU
        grad = gh[rows, :] * slope
        cs_acc[...] += jnp.sum(grad.reshape(tile // 8, 8, hidden_width), axis=0)
        gpb[rows, :] = grad.astype(bf)
        prod[rows, 0:hidden_width] = (grad * (raw - shift_fc1)).astype(bf)

    def row_sums(slot, weights, grads, products):
        wide = grads.shape[1]
        high, low = split_high(jnp.broadcast_to(weights, (8, wide)))
        ones = jnp.ones((8, wide), bf)
        first = dot_nt(high, grads) + dot_nt(low, grads)
        second = dot_nt(ones, products)
        st_mine[slot, 0:1, 0:rows_pad] = first[0:1]
        st_mine[slot, 1:2, 0:rows_pad] = second[0:1]
        all_stats[slot].start()
        st_all[slot, me] = st_mine[slot]

    def total_sums(slot):
        all_stats[slot].finish()
        total = st_all[slot, 0]
        for at in range(1, parts):
            total = total + st_all[slot, at]
        st_sum[...] = jnp.zeros_like(st_sum)
        st_sum[0:2, :] = total
        turned = jnp.transpose(st_sum[...])
        return turned[0:rows_pad, 0:1] * (1.0 / full), turned[0:rows_pad, 1:2] * (1.0 / full)

    scat_two = Scatter(0, gpb, lambda who: wfc1[pl.ds(pl.multiple_of(who * width, width), width), :])
    scat_two.term(0)
    scat_two.put(0)
    st_mine[...] = jnp.zeros_like(st_mine)
    row_sums(0, gain_fc1, gpb[...], prod[:, 0:hidden_width])
    for step in range(1, half):
        scat_two.step(step)

    def fc2_grad(number):
        result = dot_tn(hid[...], gm[:, number * 256 : (number + 1) * 256]).astype(bf)
        t2[2 * number] = result[:, 0:width]
        t2[2 * number + 1] = result[:, width : 2 * width]

    for number in range(parts // 2):
        fc2_grad(number)
    sib_sem = take(1)
    t2_pass = remote(t2, t2s, sib_sem, sib_sem, gx=sib)

    @pl.when(jnp.logical_not(is_owner))
    def _():
        t2_pass.start()

    grad_two = scat_two.finish()
    first, second = total_sums(0)
    upstream = cg[me].astype(f32)
    attn_own = ao[me]
    satt_own = vecs[me, SATT : SATT + 1, :]
    mid_value = tg[me].astype(f32) + satt_own * attn_own
    mid_own[...] = mid_value
    inv_two = stat[3]
    normed = (mid_value - stat[2]) * inv_two
    gain_own = vecs[me, GAIN2 : GAIN2 + 1, :]
    grad_mid = upstream + inv_two * (grad_two * gain_own - first - normed * second)
    gmid[...] = grad_mid
    grad_attn = grad_mid * satt_own
    hg[me] = grad_attn.astype(bf)
    ring_grad.start(0)
    ring_grad.start(1)

    def col_sum(value):
        return jnp.sum(value, axis=0, keepdims=True)

    sm[...] = jnp.zeros_like(sm)
    sm[5:6, :] = col_sum(grad_attn)
    sm[6:7, :] = col_sum(grad_mid * attn_own)
    sm[7:8, :] = col_sum(grad_two * normed)
    sm[8:9, :] = col_sum(grad_two)
    fc1_sum = col_sum(cs_acc[...])
    for at in range(hidden_width // width):
        sm[16 + at : 17 + at, :] = fc1_sum[:, at * width : (at + 1) * width]

    def rows_grad(dest, left_of, grads):
        for shard in range(4):
            dest[shard % 2, shard // 2] = dot_tn(left_of(shard), grads).astype(bf)

    rows_grad(t1, lambda shard: nt[:, shard * quarter : (shard + 1) * quarter], gpb[...])
    sum_fc1.start()
    ring_grad.advance(0)
    blocks_in = quarter // width
    rows_grad(
        tp,
        lambda shard: jnp.concatenate(
            [ag[shard * blocks_in + b] for b in range(blocks_in)], axis=1
        ),
        hg[me],
    )
    sum_proj.start()
    sum_fc1.cross()

    t2_recv = take(parts)
    t2_send = take(parts)

    def t2_copy(step):
        to = (me + step) % parts
        return remote(t2c.at[to], t2r.at[me], t2_send + step, t2_recv + me, gy=to)

    @pl.when(is_owner)
    def _():
        t2_pass.wait_recv()
        for at in range(parts):
            t2c[at] = (t2[at].astype(f32) + t2s[at].astype(f32)).astype(bf)

    ring_grad.advance(1)
    sum_proj.cross()
    ring_grad.advance(2)
    for step in range(3, half):
        ring_grad.advance(step)
    own_rows = pl.ds(pl.multiple_of(me * width, width), width)

    @pl.loop(0, 4)
    def _(number):
        rows = row_tile(number)
        whole = jnp.concatenate([hg[at, rows, :] for at in range(parts)], axis=1)
        gat[rows, :] = dot_nt(whole, wproj[own_rows, :]).astype(bf)

    gat[rows_pad:qpad, :] = jnp.zeros((qpad - rows_pad, 2 * HD), bf)
    scat_mlp = Scatter(1, hid, lambda who: wfc2_rows(who))

    def wfc2_rows(who):
        return fc2g[who].T

    class ScatterPlain(Scatter):
        def term(self, step):
            first = fc2g[index_of(place + half - step)]
            if 0 < step < half:
                weight = jnp.concatenate([first, fc2g[index_of(place - half + step)]], axis=1)
            else:
                weight = first
            wide = weight.shape[1]

            @pl.loop(0, 2)
            def _(piece):
                at = pl.ds(pl.multiple_of(piece * mid_row, mid_row), mid_row)
                self.scr[at, 0:wide] = dot_nn(self.lhs[at, :], weight)

    scat_mlp = ScatterPlain(1, hid, None)
    scat_mlp.step(0)

    gatt = jnp.transpose(gat[...])
    delta_all = gatt.astype(f32) * att[...].astype(f32)
    for head in range(heads):
        value = gat[:, head * HD : (head + 1) * HD]
        dz[head] = jnp.concatenate([jnp.zeros_like(value), value], axis=1)
    deltas = [
        jnp.sum(delta_all[head * HD : (head + 1) * HD], axis=0, keepdims=True) for head in range(heads)
    ]
    dkv[...] = jnp.zeros_like(dkv)

    def attend_back(number):
        cols = slice(number * qtile, (number + 1) * qtile)
        for head in range(heads):
            probs = pt[head, :, cols]
            query, grad = qz[head, cols, :], dz[head, cols, :]
            slope = dot_nt(kvc[head], grad)
            scores = (probs.astype(f32) * (slope - deltas[head][:, cols])).astype(bf)
            dkv[head] += dot_nn(probs, grad) + dot_nn(scores, query)
            dqf[head * HD : (head + 1) * HD, cols] = dot_nn(kvt[head, 0:HD, :], scores)

    for number in range(qtiles):
        attend_back(number)
        if number + 1 < half:
            scat_mlp.step(number + 1)
    for step in range(qtiles + 1, half):
        scat_mlp.step(step)

    for head in range(heads):
        dks[head] = dkv[head, rows_pad : 2 * rows_pad, :].astype(bf)
    dk_sem = take(1)
    dk_copy = remote(dks, dkr, dk_sem, dk_sem, gx=sib)
    launch(dk_copy)

    @pl.when(is_owner)
    def _():
        for step in range(1, parts):
            t2_copy(step).start()
        t2r[me] = t2c[me]

    grad_query = jnp.transpose(dqf[...])[0:rows_pad] * (HD ** (-0.5))
    sm[0:1, :] = col_sum(grad_query)
    dk_copy.wait_recv()
    pieces = []
    value_sums = []
    for head in range(heads):
        own = dkv[head, 0:rows_pad, :] + dkr[head].astype(f32)
        value_sums.append(col_sum(own))
        pieces += [grad_query[:, head * HD : (head + 1) * HD], own]
    for head in range(heads):
        sm[1 + head : 2 + head, :] = value_sums[head]
    mixed_grad = jnp.concatenate(pieces, axis=1)
    gmx[...] = mixed_grad.astype(bf)
    prod[:, 0:three] = (mixed_grad * (mixf[...] - shift_qkv)).astype(bf)

    scat_one = Scatter(2, gmx, lambda who: wqkv[pl.ds(pl.multiple_of(who * width, width), width), :])
    scat_one.step(0)
    row_sums(1, gain_qkv, gmx[...], prod[:, 0:three])
    rows_grad(tq, lambda shard: nb[:, shard * quarter : (shard + 1) * quarter], gmx[...])
    sum_qkv.start()
    scat_one.step(1)

    mlp_out = scat_mlp.finish() + vecs[me, FC2B : FC2B + 1, :]
    smlp_own = vecs[me, SMLP : SMLP + 1, :]
    up = cg[me].astype(f32)
    out_ref[...] = mid_own[...] + smlp_own * mlp_out
    sm[9:10, :] = col_sum(up * smlp_own)
    sm[10:11, :] = col_sum(up * mlp_out)
    sum_qkv.cross()
    scat_one.step(2)
    sum_fc1.finish()
    sum_proj.finish()

    for step in range(4):
        source = (step // 2) * (parts // 2) + 2 * core + step % 2

        @pl.when(source != me)
        def _():
            remote(t2c.at[me], t2r.at[source], t2_send, t2_recv + source, gy=source).wait_recv()

    x_sem = take(1)
    t2_cross = remote(t2r.at[pl.ds(2 * opp, 2)], t2x, x_sem, x_sem, gx=opp)
    launch(t2_cross)
    for step in range(3, half):
        scat_one.step(step)
    t2_cross.wait_recv()
    for block in range(2):
        gfc2_ref[block * lines : (block + 1) * lines, :] = t2r[2 * i + block].astype(f32) + t2x[
            block
        ].astype(f32)
    sum_qkv.finish()

    grad_one = scat_one.finish()
    first, second = total_sums(1)
    inv_one = stat[1]
    normed = (tg[me].astype(f32) - stat[0]) * inv_one
    gain_own = vecs[me, GAIN1 : GAIN1 + 1, :]
    gin_ref[...] = gmid[...] + inv_one * (grad_one * gain_own - first - normed * second)
    sm[3:4, :] = col_sum(grad_one * normed)
    sm[4:5, :] = col_sum(grad_one)
    sma[i] = sm[...]
    small_sem = take(3)
    copies = [
        remote(sm, sma.at[i], small_sem + n, small_sem + n, gx=to)
        for n, to in enumerate((sib, opp, dia))
    ]
    for copy in copies:
        launch(copy)
    for copy in copies:
        copy.wait_recv()
    small_ref[...] = sma[0] + sma[1] + sma[2] + sma[3]

    for copy in started:
        copy.wait_send()
    for block in range(4):
        target, copy = fc2_copy(block)

        @pl.when(target != me)
        def _():
            copy.wait_send()

    @pl.when(is_owner)
    def _():
        fc2_pass.wait_send()
        for step in range(1, parts):
            t2_copy(step).wait_send()

    @pl.when(jnp.logical_not(is_owner))
    def _():
        t2_pass.wait_send()


def on_device(*args):
    (
        tokens,
        cotangent,
        norm1_gain,
        norm1_shift,
        qkv_weight,
        qv_bias,
        proj_weight,
        proj_bias,
        scale_attn,
        norm2_gain,
        norm2_shift,
        fc1_weight,
        fc1_bias,
        fc2_weight,
        fc2_bias,
        scale_mlp,
    ) = args
    parts, rows_over = lax.axis_size("gy"), lax.axis_size("gx")
    count, width = tokens.shape
    heads = qkv_weight.shape[1] // (3 * HD)
    hidden_width = fc1_weight.shape[1]
    if (
        rows_over != 4
        or parts != 8
        or width != 128
        or heads != 2
        or IMGS != 1
        or hidden_width % 256
    ):
        return on_device_plain(*args)
    full = parts * width
    rows = up_to(count, 64)
    qpad = up_to(rows, 256)
    three = heads * 3 * HD
    quarter = full // 4
    lines = fc2_weight.shape[0] // 2
    half = parts // 2
    bf, f32 = jnp.bfloat16, jnp.float32
    pad = ((0, rows - count), (0, 0))
    vectors = jnp.stack(
        [norm1_gain, norm1_shift, proj_bias, scale_attn, norm2_gain, norm2_shift, scale_mlp, fc2_bias]
    )
    biases = qv_bias.reshape(heads, 2, HD)
    bias_row = jnp.stack([biases[:, 0], jnp.zeros_like(biases[:, 0]), biases[:, 1]], axis=1).reshape(-1)
    scale_row = jnp.tile(
        jnp.concatenate([jnp.full((HD,), HD ** (-0.5), f32), jnp.ones((2 * HD,), f32)]), heads
    )
    wide = max(three, hidden_width)
    own = jnp.stack(
        [
            jnp.pad(bias_row, (0, wide - three)),
            jnp.pad(scale_row, (0, wide - three)),
            jnp.pad(fc1_bias, (0, wide - hidden_width)),
        ]
    )
    own = jnp.pad(own, ((0, 5), (0, 0)))
    stat_wide = up_to(rows, 256)
    V = pltpu.VMEM
    scratch = [
        V((parts, rows, width), bf),
        V((parts, rows, width), bf),
        V((parts, rows, width), bf),
        V((parts, rows, width), bf),
        V((parts, 8, width), f32),
        V((full, three), bf),
        V((full, hidden_width), bf),
        V((4, parts, quarter, width), bf),
        V((full, full), bf),
        V((2 * lines, width), bf),
        V((parts, lines, width), bf),
        V((lines, full), bf),
        V((rows, full), bf),
        V((rows, full), bf),
        V((rows, full), bf),
        V((4, rows, 1), f32),
        V((rows, three), f32),
        V((rows, three), bf),
        V((rows, three), bf),
        V((heads, 2 * rows, 2 * HD), bf),
        V((heads, 2 * HD, 2 * rows), bf),
        V((heads, qpad, 2 * HD), bf),
        V((heads, qpad, 2 * HD), bf),
        V((heads, 2 * rows, qpad), bf),
        V((heads * HD, qpad), bf),
        V((8, width), f32),
        V((parts, rows, width), f32),
        V((8, width), f32),
        V((rows, hidden_width), f32),
        V((rows, hidden_width), bf),
        V((rows, hidden_width), bf),
        V((rows, wide), bf),
        V((rows, 2 * width), f32),
        V((3, 2, half, rows, width), bf),
        V((3, 2, half, rows, width), bf),
        V((2, 2, stat_wide), f32),
        V((2, parts, 2, stat_wide), f32),
        V((8, stat_wide), f32),
        V((rows, width), f32),
        V((rows, width), f32),
        V((qpad, width), bf),
        V((heads, 2 * rows, 2 * HD), f32),
        V((heads, rows, 2 * HD), bf),
        V((heads, rows, 2 * HD), bf),
        V((heads * HD, qpad), f32),
        V((rows, three), bf),
        V((2, 2, quarter, three), bf),
        V((2, quarter, three), bf),
        V((quarter, three), bf),
        V((quarter, three), bf),
        V((2, 2, quarter, width), bf),
        V((2, quarter, width), bf),
        V((quarter, width), bf),
        V((quarter, width), bf),
        V((2, 2, quarter, hidden_width), bf),
        V((2, quarter, hidden_width), bf),
        V((quarter, hidden_width), bf),
        V((quarter, hidden_width), bf),
        V((parts, lines, width), bf),
        V((parts, lines, width), bf),
        V((parts, lines, width), bf),
        V((parts, lines, width), bf),
        V((2, lines, width), bf),
        V((24, width), f32),
        V((4, 24, width), f32),
        V((8, hidden_width), f32),
        pltpu.SemaphoreType.DMA((SEMS,)),
        pltpu.SemaphoreType.DMA((SEMS,)),
    ]
    vmem = pl.BlockSpec(memory_space=pltpu.VMEM)
    results = pl.pallas_call(
        functools.partial(mega_kernel, parts, count, heads, hidden_width, SEMS),
        out_shape=[
            jax.ShapeDtypeStruct((rows, width), f32),
            jax.ShapeDtypeStruct((rows, width), f32),
            jax.ShapeDtypeStruct((24, width), f32),
            jax.ShapeDtypeStruct((quarter, three), f32),
            jax.ShapeDtypeStruct((quarter, width), f32),
            jax.ShapeDtypeStruct((quarter, hidden_width), f32),
            jax.ShapeDtypeStruct((2 * lines, width), f32),
        ],
        in_specs=[vmem] * 8,
        out_specs=[vmem] * 7,
        scratch_shapes=scratch,
        compiler_params=pltpu.CompilerParams(
            collective_id=3, has_side_effects=True, vmem_limit_bytes=VMEM_BYTES
        ),
    )(
        jnp.pad(tokens, pad),
        jnp.pad(cotangent, pad),
        vectors,
        own,
        qkv_weight,
        proj_weight,
        fc1_weight,
        fc2_weight,
    )
    output, grad_in, small, grad_qkv, grad_proj, grad_fc1, grad_fc2 = results
    query_sum = small[0].reshape(heads, HD)
    value_sum = small[1 : 1 + heads, HD:]
    grad_qv = jnp.stack([query_sum, value_sum], axis=1).reshape(-1)
    grad_fc1_bias = small[16 : 16 + hidden_width // width].reshape(-1)
    return (
        output[:count],
        grad_in[:count],
        small[3],
        small[4],
        grad_qkv,
        grad_qv,
        grad_proj,
        small[5],
        small[6],
        small[7],
        small[8],
        grad_fc1,
        grad_fc1_bias,
        grad_fc2,
        small[9],
        small[10],
    )


def solution(mesh):
    return jax.shard_map(
        on_device,
        mesh=mesh,
        in_specs=(
            P("gx", "gy"),
            P("gx", "gy"),
            P("gy"),
            P("gy"),
            P("gx", "gy"),
            P("gy"),
            P("gx", "gy"),
            P("gy"),
            P("gy"),
            P("gy"),
            P("gy"),
            P("gx", "gy"),
            P("gy"),
            P("gx", "gy"),
            P("gy"),
            P("gy"),
        ),
        out_specs=(
            P("gx", "gy"),
            P("gx", "gy"),
            P("gy"),
            P("gy"),
            P("gx", "gy"),
            P("gy"),
            P("gx", "gy"),
            P("gy"),
            P("gy"),
            P("gy"),
            P("gy"),
            P("gx", "gy"),
            P("gy"),
            P("gx", "gy"),
            P("gy"),
            P("gy"),
        ),
        check_vma=False,
    )
```

```python
import functools

import jax
import jax.numpy as jnp
from jax import lax
from jax.experimental import pallas as pl
from jax.experimental.pallas import tpu as pltpu
from jax.sharding import PartitionSpec as P

D = 1024
HD = 64
IMGS = 1


EPS = 1e-06
ROOT_HALF = 0.7071067811865476
INV_ROOT_TAU = 0.3989422804014327
SEMS = 256
VMEM_BYTES = 62 * 1024 * 1024


def from_partner(block, axis, bit):
    count = lax.axis_size(axis)
    route = []
    for low in range(count):
        high = low | 1 << bit
        if high != low and high < count:
            route += [(low, high), (high, low)]
    return lax.ppermute(block, axis, route)


def normal_cdf(values):
    return 0.5 * (1.0 + jax.scipy.special.erf(values * ROOT_HALF))


def gelu_exact(values):
    return values * normal_cdf(values)


def gelu_slope(values):
    return normal_cdf(values) + values * jnp.exp(-0.5 * values * values) * INV_ROOT_TAU


def norm_full(rows, gain, shift):
    row_mean = jnp.mean(rows, axis=1, keepdims=True)
    inv_std = lax.rsqrt(jnp.mean(rows * rows, axis=1, keepdims=True) - row_mean * row_mean + EPS)
    normed = (rows - row_mean) * inv_std
    return (normed, inv_std, (normed * gain + shift).astype(jnp.bfloat16))


def gather_columns(block):
    return lax.all_gather(block, "gy", axis=1, tiled=True)


def ring_kernel(parts, block_ref, out_ref, send_sem, recv_sem):
    half = parts // 2

    def index_of(place):
        back = place // half
        return (1 - back) * (2 * place) + back * (2 * (parts - 1 - place) + 1)

    me = lax.axis_index("gy")
    odd = me % 2
    place = (1 - odd) * (me // 2) + odd * (parts - 1 - me // 2)
    sides = (index_of((place + 1) % parts), index_of((place + parts - 1) % parts))
    barrier = pltpu.get_barrier_semaphore()
    for side in sides:
        pl.semaphore_signal(
            barrier, inc=1, device_id={"gy": side}, device_id_type=pl.DeviceIdType.MESH
        )
    pl.semaphore_wait(barrier, 2)
    copies = []
    for step in range(half):
        owners = (
            index_of((place + parts - step) % parts),
            index_of((place + step) % parts),
        )
        started = []
        for way in range(2):
            if way == 1 and step == half - 1:
                continue
            copy = pltpu.make_async_remote_copy(
                src_ref=block_ref if step == 0 else out_ref.at[owners[way]],
                dst_ref=out_ref.at[owners[way]],
                send_sem=send_sem.at[way, step],
                recv_sem=recv_sem.at[way, step],
                device_id={"gy": sides[way]},
                device_id_type=pl.DeviceIdType.MESH,
            )
            copy.start()
            started.append(copy)
        if step == 0:
            out_ref[me] = block_ref[...]
        for copy in started:
            copy.wait_recv()
        copies += started
    for copy in copies:
        copy.wait_send()


def ring_columns(block, call):
    parts = lax.axis_size("gy")
    count, width = block.shape
    if parts % 2 or parts < 4:
        return gather_columns(block)
    got = pl.pallas_call(
        functools.partial(ring_kernel, parts),
        out_shape=jax.ShapeDtypeStruct((parts, count, width), block.dtype),
        in_specs=[pl.BlockSpec(memory_space=pltpu.VMEM)],
        out_specs=pl.BlockSpec(memory_space=pltpu.VMEM),
        scratch_shapes=[
            pltpu.SemaphoreType.DMA((2, parts // 2)),
            pltpu.SemaphoreType.DMA((2, parts // 2)),
        ],
        compiler_params=pltpu.CompilerParams(collective_id=call, has_side_effects=True),
    )(block)
    return jnp.transpose(got, (1, 0, 2)).reshape(count, parts * width)


def spread_columns(block):
    parts = lax.axis_size("gy")
    got = lax.all_to_all(
        jnp.broadcast_to(block[None], (parts,) + block.shape), "gy", 0, 0, tiled=True
    )
    return jnp.transpose(got, (1, 0, 2)).reshape(block.shape[0], parts * block.shape[1])


def column_blocks(block):
    parts = lax.axis_size("gy")
    count, full = block.shape
    return jnp.transpose(block.reshape(count, parts, full // parts), (1, 0, 2))


def scatter_sum(blocks, axis):
    got = lax.all_to_all(blocks, axis, 0, 0, tiled=True)
    return jnp.sum(got.astype(jnp.float32), axis=0)


def own_columns(block, width):
    return lax.dynamic_slice_in_dim(block, lax.axis_index("gy") * width, width, axis=1)


def sum_rows(term):
    parts = lax.axis_size("gx")
    blocks = term.reshape(parts, term.shape[0] // parts, term.shape[1])
    return scatter_sum(blocks, "gx")


def weight_grad_rows(saved, grad_out):
    term = jnp.einsum("tk,tn->kn", saved, grad_out, preferred_element_type=jnp.float32)
    return lax.psum_scatter(
        term.astype(jnp.bfloat16), "gx", scatter_dimension=0, tiled=True
    ).astype(jnp.float32)


def weight_grad(saved, grad_out):
    term = jnp.einsum("tk,tn->kn", saved, grad_out, preferred_element_type=jnp.float32)
    return sum_rows(term.astype(jnp.bfloat16))


def lanes_of(column, width):
    count = column.shape[0]
    lines = -(-count // width)
    return jnp.pad(column, (0, lines * width - count)).reshape(lines, width)


def back_norm(grad_out, weight, normed, normed_own, inv_std, gain, gain_own):
    parts = lax.axis_size("gy")
    count, full = normed.shape
    width = full // parts
    term = jnp.einsum("tn,kn->tk", grad_out, weight, preferred_element_type=jnp.float32)
    scaled = term * gain
    first = lanes_of(jnp.sum(scaled, axis=1), width)
    second = lanes_of(jnp.sum(scaled * normed, axis=1), width)
    lines = first.shape[0]
    sums = jnp.concatenate([first, second], axis=0).astype(jnp.bfloat16)
    blocks = column_blocks(term.astype(jnp.bfloat16))
    sent = jnp.concatenate(
        [blocks, jnp.broadcast_to(sums[None], (parts,) + sums.shape)], axis=1
    )
    back = scatter_sum(sent, "gy")
    grad_normed = back[:count]
    first = back[count : count + lines].reshape(-1)[:count, None]
    second = back[count + lines :].reshape(-1)[:count, None]
    grad_rows = inv_std * (
        grad_normed * gain_own - first / full - normed_own * (second / full)
    )
    return (
        grad_rows,
        jnp.sum(grad_normed * normed_own, axis=0),
        jnp.sum(grad_normed, axis=0),
    )


def on_device_plain(
    tokens,
    cotangent,
    norm1_gain,
    norm1_shift,
    qkv_weight,
    qv_bias,
    proj_weight,
    proj_bias,
    scale_attn,
    norm2_gain,
    norm2_shift,
    fc1_weight,
    fc1_bias,
    fc2_weight,
    fc2_bias,
    scale_mlp,
):
    count = tokens.shape[0]
    half_len = count // IMGS
    heads_here = qkv_weight.shape[1] // (3 * HD)
    factor = HD ** (-0.5)
    width = tokens.shape[1]
    full_tokens = ring_columns(tokens, 0)
    vectors = spread_columns(
        jnp.stack([norm1_gain, norm1_shift, proj_bias, scale_attn, norm2_gain, norm2_shift, scale_mlp])
    )
    gain_one, shift_one, bias_proj, full_scale_attn, gain_two, shift_two, full_scale_mlp = vectors
    full_qkv = lax.all_gather(qkv_weight, "gx", axis=0, tiled=True)
    all_proj = lax.all_gather(ring_columns(proj_weight, 1), "gx", axis=0, tiled=True)
    full_fc1 = lax.all_gather(fc1_weight, "gx", axis=0, tiled=True)
    full_fc2 = lax.all_gather(fc2_weight, "gx", axis=0, tiled=True)
    rows_fc2 = lax.all_to_all(full_fc2, "gy", split_axis=0, concat_axis=1, tiled=True)
    full_cotangent = gather_columns(cotangent)
    inputs = full_tokens.astype(jnp.float32)
    normed_one, inv_one, norm_one = norm_full(inputs, gain_one, shift_one)
    mixed = jnp.dot(norm_one, full_qkv, preferred_element_type=jnp.float32)
    mixed = mixed.reshape(count, heads_here, 3, HD)
    biases = qv_bias.reshape(heads_here, 2, HD)
    queries = (mixed[:, :, 0] + biases[:, 0]).astype(jnp.bfloat16)
    keys = mixed[:, :, 1].astype(jnp.bfloat16)
    values = (mixed[:, :, 2] + biases[:, 1]).astype(jnp.bfloat16)
    lower = lax.axis_index("gx") % 2 == 0
    pair_kv = jnp.concatenate([keys, values], axis=2).reshape(count, heads_here * 2 * HD)
    other_kv = from_partner(pair_kv, "gx", 0)
    first_kv = jnp.where(lower, pair_kv, other_kv)
    second_kv = jnp.where(lower, other_kv, pair_kv)
    image_shape = (IMGS, half_len, heads_here, 2 * HD)
    both_kv = jnp.concatenate(
        [first_kv.reshape(image_shape), second_kv.reshape(image_shape)], axis=1
    )
    key_all = both_kv[..., :HD]
    value_all = both_kv[..., HD:]
    query_img = queries.reshape(IMGS, half_len, heads_here, HD)
    scores = (
        jnp.einsum("iqhe,ikhe->ihqk", query_img, key_all, preferred_element_type=jnp.float32)
        * factor
    )
    row_max = jnp.max(scores, axis=3, keepdims=True)
    exponent = jnp.exp(scores - row_max)
    totals = jnp.sum(exponent, axis=3, keepdims=True)
    log_total = row_max + jnp.log(totals)
    probs = (exponent / totals).astype(jnp.bfloat16)
    attended_img = jnp.einsum(
        "ihqk,ikhe->iqhe", probs, value_all, preferred_element_type=jnp.float32
    ).astype(jnp.bfloat16)
    attended = attended_img.reshape(count, heads_here * HD)
    full_attended = ring_columns(attended, 0)
    attn_out = jnp.dot(full_attended, all_proj, preferred_element_type=jnp.float32) + bias_proj
    middle = inputs + full_scale_attn * attn_out
    normed_two, inv_two, norm_two = norm_full(middle, gain_two, shift_two)
    pre_act = jnp.dot(norm_two, full_fc1, preferred_element_type=jnp.float32) + fc1_bias
    hidden = gelu_exact(pre_act).astype(jnp.bfloat16)
    upstream = cotangent.astype(jnp.float32)
    grad_mlp = upstream * scale_mlp
    grad_fc2_bias = jnp.sum(grad_mlp, axis=0)
    full_grad_mlp_b = (full_cotangent.astype(jnp.float32) * full_scale_mlp).astype(jnp.bfloat16)
    grad_hidden = jnp.einsum(
        "tn,kn->tk", full_grad_mlp_b, rows_fc2, preferred_element_type=jnp.float32
    )
    grad_pre = grad_hidden * gelu_slope(pre_act)
    grad_fc1_bias = jnp.sum(grad_pre, axis=0)
    grad_pre_b = grad_pre.astype(jnp.bfloat16)
    own_two = own_columns(normed_two, width)
    grad_rows, grad_gain_two, grad_shift_two = back_norm(
        grad_pre_b, full_fc1, normed_two, own_two, inv_two, gain_two, norm2_gain
    )
    grad_middle = upstream + grad_rows
    grad_scale_attn = jnp.sum(grad_middle * own_columns(attn_out, width), axis=0)
    grad_attn = grad_middle * scale_attn
    grad_proj_bias = jnp.sum(grad_attn, axis=0)
    grad_attn_b = grad_attn.astype(jnp.bfloat16)
    full_grad_attn_b = ring_columns(grad_attn_b, 0)
    own_rows_proj = lax.dynamic_slice_in_dim(
        all_proj, lax.axis_index("gy") * width, width, axis=0
    )
    grad_attended = jnp.einsum(
        "tn,kn->tk", full_grad_attn_b, own_rows_proj, preferred_element_type=jnp.float32
    ).astype(jnp.bfloat16)
    mlp_term = jnp.dot(hidden, rows_fc2, preferred_element_type=jnp.float32)
    mlp_out = (
        lax.psum_scatter(
            column_blocks(mlp_term.astype(jnp.bfloat16)), "gy", scatter_dimension=0, tiled=False
        ).astype(jnp.float32)
        + fc2_bias
    )
    output = own_columns(middle, width) + scale_mlp * mlp_out
    grad_scale_mlp = jnp.sum(upstream * mlp_out, axis=0)
    fc2_term = jnp.einsum(
        "tk,tn->kn", hidden, full_grad_mlp_b, preferred_element_type=jnp.float32
    )
    fc2_blocks = lax.all_to_all(column_blocks(fc2_term.astype(jnp.bfloat16)), "gy", 0, 0, tiled=True)
    grad_fc2 = sum_rows(fc2_blocks.reshape(-1, width))
    grad_fc1 = weight_grad_rows(norm_two, grad_pre_b)
    grad_proj = weight_grad_rows(full_attended, grad_attn_b)
    grad_att_img = grad_attended.reshape(IMGS, half_len, heads_here, HD)
    recomputed = jnp.exp(scores - log_total)
    probs_b = recomputed.astype(jnp.bfloat16)
    grad_value_all = jnp.einsum(
        "ihqk,iqhe->ikhe", probs_b, grad_att_img, preferred_element_type=jnp.float32
    )
    grad_probs = jnp.einsum(
        "iqhe,ikhe->ihqk", grad_att_img, value_all, preferred_element_type=jnp.float32
    )
    delta = jnp.sum(grad_att_img.astype(jnp.float32) * attended_img.astype(jnp.float32), axis=3)
    grad_scores = recomputed * (grad_probs - jnp.transpose(delta, (0, 2, 1))[..., None])
    grad_scores_b = grad_scores.astype(jnp.bfloat16)
    grad_query = (
        jnp.einsum("ihqk,ikhe->iqhe", grad_scores_b, key_all, preferred_element_type=jnp.float32)
        * factor
    )
    grad_key_all = (
        jnp.einsum("ihqk,iqhe->ikhe", grad_scores_b, query_img, preferred_element_type=jnp.float32)
        * factor
    )
    grad_kv_all = jnp.concatenate([grad_key_all, grad_value_all], axis=3)
    first_part = grad_kv_all[:, :half_len].reshape(count, heads_here * 2 * HD)
    second_part = grad_kv_all[:, half_len:].reshape(count, heads_here * 2 * HD)
    own_part = jnp.where(lower, first_part, second_part)
    sent_part = jnp.where(lower, second_part, first_part)
    grad_kv = own_part + from_partner(sent_part.astype(jnp.bfloat16), "gx", 0).astype(
        sent_part.dtype
    )
    grad_kv = grad_kv.reshape(count, heads_here, 2, HD)
    grad_query = grad_query.reshape(count, heads_here, HD)
    grad_qv_bias = jnp.stack(
        [jnp.sum(grad_query, axis=0), jnp.sum(grad_kv[:, :, 1], axis=0)], axis=1
    ).reshape(heads_here * 2 * HD)
    grad_mixed = (
        jnp.stack([grad_query, grad_kv[:, :, 0], grad_kv[:, :, 1]], axis=2)
        .astype(jnp.bfloat16)
        .reshape(count, heads_here * 3 * HD)
    )
    grad_qkv = weight_grad(norm_one, grad_mixed)
    own_one = own_columns(normed_one, width)
    grad_rows, grad_gain_one, grad_shift_one = back_norm(
        grad_mixed, full_qkv, normed_one, own_one, inv_one, gain_one, norm1_gain
    )
    grad_input = grad_middle + grad_rows
    smalls = lax.psum(
        (
            grad_gain_one,
            grad_shift_one,
            grad_qv_bias,
            grad_proj_bias,
            grad_scale_attn,
            grad_gain_two,
            grad_shift_two,
            grad_fc1_bias,
            grad_fc2_bias,
            grad_scale_mlp,
        ),
        "gx",
    )
    return (
        output,
        grad_input,
        smalls[0],
        smalls[1],
        grad_qkv,
        smalls[2],
        grad_proj,
        smalls[3],
        smalls[4],
        smalls[5],
        smalls[6],
        grad_fc1,
        smalls[7],
        grad_fc2,
        smalls[8],
        smalls[9],
    )


def up_to(value, step):
    return -(-value // step) * step


def dot_nn(a, b):
    return lax.dot_general(a, b, (((1,), (0,)), ((), ())), preferred_element_type=jnp.float32)


def dot_nt(a, b):
    return lax.dot_general(a, b, (((1,), (1,)), ((), ())), preferred_element_type=jnp.float32)


def dot_tn(a, b):
    return lax.dot_general(a, b, (((0,), (0,)), ((), ())), preferred_element_type=jnp.float32)


def split_high(values):
    high = values.astype(jnp.bfloat16)
    return high, (values - high.astype(jnp.float32)).astype(jnp.bfloat16)


def mega_kernel(
    parts,
    count,
    heads,
    hidden_width,
    sems,
    tok_ref,
    cot_ref,
    gain1_ref,
    shift1_ref,
    qkv_ref,
    qv_ref,
    proj_ref,
    bproj_ref,
    satt_ref,
    gain2_ref,
    shift2_ref,
    fc1_ref,
    bfc1_ref,
    fc2_ref,
    bfc2_ref,
    smlp_ref,
    out_ref,
    gin_ref,
    small_ref,
    gqkv_ref,
    gproj_ref,
    gfc1_ref,
    gfc2_ref,
    tg,
    cg,
    ag,
    hg,
    vecs,
    wqkv,
    wfc1,
    projg,
    wproj,
    fc2x,
    fc2h,
    wfc2,
    nb,
    nt,
    gm,
    stat,
    mixf,
    qkvb,
    qkvo,
    kvc,
    kvt,
    qz,
    dz,
    pt,
    att,
    vec_ref,
    ao,
    gh,
    hid,
    gpb,
    prod,
    tscr,
    rs_send,
    rs_recv,
    st_mine,
    st_all,
    st_sum,
    mid_own,
    gmid,
    gat,
    dkv,
    dks,
    dkr,
    dqf,
    gmx,
    tq,
    tqs,
    tqc,
    tqx,
    tp,
    tps,
    tpc,
    tpx,
    t1,
    t1s,
    t1c,
    t1x,
    t2,
    t2s,
    t2c,
    t2o,
    t2d,
    t2r,
    t2x,
    sm,
    sma,
    cs_acc,
    ssem,
    rsem,
):
    width = 128
    full = parts * width
    half = parts // 2
    rows_pad = tg.shape[1]
    tile = rows_pad // 4
    mid_row = rows_pad // 2
    three = heads * 3 * HD
    qpad = qz.shape[1]
    f32, bf = jnp.float32, jnp.bfloat16
    MESH = pl.DeviceIdType.MESH
    i = lax.axis_index("gx")
    me = lax.axis_index("gy")
    core = i % 2
    plane = i // 2
    sib = plane * 2 + (1 - core)
    opp = (1 - plane) * 2 + core
    dia = (1 - plane) * 2 + (1 - core)
    odd = me % 2
    place = (1 - odd) * (me // 2) + odd * (parts - 1 - me // 2)

    def index_of(spot):
        spot = (spot + 2 * parts) % parts
        back = spot // half
        return (1 - back) * (2 * spot) + back * (2 * (parts - 1 - spot) + 1)

    right, left = index_of(place + 1), index_of(place - 1)
    used = [0]
    started = []

    def take(number):
        first = used[0]
        used[0] += number
        assert used[0] <= sems
        return first

    def remote(src, dst, send, recv, **where):
        return pltpu.make_async_remote_copy(
            src_ref=src,
            dst_ref=dst,
            send_sem=ssem.at[send],
            recv_sem=rsem.at[recv],
            device_id=where,
            device_id_type=MESH,
        )

    def launch(copy):
        copy.start()
        started.append(copy)

    class Ring:
        def __init__(self, buf, height):
            self.buf, self.height, self.base = buf, height, take(4 * half)

        def has(self, way, step, chunk):
            return step < half - 1 or (step == half - 1 and way == chunk)

        def copy(self, way, step, chunk):
            owner = index_of(place - step if way == 0 else place + step)
            cut = self.height // 2
            ref = self.buf.at[owner, pl.ds(chunk * cut, cut)]
            sem = self.base + (way * half + step) * 2 + chunk
            return remote(ref, ref, sem, sem, gy=right if way == 0 else left)

        def start(self, chunk):
            for way in range(2):
                if self.has(way, 0, chunk):
                    launch(self.copy(way, 0, chunk))

        def advance(self, step):
            for chunk in range(2):
                for way in range(2):
                    if self.has(way, step, chunk):
                        self.copy(way, step, chunk).wait_recv()
                        if self.has(way, step + 1, chunk):
                            launch(self.copy(way, step + 1, chunk))

    class Scatter:
        def __init__(self, slot, lhs, weight_rows):
            self.send, self.recv = rs_send.at[slot], rs_recv.at[slot]
            self.lhs, self.weight_rows = lhs, weight_rows
            self.base = take(4 * half)
            self.scr = tscr

        def has(self, way, step, chunk):
            return 0 <= step < half and (step > 0 or way == chunk)

        def copy(self, way, step, chunk):
            sem = self.base + (way * half + step) * 2 + chunk
            piece = pl.ds(chunk * mid_row, mid_row)
            return remote(
                self.send.at[way, step, piece],
                self.recv.at[way, step, piece],
                sem,
                sem,
                gy=right if way == 0 else left,
            )

        def term(self, step):
            first = self.weight_rows(index_of(place + half - step))
            if 0 < step < half:
                weight = jnp.concatenate(
                    [first, self.weight_rows(index_of(place - half + step))], axis=0
                )
            else:
                weight = first
            wide = weight.shape[0]

            @pl.loop(0, 2)
            def _(piece):
                at = pl.ds(pl.multiple_of(piece * mid_row, mid_row), mid_row)
                self.scr[at, 0:wide] = dot_nt(self.lhs[at, :], weight)

        def put(self, step):
            for chunk in range(2):
                at = pl.ds(chunk * mid_row, mid_row)
                for way in range(2):
                    if not self.has(way, step, chunk):
                        continue
                    lane = 0 if step == 0 or way == 0 else width
                    value = self.scr[at, lane : lane + width]
                    if self.has(way, step - 1, chunk):
                        self.copy(way, step - 1, chunk).wait_recv()
                        value = value + self.recv[way, step - 1, at, :].astype(f32)
                    self.send[way, step, at, :] = value.astype(bf)
                    launch(self.copy(way, step, chunk))

        def step(self, step):
            self.term(step)
            self.put(step)

        def finish(self):
            self.term(half)
            total = self.scr[:, 0:width]
            for way in range(2):
                for chunk in range(2):
                    self.copy(way, half - 1, chunk).wait_recv()
                total = total + self.recv[way, half - 1].astype(f32)
            return total

    class Gather:
        def __init__(self, view):
            self.view, self.base = view, take(3)

        def copy(self, which):
            shard = opp if which == 2 else i
            to = opp if which == 1 else sib
            ref = self.view(shard)
            return remote(ref, ref, self.base + which, self.base + which, gx=to)

        def start(self):
            launch(self.copy(1))
            launch(self.copy(0))

        def forward(self):
            self.copy(1).wait_recv()
            launch(self.copy(2))

        def finish(self):
            self.copy(0).wait_recv()
            self.copy(2).wait_recv()

    class RowSum:
        def __init__(self, term, from_sib, sent, from_opp, out):
            self.refs = (term, from_sib, sent, from_opp, out)
            self.base = take(2)

        def first(self):
            term, from_sib = self.refs[:2]
            return remote(term.at[1 - core], from_sib, self.base, self.base, gx=sib)

        def second(self):
            sent, from_opp = self.refs[2:4]
            return remote(sent, from_opp, self.base + 1, self.base + 1, gx=opp)

        def start(self):
            launch(self.first())

        def cross(self):
            term, from_sib, sent = self.refs[:3]
            self.first().wait_recv()
            sent[...] = (
                term[core, 1 - plane].astype(f32) + from_sib[1 - plane].astype(f32)
            ).astype(bf)
            launch(self.second())

        def finish(self):
            term, from_sib, _, from_opp, out = self.refs
            self.second().wait_recv()
            out[...] = (
                term[core, plane].astype(f32)
                + from_sib[plane].astype(f32)
                + from_opp[...].astype(f32)
            )

    ring_tok, ring_cot = Ring(tg, rows_pad), Ring(cg, rows_pad)
    ring_att, ring_grad = Ring(ag, rows_pad), Ring(hg, rows_pad)
    quarter = full // 4
    ring_proj = Ring(projg.at[i], quarter)
    gat_qkv = Gather(lambda shard: wqkv.at[pl.ds(pl.multiple_of(shard * quarter, quarter), quarter)])
    gat_fc1 = Gather(lambda shard: wfc1.at[pl.ds(pl.multiple_of(shard * quarter, quarter), quarter)])
    gat_proj = Gather(lambda shard: projg.at[shard])
    sum_qkv = RowSum(tq, tqs, tqc, tqx, gqkv_ref)
    sum_proj = RowSum(tp, tps, tpc, tpx, gproj_ref)
    sum_fc1 = RowSum(t1, t1s, t1c, t1x, gfc1_ref)

    class Spread:
        def __init__(self, src, view, number):
            self.src, self.view = src, view
            self.sends, self.recvs = take(parts), take(parts)

        def start(self):
            for step in range(1, parts):
                to = (me + step) % parts
                launch(
                    remote(self.src(to), self.view(me), self.sends + step, self.recvs + me, gy=to)
                )

        def wait(self, other):
            remote(self.src(other), self.view(other), self.sends, self.recvs + other, gy=other).wait_recv()

        def finish(self):
            for step in range(1, parts):
                self.wait((me + step) % parts)

    all_vecs = Spread(lambda to: vec_ref, lambda who: vecs.at[who], 0)
    all_stats = [
        Spread(lambda to, k=k: st_mine.at[k], lambda who, k=k: st_all.at[k, who], 0) for k in range(2)
    ]

    barrier = pltpu.get_barrier_semaphore()
    for step in range(1, parts):
        pl.semaphore_signal(
            barrier, inc=1, device_id={"gy": (me + step) % parts}, device_id_type=MESH
        )
    for to in (sib, opp, dia):
        pl.semaphore_signal(barrier, inc=1, device_id={"gx": to}, device_id_type=MESH)
    whole_rows = count // 16 * 16

    def take_rows(dest, src):
        dest[me, 0:whole_rows, :] = src[0:whole_rows, :]
        dest[me, whole_rows:rows_pad, :] = jnp.zeros((rows_pad - whole_rows, width), bf)
        if count > whole_rows:
            dest[me, whole_rows:count, :] = src[whole_rows:count, :]

    take_rows(tg, tok_ref)
    own_vectors = (
        gain1_ref,
        shift1_ref,
        bproj_ref,
        satt_ref,
        gain2_ref,
        shift2_ref,
        smlp_ref,
        bfc2_ref,
    )
    for at, ref in enumerate(own_vectors):
        vec_ref[at : at + 1, :] = ref[...].reshape(1, width)
    wqkv[pl.ds(pl.multiple_of(i * quarter, quarter), quarter), :] = qkv_ref[...]
    pl.semaphore_wait(barrier, parts + 2)

    ring_tok.start(0)
    ring_tok.start(1)
    gat_qkv.start()
    all_vecs.start()
    vecs[me] = vec_ref[...]
    take_rows(cg, cot_ref)
    projg[i, me] = proj_ref[...]
    wfc1[pl.ds(pl.multiple_of(i * quarter, quarter), quarter), :] = fc1_ref[...]
    ring_tok.advance(0)
    lines = fc2_ref.shape[0] // 2
    part = lines // 2
    fc2_cross = take(2)
    crosses = [
        remote(
            fc2_ref.at[pl.ds(pl.multiple_of(block * lines + (1 - plane) * part, part), part)],
            fc2x.at[block],
            fc2_cross + block,
            fc2_cross + block,
            gx=opp,
        )
        for block in range(2)
    ]
    gat_qkv.forward()
    for cross in crosses:
        launch(cross)
    ring_tok.advance(1)
    gat_fc1.start()
    ring_tok.advance(2)
    ring_proj.start(0)
    ring_proj.start(1)
    gat_qkv.finish()
    ring_tok.advance(3) if half > 3 else None
    for step in range(4, half):
        ring_tok.advance(step)
    is_owner = core == (me // 2) % 2
    spread_send, spread_recv = take(4), take(parts)

    def fc2_copy(block):
        if block < 2:
            source = fc2_ref.at[pl.ds(pl.multiple_of(block * lines + plane * part, part), part)]
        else:
            source = fc2x.at[block - 2]
        target = 2 * (i if block < 2 else opp) + block % 2
        return target, source, remote(
            source, fc2h.at[plane, me], spread_send + block, spread_recv + me, gy=target
        )

    def spread_fc2():
        for cross in crosses:
            cross.wait_recv()
        for block in range(4):
            target, source, copy = fc2_copy(block)

            @pl.when(target != me)
            def _():
                copy.start()

            @pl.when(target == me)
            def _():
                fc2h[plane, me] = source[...]

    pass_sem = take(3)
    fc2_sib = remote(fc2h.at[plane], fc2h.at[plane], pass_sem, pass_sem, gx=sib)
    fc2_opp = remote(fc2h.at[plane], fc2h.at[plane], pass_sem + 1, pass_sem + 1, gx=opp)
    fc2_far = remote(fc2h.at[1 - plane], fc2h.at[1 - plane], pass_sem + 2, pass_sem + 2, gx=sib)

    def pass_fc2():
        @pl.when(is_owner)
        def _():
            for step in range(1, parts):
                other = (me + step) % parts
                ref = fc2h.at[plane, other]
                remote(ref, ref, spread_send, spread_recv + other, gy=other).wait_recv()
            fc2_opp.start()
            fc2_sib.start()

    def forward_fc2():
        @pl.when(is_owner)
        def _():
            fc2_opp.wait_recv()
            fc2_far.start()

    def finish_fc2():
        @pl.when(jnp.logical_not(is_owner))
        def _():
            fc2_sib.wait_recv()
            fc2_far.wait_recv()

        for at in range(parts):
            for piece in range(2):
                wfc2[piece * part : (piece + 1) * part, at * width : (at + 1) * width] = fc2h[piece, at]

    spread_fc2()
    ring_cot.start(0)
    ring_cot.start(1)
    all_vecs.finish()

    GAIN1, SHIFT1, BPROJ, SATT, GAIN2, SHIFT2, SMLP = range(7)
    FC2B = 7

    def vec_block(block, which):
        return vecs[block, which : which + 1, :]

    def row_tile(number, size=tile):
        return pl.ds(pl.multiple_of(number * size, size), size)

    def normalise(blocks, gain, shift, rows, slot, dest):
        acc = blocks[0]
        for block in blocks[1:]:
            acc = acc + block
        row_mean = jnp.sum(acc, axis=1, keepdims=True) * (1.0 / full)
        blocks = [block - row_mean for block in blocks]
        acc = blocks[0] * blocks[0]
        for block in blocks[1:]:
            acc = acc + block * block
        inv = lax.rsqrt(jnp.sum(acc, axis=1, keepdims=True) * (1.0 / full) + EPS)
        for at in range(parts):
            value = blocks[at] * inv * vec_block(at, gain) + vec_block(at, shift)
            dest[rows, at * width : (at + 1) * width] = value.astype(bf)
        stat[slot, rows, :] = row_mean
        stat[slot + 1, rows, :] = inv

    @pl.loop(0, 4)
    def _(number):
        rows = row_tile(number)
        normalise([tg[at, rows, :].astype(f32) for at in range(parts)], GAIN1, SHIFT1, rows, 0, nb)

    qv_row = qv_ref[...].reshape(1, heads * 2 * HD)
    blank = jnp.zeros((1, HD), f32)
    pieces = []
    for head in range(heads):
        at = head * 2 * HD
        pieces += [qv_row[:, at : at + HD], blank, qv_row[:, at + HD : at + 2 * HD]]
    qkv_bias = jnp.concatenate(pieces, axis=1)
    lane = lax.broadcasted_iota(jnp.int32, (1, three), 1)
    qkv_scale = jnp.where(lane % (3 * HD) < HD, HD ** (-0.5), 1.0).astype(f32)

    @pl.loop(0, 2)
    def _(number):
        rows = row_tile(number, mid_row)
        mixed = dot_nn(nb[rows, :], wqkv[...])
        mixf[rows, :] = mixed
        qkvb[rows, :] = ((mixed + qkv_bias) * qkv_scale).astype(bf)

    kv_sem = take(1)
    kv_copy = remote(qkvb, qkvo, kv_sem, kv_sem, gx=sib)
    launch(kv_copy)
    ring_proj.advance(0)
    ring_cot.advance(0)
    gat_fc1.forward()
    zero_half = jnp.zeros((qpad - rows_pad, 2 * HD), bf)
    for head in range(heads):
        at = head * 3 * HD
        query = qkvb[:, at : at + HD]
        qz[head, 0:rows_pad, :] = jnp.concatenate([query, jnp.zeros_like(query)], axis=1)
        qz[head, rows_pad:qpad, :] = zero_half
        kvc[head, 0:rows_pad, :] = qkvb[:, at + HD : at + 3 * HD]
    kv_copy.wait_recv()
    for head in range(heads):
        at = head * 3 * HD
        kvc[head, rows_pad : 2 * rows_pad, :] = qkvo[:, at + HD : at + 3 * HD]
        kvt[head] = jnp.transpose(kvc[head])
    ring_proj.advance(1)

    lo = count // 8 * 8
    qtile = 256
    qtiles = qpad // qtile

    def mask_keys(scores):
        pieces = []
        for base in (0, rows_pad):
            pieces.append(scores[base : base + lo])
            edge = scores[base + lo : base + rows_pad]
            index = lax.broadcasted_iota(jnp.int32, edge.shape, 0) + lo
            pieces.append(jnp.where(index < count, edge, -1e30))
        return jnp.concatenate(pieces, axis=0)

    def attend_tile(number):
        cols = slice(number * qtile, (number + 1) * qtile)
        for head in range(heads):
            scores = mask_keys(dot_nt(kvc[head], qz[head, cols, :]))
            top = jnp.max(scores, axis=0, keepdims=True)
            exponent = jnp.exp(scores - top)
            total = jnp.sum(exponent, axis=0, keepdims=True)
            probs = (exponent * (1.0 / total)).astype(bf)
            pt[head, :, cols] = probs
            result = dot_nn(kvt[head, HD : 2 * HD, :], probs).astype(bf)
            att[head * HD : (head + 1) * HD, cols] = result
        stop = min((number + 1) * qtile, rows_pad)
        got = jnp.transpose(att[:, cols])
        ag[me, number * qtile : stop, :] = got[0 : stop - number * qtile]

    sent_chunks = 0
    for number in range(qtiles):
        attend_tile(number)
        if number == 0:
            ring_cot.advance(1)
            pass_fc2()
            ring_proj.advance(2)
            gat_fc1.finish()
        if number == 1:
            for step in range(3, half):
                ring_proj.advance(step)
            gat_proj.start()
        while sent_chunks < 2 and (number + 1) * qtile >= (sent_chunks + 1) * mid_row:
            ring_att.start(sent_chunks)
            sent_chunks += 1
    ring_att.advance(0)
    gat_proj.forward()
    ring_cot.advance(2)
    ring_att.advance(1)
    forward_fc2()
    for step in range(3, half):
        ring_cot.advance(step)

    @pl.loop(0, 4)
    def _(number):
        rows = row_tile(number)
        for at in range(parts):
            gm[rows, at * width : (at + 1) * width] = (
                cg[at, rows, :].astype(f32) * vec_block(at, SMLP)
            ).astype(bf)

    ring_att.advance(2)
    gat_proj.finish()
    for shard in range(4):
        for at in range(parts):
            wproj[shard * quarter : (shard + 1) * quarter, at * width : (at + 1) * width] = projg[shard, at]

    def weigh(which, weight):
        whole = jnp.concatenate([vec_block(at, which) for at in range(parts)], axis=1)
        high, low = split_high(jnp.broadcast_to(whole, (16, full)))
        return (dot_nn(high, weight) + dot_nn(low, weight))[0:1]

    gain_fc1 = weigh(GAIN2, wfc1[...])
    shift_fc1 = weigh(SHIFT2, wfc1[...])
    gain_qkv = weigh(GAIN1, wqkv[...])
    shift_qkv = weigh(SHIFT1, wqkv[...])
    for step in range(3, half):
        ring_att.advance(step)

    @pl.loop(0, 4)
    def _(number):
        rows = row_tile(number)
        whole = jnp.concatenate([ag[at, rows, :] for at in range(parts)], axis=1)
        result = dot_nn(whole, wproj[...])
        blocks = []
        for at in range(parts):
            attn = result[:, at * width : (at + 1) * width] + vec_block(at, BPROJ)
            ao[at, rows, :] = attn
            blocks.append(tg[at, rows, :].astype(f32) + vec_block(at, SATT) * attn)
        normalise(blocks, GAIN2, SHIFT2, rows, 2, nt)

    fc1_bias = bfc1_ref[...].reshape(1, hidden_width)
    cs_acc[...] = jnp.zeros_like(cs_acc)
    finish_fc2()

    @pl.loop(0, 2)
    def _(number):
        rows = row_tile(number, mid_row)
        gh[rows, :] = dot_nt(gm[rows, :], wfc2[...])


    @pl.loop(0, 4)
    def _(number):
        rows = row_tile(number)
        raw = dot_nn(nt[rows, :], wfc1[...])
        act = raw + fc1_bias
        cdf = normal_cdf(act)
        hid[rows, :] = (act * cdf).astype(bf)
        slope = cdf + act * jnp.exp(-0.5 * act * act) * INV_ROOT_TAU
        grad = gh[rows, :] * slope
        cs_acc[...] += jnp.sum(grad.reshape(tile // 8, 8, hidden_width), axis=0)
        gpb[rows, :] = grad.astype(bf)
        prod[rows, 0:hidden_width] = (grad * (raw - shift_fc1)).astype(bf)

    def row_sums(slot, weights, grads, products):
        wide = grads.shape[1]
        high, low = split_high(jnp.broadcast_to(weights, (8, wide)))
        ones = jnp.ones((8, wide), bf)
        first = dot_nt(high, grads) + dot_nt(low, grads)
        second = dot_nt(ones, products)
        st_mine[slot, 0:1, 0:rows_pad] = first[0:1]
        st_mine[slot, 1:2, 0:rows_pad] = second[0:1]
        all_stats[slot].start()
        st_all[slot, me] = st_mine[slot]

    def total_sums(slot):
        all_stats[slot].finish()
        total = st_all[slot, 0]
        for at in range(1, parts):
            total = total + st_all[slot, at]
        st_sum[...] = jnp.zeros_like(st_sum)
        st_sum[0:2, :] = total
        turned = jnp.transpose(st_sum[...])
        return turned[0:rows_pad, 0:1] * (1.0 / full), turned[0:rows_pad, 1:2] * (1.0 / full)

    scat_two = Scatter(0, gpb, lambda who: wfc1[pl.ds(pl.multiple_of(who * width, width), width), :])
    scat_two.term(0)
    scat_two.put(0)
    st_mine[...] = jnp.zeros_like(st_mine)
    row_sums(0, gain_fc1, gpb[...], prod[:, 0:hidden_width])
    for step in range(1, half):
        scat_two.step(step)

    def fc2_cols(who):
        return wfc2[:, pl.ds(pl.multiple_of(who * width, width), width)]

    class ScatterPlain(Scatter):
        def term(self, step):
            first = self.weight_rows(index_of(place + half - step))
            if 0 < step < half:
                weight = jnp.concatenate(
                    [first, self.weight_rows(index_of(place - half + step))], axis=1
                )
            else:
                weight = first
            wide = weight.shape[1]

            @pl.loop(0, 2)
            def _(piece):
                at = pl.ds(pl.multiple_of(piece * mid_row, mid_row), mid_row)
                self.scr[at, 0:wide] = dot_nn(self.lhs[at, :], weight)

    scat_mlp = ScatterPlain(1, hid, fc2_cols)
    scat_mlp.step(0)

    def fc2_grad(number):
        result = dot_tn(hid[...], gm[:, number * 256 : (number + 1) * 256]).astype(bf)
        for piece in range(2):
            for side in range(2):
                t2[piece, 2 * number + side] = result[
                    piece * part : (piece + 1) * part, side * width : (side + 1) * width
                ]

    for number in range(parts // 2):
        fc2_grad(number)
    sib_sem = take(1)
    t2_pass = remote(t2, t2s, sib_sem, sib_sem, gx=sib)

    @pl.when(jnp.logical_not(is_owner))
    def _():
        t2_pass.start()

    grad_two = scat_two.finish()
    first, second = total_sums(0)
    upstream = cg[me].astype(f32)
    attn_own = ao[me]
    satt_own = vecs[me, SATT : SATT + 1, :]
    mid_value = tg[me].astype(f32) + satt_own * attn_own
    mid_own[...] = mid_value
    inv_two = stat[3]
    normed = (mid_value - stat[2]) * inv_two
    gain_own = vecs[me, GAIN2 : GAIN2 + 1, :]
    grad_mid = upstream + inv_two * (grad_two * gain_own - first - normed * second)
    gmid[...] = grad_mid
    grad_attn = grad_mid * satt_own
    hg[me] = grad_attn.astype(bf)
    ring_grad.start(0)
    ring_grad.start(1)

    def col_sum(value):
        return jnp.sum(value, axis=0, keepdims=True)

    sm[...] = jnp.zeros_like(sm)
    sm[5:6, :] = col_sum(grad_attn)
    sm[6:7, :] = col_sum(grad_mid * attn_own)
    sm[7:8, :] = col_sum(grad_two * normed)
    sm[8:9, :] = col_sum(grad_two)
    fc1_sum = col_sum(cs_acc[...])
    for at in range(hidden_width // width):
        sm[16 + at : 17 + at, :] = fc1_sum[:, at * width : (at + 1) * width]

    def rows_grad(dest, left_of, grads):
        for shard in range(4):
            dest[shard % 2, shard // 2] = dot_tn(left_of(shard), grads).astype(bf)

    rows_grad(t1, lambda shard: nt[:, shard * quarter : (shard + 1) * quarter], gpb[...])
    sum_fc1.start()
    ring_grad.advance(0)
    blocks_in = quarter // width
    rows_grad(
        tp,
        lambda shard: jnp.concatenate(
            [ag[shard * blocks_in + b] for b in range(blocks_in)], axis=1
        ),
        hg[me],
    )
    sum_proj.start()
    sum_fc1.cross()

    t2_recv = take(parts)
    t2_send = take(parts)

    def t2_copy(step):
        to = (me + step) % parts
        return remote(t2d.at[to], t2r.at[me], t2_send + step, t2_recv + me, gy=to)

    plane_sem = take(1)
    t2_plane = remote(t2c, t2o, plane_sem, plane_sem, gx=opp)

    @pl.when(is_owner)
    def _():
        t2_pass.wait_recv()
        for at in range(parts):
            t2c[at] = (t2[1 - plane, at].astype(f32) + t2s[1 - plane, at].astype(f32)).astype(bf)
        t2_plane.start()

    ring_grad.advance(1)
    scat_mlp.step(1)
    sum_proj.cross()
    ring_grad.advance(2)
    for step in range(3, half):
        ring_grad.advance(step)
    own_rows = pl.ds(pl.multiple_of(me * width, width), width)

    @pl.loop(0, 4)
    def _(number):
        rows = row_tile(number)
        whole = jnp.concatenate([hg[at, rows, :] for at in range(parts)], axis=1)
        gat[rows, :] = dot_nt(whole, wproj[own_rows, :]).astype(bf)

    gat[rows_pad:qpad, :] = jnp.zeros((qpad - rows_pad, 2 * HD), bf)
    gatt = jnp.transpose(gat[...])
    delta_all = gatt.astype(f32) * att[...].astype(f32)
    for head in range(heads):
        value = gat[:, head * HD : (head + 1) * HD]
        dz[head] = jnp.concatenate([jnp.zeros_like(value), value], axis=1)
    deltas = [
        jnp.sum(delta_all[head * HD : (head + 1) * HD], axis=0, keepdims=True) for head in range(heads)
    ]
    dkv[...] = jnp.zeros_like(dkv)

    def attend_back(number):
        cols = slice(number * qtile, (number + 1) * qtile)
        for head in range(heads):
            probs = pt[head, :, cols]
            query, grad = qz[head, cols, :], dz[head, cols, :]
            slope = dot_nt(kvc[head], grad)
            scores = (probs.astype(f32) * (slope - deltas[head][:, cols])).astype(bf)
            dkv[head] += dot_nn(probs, grad) + dot_nn(scores, query)
            dqf[head * HD : (head + 1) * HD, cols] = dot_nn(kvt[head, 0:HD, :], scores)

    next_step = 2
    for number in range(qtiles):
        attend_back(number)
        if next_step < half:
            scat_mlp.step(next_step)
            next_step += 1
    for step in range(next_step, half):
        scat_mlp.step(step)

    for head in range(heads):
        dks[head] = dkv[head, rows_pad : 2 * rows_pad, :].astype(bf)
    dk_sem = take(1)
    dk_copy = remote(dks, dkr, dk_sem, dk_sem, gx=sib)
    launch(dk_copy)

    @pl.when(is_owner)
    def _():
        t2_plane.wait_recv()
        for at in range(parts):
            t2d[at] = (
                t2[plane, at].astype(f32) + t2s[plane, at].astype(f32) + t2o[at].astype(f32)
            ).astype(bf)
        for step in range(1, parts):
            t2_copy(step).start()
        t2r[me] = t2d[me]

    grad_query = jnp.transpose(dqf[...])[0:rows_pad] * (HD ** (-0.5))
    sm[0:1, :] = col_sum(grad_query)
    dk_copy.wait_recv()
    pieces = []
    value_sums = []
    for head in range(heads):
        own = dkv[head, 0:rows_pad, :] + dkr[head].astype(f32)
        value_sums.append(col_sum(own))
        pieces += [grad_query[:, head * HD : (head + 1) * HD], own]
    for head in range(heads):
        sm[1 + head : 2 + head, :] = value_sums[head]
    mixed_grad = jnp.concatenate(pieces, axis=1)
    gmx[...] = mixed_grad.astype(bf)
    prod[:, 0:three] = (mixed_grad * (mixf[...] - shift_qkv)).astype(bf)

    scat_one = Scatter(2, gmx, lambda who: wqkv[pl.ds(pl.multiple_of(who * width, width), width), :])
    scat_one.step(0)
    row_sums(1, gain_qkv, gmx[...], prod[:, 0:three])
    rows_grad(tq, lambda shard: nb[:, shard * quarter : (shard + 1) * quarter], gmx[...])
    sum_qkv.start()
    scat_one.step(1)

    mlp_out = scat_mlp.finish() + vecs[me, FC2B : FC2B + 1, :]
    smlp_own = vecs[me, SMLP : SMLP + 1, :]
    up = cg[me].astype(f32)
    out_ref[...] = (mid_own[...] + smlp_own * mlp_out)[0:count]
    sm[9:10, :] = col_sum(up * smlp_own)
    sm[10:11, :] = col_sum(up * mlp_out)
    sum_qkv.cross()
    scat_one.step(2)
    sum_fc1.finish()
    sum_proj.finish()

    for step in range(4):
        source = (step // 2) * (parts // 2) + 2 * core + step % 2

        @pl.when(source != me)
        def _():
            remote(t2d.at[me], t2r.at[source], t2_send, t2_recv + source, gy=source).wait_recv()

    x_sem = take(1)
    t2_cross = remote(t2r.at[pl.ds(2 * opp, 2)], t2x, x_sem, x_sem, gx=opp)
    launch(t2_cross)
    for step in range(3, half):
        scat_one.step(step)
    t2_cross.wait_recv()
    for block in range(2):
        for at, value in ((plane, t2r[2 * i + block]), (1 - plane, t2x[block])):
            rows = pl.ds(pl.multiple_of(block * lines + at * part, part), part)
            gfc2_ref[rows, :] = value.astype(f32)
    sum_qkv.finish()

    grad_one = scat_one.finish()
    first, second = total_sums(1)
    inv_one = stat[1]
    normed = (tg[me].astype(f32) - stat[0]) * inv_one
    gain_own = vecs[me, GAIN1 : GAIN1 + 1, :]
    gin_ref[...] = (gmid[...] + inv_one * (grad_one * gain_own - first - normed * second))[0:count]
    sm[3:4, :] = col_sum(grad_one * normed)
    sm[4:5, :] = col_sum(grad_one)
    sma[i] = sm[...]
    small_sem = take(3)
    copies = [
        remote(sm, sma.at[i], small_sem + n, small_sem + n, gx=to)
        for n, to in enumerate((sib, opp, dia))
    ]
    for copy in copies:
        launch(copy)
    for copy in copies:
        copy.wait_recv()
    small_ref[...] = sma[0] + sma[1] + sma[2] + sma[3]

    for copy in started:
        copy.wait_send()
    for block in range(4):
        target, _, copy = fc2_copy(block)

        @pl.when(target != me)
        def _():
            copy.wait_send()

    @pl.when(is_owner)
    def _():
        fc2_opp.wait_send()
        fc2_sib.wait_send()
        fc2_far.wait_send()
        t2_plane.wait_send()
        for step in range(1, parts):
            t2_copy(step).wait_send()

    @pl.when(jnp.logical_not(is_owner))
    def _():
        t2_pass.wait_send()


def emit_kernel(heads, hidden_width, small_ref, *refs):
    sources, results = refs[:6], refs[6:22]
    for source, result in zip(sources, results):
        result[...] = source[...]
    qv_ref, fc1_ref = results[6:8]
    width = small_ref.shape[1]
    for head in range(heads):
        row = jnp.concatenate(
            [small_ref[0:1, head * HD : (head + 1) * HD], small_ref[1 + head : 2 + head, HD : 2 * HD]],
            axis=1,
        )
        qv_ref[head * 2 * HD : (head + 1) * 2 * HD] = row.reshape(2 * HD)
    for at in range(hidden_width // width):
        fc1_ref[at * width : (at + 1) * width] = small_ref[16 + at : 17 + at, :].reshape(width)
    for at, ref in enumerate(results[8:]):
        ref[...] = small_ref[3 + at : 4 + at, :].reshape(width)


def on_device(*args):
    (
        tokens,
        cotangent,
        norm1_gain,
        norm1_shift,
        qkv_weight,
        qv_bias,
        proj_weight,
        proj_bias,
        scale_attn,
        norm2_gain,
        norm2_shift,
        fc1_weight,
        fc1_bias,
        fc2_weight,
        fc2_bias,
        scale_mlp,
    ) = args
    parts, rows_over = lax.axis_size("gy"), lax.axis_size("gx")
    count, width = tokens.shape
    heads = qkv_weight.shape[1] // (3 * HD)
    hidden_width = fc1_weight.shape[1]
    if (
        rows_over != 4
        or parts != 8
        or width != 128
        or heads != 2
        or IMGS != 1
        or hidden_width % 256
    ):
        return on_device_plain(*args)
    full = parts * width
    rows = up_to(count, 64)
    qpad = up_to(rows, 256)
    three = heads * 3 * HD
    quarter = full // 4
    lines = fc2_weight.shape[0] // 2
    half = parts // 2
    bf, f32 = jnp.bfloat16, jnp.float32
    wide = max(three, hidden_width)
    stat_wide = up_to(rows, 256)
    V = pltpu.VMEM
    scratch = [
        V((parts, rows, width), bf),
        V((parts, rows, width), bf),
        V((parts, rows, width), bf),
        V((parts, rows, width), bf),
        V((parts, 8, width), f32),
        V((full, three), bf),
        V((full, hidden_width), bf),
        V((4, parts, quarter, width), bf),
        V((full, full), bf),
        V((2, lines // 2, width), bf),
        V((2, parts, lines // 2, width), bf),
        V((lines, full), bf),
        V((rows, full), bf),
        V((rows, full), bf),
        V((rows, full), bf),
        V((4, rows, 1), f32),
        V((rows, three), f32),
        V((rows, three), bf),
        V((rows, three), bf),
        V((heads, 2 * rows, 2 * HD), bf),
        V((heads, 2 * HD, 2 * rows), bf),
        V((heads, qpad, 2 * HD), bf),
        V((heads, qpad, 2 * HD), bf),
        V((heads, 2 * rows, qpad), bf),
        V((heads * HD, qpad), bf),
        V((8, width), f32),
        V((parts, rows, width), f32),
        V((rows, hidden_width), f32),
        V((rows, hidden_width), bf),
        V((rows, hidden_width), bf),
        V((rows, wide), bf),
        V((rows, 2 * width), f32),
        V((3, 2, half, rows, width), bf),
        V((3, 2, half, rows, width), bf),
        V((2, 2, stat_wide), f32),
        V((2, parts, 2, stat_wide), f32),
        V((8, stat_wide), f32),
        V((rows, width), f32),
        V((rows, width), f32),
        V((qpad, width), bf),
        V((heads, 2 * rows, 2 * HD), f32),
        V((heads, rows, 2 * HD), bf),
        V((heads, rows, 2 * HD), bf),
        V((heads * HD, qpad), f32),
        V((rows, three), bf),
        V((2, 2, quarter, three), bf),
        V((2, quarter, three), bf),
        V((quarter, three), bf),
        V((quarter, three), bf),
        V((2, 2, quarter, width), bf),
        V((2, quarter, width), bf),
        V((quarter, width), bf),
        V((quarter, width), bf),
        V((2, 2, quarter, hidden_width), bf),
        V((2, quarter, hidden_width), bf),
        V((quarter, hidden_width), bf),
        V((quarter, hidden_width), bf),
        V((2, parts, lines // 2, width), bf),
        V((2, parts, lines // 2, width), bf),
        V((parts, lines // 2, width), bf),
        V((parts, lines // 2, width), bf),
        V((parts, lines // 2, width), bf),
        V((parts, lines // 2, width), bf),
        V((2, lines // 2, width), bf),
        V((24, width), f32),
        V((4, 24, width), f32),
        V((8, hidden_width), f32),
        pltpu.SemaphoreType.DMA((SEMS,)),
        pltpu.SemaphoreType.DMA((SEMS,)),
    ]
    vmem = pl.BlockSpec(memory_space=pltpu.VMEM)
    results = pl.pallas_call(
        functools.partial(mega_kernel, parts, count, heads, hidden_width, SEMS),
        out_shape=[
            jax.ShapeDtypeStruct((count, width), f32),
            jax.ShapeDtypeStruct((count, width), f32),
            jax.ShapeDtypeStruct((24, width), f32),
            jax.ShapeDtypeStruct((quarter, three), f32),
            jax.ShapeDtypeStruct((quarter, width), f32),
            jax.ShapeDtypeStruct((quarter, hidden_width), f32),
            jax.ShapeDtypeStruct((2 * lines, width), f32),
        ],
        in_specs=[vmem] * 16,
        out_specs=[vmem] * 7,
        scratch_shapes=scratch,
        compiler_params=pltpu.CompilerParams(
            collective_id=3, has_side_effects=True, vmem_limit_bytes=VMEM_BYTES
        ),
    )(
        tokens,
        cotangent,
        norm1_gain,
        norm1_shift,
        qkv_weight,
        qv_bias,
        proj_weight,
        proj_bias,
        scale_attn,
        norm2_gain,
        norm2_shift,
        fc1_weight,
        fc1_bias,
        fc2_weight,
        fc2_bias,
        scale_mlp,
    )
    output, grad_in, small, grad_qkv, grad_proj, grad_fc1, grad_fc2 = results
    line = jax.ShapeDtypeStruct((width,), f32)
    large = [output, grad_in, grad_qkv, grad_proj, grad_fc1, grad_fc2]
    written = pl.pallas_call(
        functools.partial(emit_kernel, heads, hidden_width),
        out_shape=[jax.ShapeDtypeStruct(array.shape, f32) for array in large]
        + [
            jax.ShapeDtypeStruct((heads * 2 * HD,), f32),
            jax.ShapeDtypeStruct((hidden_width,), f32),
        ]
        + [line] * 8,
        in_specs=[vmem] * 7,
        out_specs=[vmem] * 16,
    )(small, *large)
    output, grad_in, grad_qkv, grad_proj, grad_fc1, grad_fc2, grad_qv, grad_fc1_bias = written[:8]
    lines_out = written[8:]
    return (
        output,
        grad_in,
        lines_out[0],
        lines_out[1],
        grad_qkv,
        grad_qv,
        grad_proj,
        lines_out[2],
        lines_out[3],
        lines_out[4],
        lines_out[5],
        grad_fc1,
        grad_fc1_bias,
        grad_fc2,
        lines_out[6],
        lines_out[7],
    )


def solution(mesh):
    return jax.shard_map(
        on_device,
        mesh=mesh,
        in_specs=(
            P("gx", "gy"),
            P("gx", "gy"),
            P("gy"),
            P("gy"),
            P("gx", "gy"),
            P("gy"),
            P("gx", "gy"),
            P("gy"),
            P("gy"),
            P("gy"),
            P("gy"),
            P("gx", "gy"),
            P("gy"),
            P("gx", "gy"),
            P("gy"),
            P("gy"),
        ),
        out_specs=(
            P("gx", "gy"),
            P("gx", "gy"),
            P("gy"),
            P("gy"),
            P("gx", "gy"),
            P("gy"),
            P("gx", "gy"),
            P("gy"),
            P("gy"),
            P("gy"),
            P("gy"),
            P("gx", "gy"),
            P("gy"),
            P("gx", "gy"),
            P("gy"),
            P("gy"),
        ),
        check_vma=False,
    )
```

```python
import functools

import jax
import jax.numpy as jnp
from jax import lax
from jax.experimental import pallas as pl
from jax.experimental.pallas import tpu as pltpu
from jax.sharding import PartitionSpec as P

D = 1024
HD = 64
IMGS = 1


EPS = 1e-06
ROOT_HALF = 0.7071067811865476
INV_ROOT_TAU = 0.3989422804014327
SEMS = 400
VMEM_BYTES = 62 * 1024 * 1024


def from_partner(block, axis, bit):
    count = lax.axis_size(axis)
    route = []
    for low in range(count):
        high = low | 1 << bit
        if high != low and high < count:
            route += [(low, high), (high, low)]
    return lax.ppermute(block, axis, route)


def normal_cdf(values):
    return 0.5 * (1.0 + jax.scipy.special.erf(values * ROOT_HALF))


def gelu_exact(values):
    return values * normal_cdf(values)


def gelu_slope(values):
    return normal_cdf(values) + values * jnp.exp(-0.5 * values * values) * INV_ROOT_TAU


def norm_full(rows, gain, shift):
    row_mean = jnp.mean(rows, axis=1, keepdims=True)
    inv_std = lax.rsqrt(jnp.mean(rows * rows, axis=1, keepdims=True) - row_mean * row_mean + EPS)
    normed = (rows - row_mean) * inv_std
    return (normed, inv_std, (normed * gain + shift).astype(jnp.bfloat16))


def gather_columns(block):
    return lax.all_gather(block, "gy", axis=1, tiled=True)


def ring_kernel(parts, block_ref, out_ref, send_sem, recv_sem):
    half = parts // 2

    def index_of(place):
        back = place // half
        return (1 - back) * (2 * place) + back * (2 * (parts - 1 - place) + 1)

    me = lax.axis_index("gy")
    odd = me % 2
    place = (1 - odd) * (me // 2) + odd * (parts - 1 - me // 2)
    sides = (index_of((place + 1) % parts), index_of((place + parts - 1) % parts))
    barrier = pltpu.get_barrier_semaphore()
    for side in sides:
        pl.semaphore_signal(
            barrier, inc=1, device_id={"gy": side}, device_id_type=pl.DeviceIdType.MESH
        )
    pl.semaphore_wait(barrier, 2)
    copies = []
    for step in range(half):
        owners = (
            index_of((place + parts - step) % parts),
            index_of((place + step) % parts),
        )
        started = []
        for way in range(2):
            if way == 1 and step == half - 1:
                continue
            copy = pltpu.make_async_remote_copy(
                src_ref=block_ref if step == 0 else out_ref.at[owners[way]],
                dst_ref=out_ref.at[owners[way]],
                send_sem=send_sem.at[way, step],
                recv_sem=recv_sem.at[way, step],
                device_id={"gy": sides[way]},
                device_id_type=pl.DeviceIdType.MESH,
            )
            copy.start()
            started.append(copy)
        if step == 0:
            out_ref[me] = block_ref[...]
        for copy in started:
            copy.wait_recv()
        copies += started
    for copy in copies:
        copy.wait_send()


def ring_columns(block, call):
    parts = lax.axis_size("gy")
    count, width = block.shape
    if parts % 2 or parts < 4:
        return gather_columns(block)
    got = pl.pallas_call(
        functools.partial(ring_kernel, parts),
        out_shape=jax.ShapeDtypeStruct((parts, count, width), block.dtype),
        in_specs=[pl.BlockSpec(memory_space=pltpu.VMEM)],
        out_specs=pl.BlockSpec(memory_space=pltpu.VMEM),
        scratch_shapes=[
            pltpu.SemaphoreType.DMA((2, parts // 2)),
            pltpu.SemaphoreType.DMA((2, parts // 2)),
        ],
        compiler_params=pltpu.CompilerParams(collective_id=call, has_side_effects=True),
    )(block)
    return jnp.transpose(got, (1, 0, 2)).reshape(count, parts * width)


def spread_columns(block):
    parts = lax.axis_size("gy")
    got = lax.all_to_all(
        jnp.broadcast_to(block[None], (parts,) + block.shape), "gy", 0, 0, tiled=True
    )
    return jnp.transpose(got, (1, 0, 2)).reshape(block.shape[0], parts * block.shape[1])


def column_blocks(block):
    parts = lax.axis_size("gy")
    count, full = block.shape
    return jnp.transpose(block.reshape(count, parts, full // parts), (1, 0, 2))


def scatter_sum(blocks, axis):
    got = lax.all_to_all(blocks, axis, 0, 0, tiled=True)
    return jnp.sum(got.astype(jnp.float32), axis=0)


def own_columns(block, width):
    return lax.dynamic_slice_in_dim(block, lax.axis_index("gy") * width, width, axis=1)


def sum_rows(term):
    parts = lax.axis_size("gx")
    blocks = term.reshape(parts, term.shape[0] // parts, term.shape[1])
    return scatter_sum(blocks, "gx")


def weight_grad_rows(saved, grad_out):
    term = jnp.einsum("tk,tn->kn", saved, grad_out, preferred_element_type=jnp.float32)
    return lax.psum_scatter(
        term.astype(jnp.bfloat16), "gx", scatter_dimension=0, tiled=True
    ).astype(jnp.float32)


def weight_grad(saved, grad_out):
    term = jnp.einsum("tk,tn->kn", saved, grad_out, preferred_element_type=jnp.float32)
    return sum_rows(term.astype(jnp.bfloat16))


def lanes_of(column, width):
    count = column.shape[0]
    lines = -(-count // width)
    return jnp.pad(column, (0, lines * width - count)).reshape(lines, width)


def back_norm(grad_out, weight, normed, normed_own, inv_std, gain, gain_own):
    parts = lax.axis_size("gy")
    count, full = normed.shape
    width = full // parts
    term = jnp.einsum("tn,kn->tk", grad_out, weight, preferred_element_type=jnp.float32)
    scaled = term * gain
    first = lanes_of(jnp.sum(scaled, axis=1), width)
    second = lanes_of(jnp.sum(scaled * normed, axis=1), width)
    lines = first.shape[0]
    sums = jnp.concatenate([first, second], axis=0).astype(jnp.bfloat16)
    blocks = column_blocks(term.astype(jnp.bfloat16))
    sent = jnp.concatenate(
        [blocks, jnp.broadcast_to(sums[None], (parts,) + sums.shape)], axis=1
    )
    back = scatter_sum(sent, "gy")
    grad_normed = back[:count]
    first = back[count : count + lines].reshape(-1)[:count, None]
    second = back[count + lines :].reshape(-1)[:count, None]
    grad_rows = inv_std * (
        grad_normed * gain_own - first / full - normed_own * (second / full)
    )
    return (
        grad_rows,
        jnp.sum(grad_normed * normed_own, axis=0),
        jnp.sum(grad_normed, axis=0),
    )


def on_device_plain(
    tokens,
    cotangent,
    norm1_gain,
    norm1_shift,
    qkv_weight,
    qv_bias,
    proj_weight,
    proj_bias,
    scale_attn,
    norm2_gain,
    norm2_shift,
    fc1_weight,
    fc1_bias,
    fc2_weight,
    fc2_bias,
    scale_mlp,
):
    count = tokens.shape[0]
    half_len = count // IMGS
    heads_here = qkv_weight.shape[1] // (3 * HD)
    factor = HD ** (-0.5)
    width = tokens.shape[1]
    full_tokens = ring_columns(tokens, 0)
    vectors = spread_columns(
        jnp.stack([norm1_gain, norm1_shift, proj_bias, scale_attn, norm2_gain, norm2_shift, scale_mlp])
    )
    gain_one, shift_one, bias_proj, full_scale_attn, gain_two, shift_two, full_scale_mlp = vectors
    full_qkv = lax.all_gather(qkv_weight, "gx", axis=0, tiled=True)
    all_proj = lax.all_gather(ring_columns(proj_weight, 1), "gx", axis=0, tiled=True)
    full_fc1 = lax.all_gather(fc1_weight, "gx", axis=0, tiled=True)
    full_fc2 = lax.all_gather(fc2_weight, "gx", axis=0, tiled=True)
    rows_fc2 = lax.all_to_all(full_fc2, "gy", split_axis=0, concat_axis=1, tiled=True)
    full_cotangent = gather_columns(cotangent)
    inputs = full_tokens.astype(jnp.float32)
    normed_one, inv_one, norm_one = norm_full(inputs, gain_one, shift_one)
    mixed = jnp.dot(norm_one, full_qkv, preferred_element_type=jnp.float32)
    mixed = mixed.reshape(count, heads_here, 3, HD)
    biases = qv_bias.reshape(heads_here, 2, HD)
    queries = (mixed[:, :, 0] + biases[:, 0]).astype(jnp.bfloat16)
    keys = mixed[:, :, 1].astype(jnp.bfloat16)
    values = (mixed[:, :, 2] + biases[:, 1]).astype(jnp.bfloat16)
    lower = lax.axis_index("gx") % 2 == 0
    pair_kv = jnp.concatenate([keys, values], axis=2).reshape(count, heads_here * 2 * HD)
    other_kv = from_partner(pair_kv, "gx", 0)
    first_kv = jnp.where(lower, pair_kv, other_kv)
    second_kv = jnp.where(lower, other_kv, pair_kv)
    image_shape = (IMGS, half_len, heads_here, 2 * HD)
    both_kv = jnp.concatenate(
        [first_kv.reshape(image_shape), second_kv.reshape(image_shape)], axis=1
    )
    key_all = both_kv[..., :HD]
    value_all = both_kv[..., HD:]
    query_img = queries.reshape(IMGS, half_len, heads_here, HD)
    scores = (
        jnp.einsum("iqhe,ikhe->ihqk", query_img, key_all, preferred_element_type=jnp.float32)
        * factor
    )
    row_max = jnp.max(scores, axis=3, keepdims=True)
    exponent = jnp.exp(scores - row_max)
    totals = jnp.sum(exponent, axis=3, keepdims=True)
    log_total = row_max + jnp.log(totals)
    probs = (exponent / totals).astype(jnp.bfloat16)
    attended_img = jnp.einsum(
        "ihqk,ikhe->iqhe", probs, value_all, preferred_element_type=jnp.float32
    ).astype(jnp.bfloat16)
    attended = attended_img.reshape(count, heads_here * HD)
    full_attended = ring_columns(attended, 0)
    attn_out = jnp.dot(full_attended, all_proj, preferred_element_type=jnp.float32) + bias_proj
    middle = inputs + full_scale_attn * attn_out
    normed_two, inv_two, norm_two = norm_full(middle, gain_two, shift_two)
    pre_act = jnp.dot(norm_two, full_fc1, preferred_element_type=jnp.float32) + fc1_bias
    hidden = gelu_exact(pre_act).astype(jnp.bfloat16)
    upstream = cotangent.astype(jnp.float32)
    grad_mlp = upstream * scale_mlp
    grad_fc2_bias = jnp.sum(grad_mlp, axis=0)
    full_grad_mlp_b = (full_cotangent.astype(jnp.float32) * full_scale_mlp).astype(jnp.bfloat16)
    grad_hidden = jnp.einsum(
        "tn,kn->tk", full_grad_mlp_b, rows_fc2, preferred_element_type=jnp.float32
    )
    grad_pre = grad_hidden * gelu_slope(pre_act)
    grad_fc1_bias = jnp.sum(grad_pre, axis=0)
    grad_pre_b = grad_pre.astype(jnp.bfloat16)
    own_two = own_columns(normed_two, width)
    grad_rows, grad_gain_two, grad_shift_two = back_norm(
        grad_pre_b, full_fc1, normed_two, own_two, inv_two, gain_two, norm2_gain
    )
    grad_middle = upstream + grad_rows
    grad_scale_attn = jnp.sum(grad_middle * own_columns(attn_out, width), axis=0)
    grad_attn = grad_middle * scale_attn
    grad_proj_bias = jnp.sum(grad_attn, axis=0)
    grad_attn_b = grad_attn.astype(jnp.bfloat16)
    full_grad_attn_b = ring_columns(grad_attn_b, 0)
    own_rows_proj = lax.dynamic_slice_in_dim(
        all_proj, lax.axis_index("gy") * width, width, axis=0
    )
    grad_attended = jnp.einsum(
        "tn,kn->tk", full_grad_attn_b, own_rows_proj, preferred_element_type=jnp.float32
    ).astype(jnp.bfloat16)
    mlp_term = jnp.dot(hidden, rows_fc2, preferred_element_type=jnp.float32)
    mlp_out = (
        lax.psum_scatter(
            column_blocks(mlp_term.astype(jnp.bfloat16)), "gy", scatter_dimension=0, tiled=False
        ).astype(jnp.float32)
        + fc2_bias
    )
    output = own_columns(middle, width) + scale_mlp * mlp_out
    grad_scale_mlp = jnp.sum(upstream * mlp_out, axis=0)
    fc2_term = jnp.einsum(
        "tk,tn->kn", hidden, full_grad_mlp_b, preferred_element_type=jnp.float32
    )
    fc2_blocks = lax.all_to_all(column_blocks(fc2_term.astype(jnp.bfloat16)), "gy", 0, 0, tiled=True)
    grad_fc2 = sum_rows(fc2_blocks.reshape(-1, width))
    grad_fc1 = weight_grad_rows(norm_two, grad_pre_b)
    grad_proj = weight_grad_rows(full_attended, grad_attn_b)
    grad_att_img = grad_attended.reshape(IMGS, half_len, heads_here, HD)
    recomputed = jnp.exp(scores - log_total)
    probs_b = recomputed.astype(jnp.bfloat16)
    grad_value_all = jnp.einsum(
        "ihqk,iqhe->ikhe", probs_b, grad_att_img, preferred_element_type=jnp.float32
    )
    grad_probs = jnp.einsum(
        "iqhe,ikhe->ihqk", grad_att_img, value_all, preferred_element_type=jnp.float32
    )
    delta = jnp.sum(grad_att_img.astype(jnp.float32) * attended_img.astype(jnp.float32), axis=3)
    grad_scores = recomputed * (grad_probs - jnp.transpose(delta, (0, 2, 1))[..., None])
    grad_scores_b = grad_scores.astype(jnp.bfloat16)
    grad_query = (
        jnp.einsum("ihqk,ikhe->iqhe", grad_scores_b, key_all, preferred_element_type=jnp.float32)
        * factor
    )
    grad_key_all = (
        jnp.einsum("ihqk,iqhe->ikhe", grad_scores_b, query_img, preferred_element_type=jnp.float32)
        * factor
    )
    grad_kv_all = jnp.concatenate([grad_key_all, grad_value_all], axis=3)
    first_part = grad_kv_all[:, :half_len].reshape(count, heads_here * 2 * HD)
    second_part = grad_kv_all[:, half_len:].reshape(count, heads_here * 2 * HD)
    own_part = jnp.where(lower, first_part, second_part)
    sent_part = jnp.where(lower, second_part, first_part)
    grad_kv = own_part + from_partner(sent_part.astype(jnp.bfloat16), "gx", 0).astype(
        sent_part.dtype
    )
    grad_kv = grad_kv.reshape(count, heads_here, 2, HD)
    grad_query = grad_query.reshape(count, heads_here, HD)
    grad_qv_bias = jnp.stack(
        [jnp.sum(grad_query, axis=0), jnp.sum(grad_kv[:, :, 1], axis=0)], axis=1
    ).reshape(heads_here * 2 * HD)
    grad_mixed = (
        jnp.stack([grad_query, grad_kv[:, :, 0], grad_kv[:, :, 1]], axis=2)
        .astype(jnp.bfloat16)
        .reshape(count, heads_here * 3 * HD)
    )
    grad_qkv = weight_grad(norm_one, grad_mixed)
    own_one = own_columns(normed_one, width)
    grad_rows, grad_gain_one, grad_shift_one = back_norm(
        grad_mixed, full_qkv, normed_one, own_one, inv_one, gain_one, norm1_gain
    )
    grad_input = grad_middle + grad_rows
    smalls = lax.psum(
        (
            grad_gain_one,
            grad_shift_one,
            grad_qv_bias,
            grad_proj_bias,
            grad_scale_attn,
            grad_gain_two,
            grad_shift_two,
            grad_fc1_bias,
            grad_fc2_bias,
            grad_scale_mlp,
        ),
        "gx",
    )
    return (
        output,
        grad_input,
        smalls[0],
        smalls[1],
        grad_qkv,
        smalls[2],
        grad_proj,
        smalls[3],
        smalls[4],
        smalls[5],
        smalls[6],
        grad_fc1,
        smalls[7],
        grad_fc2,
        smalls[8],
        smalls[9],
    )


def up_to(value, step):
    return -(-value // step) * step


def dot_nn(a, b):
    return lax.dot_general(a, b, (((1,), (0,)), ((), ())), preferred_element_type=jnp.float32)


def dot_nt(a, b):
    return lax.dot_general(a, b, (((1,), (1,)), ((), ())), preferred_element_type=jnp.float32)


def dot_tn(a, b):
    return lax.dot_general(a, b, (((0,), (0,)), ((), ())), preferred_element_type=jnp.float32)


def split_high(values):
    high = values.astype(jnp.bfloat16)
    return high, (values - high.astype(jnp.float32)).astype(jnp.bfloat16)


def mega_kernel(
    parts,
    count,
    heads,
    hidden_width,
    sems,
    tok_ref,
    cot_ref,
    gain1_ref,
    shift1_ref,
    qkv_ref,
    qv_ref,
    proj_ref,
    bproj_ref,
    satt_ref,
    gain2_ref,
    shift2_ref,
    fc1_ref,
    bfc1_ref,
    fc2_ref,
    bfc2_ref,
    smlp_ref,
    out_ref,
    gin_ref,
    small_ref,
    gqkv_ref,
    gproj_ref,
    gfc1_ref,
    gfc2_ref,
    tg,
    cg,
    ag,
    hg,
    vecs,
    wqkv,
    wfc1,
    projg,
    wproj,
    fc2x,
    fc2h,
    wfc2,
    nb,
    nt,
    gm,
    stat,
    mixf,
    qkvb,
    qkvo,
    kvc,
    kvt,
    qz,
    dz,
    pt,
    att,
    vec_ref,
    ao,
    gh,
    hid,
    gpb,
    prod,
    tscr,
    rs_send,
    rs_recv,
    st_mine,
    st_all,
    st_sum,
    mid_own,
    gmid,
    gat,
    dkv,
    dks,
    dkr,
    dqf,
    gmx,
    tq,
    tqs,
    tqc,
    tqx,
    tp,
    tps,
    tpc,
    tpx,
    t1,
    t1s,
    t1c,
    t1x,
    t2,
    t2s,
    t2c,
    t2o,
    t2d,
    t2r,
    t2x,
    sm,
    sma,
    cs_acc,
    ssem,
    rsem,
):
    width = 128
    full = parts * width
    half = parts // 2
    rows_pad = tg.shape[1]
    tile = rows_pad // 4
    mid_row = rows_pad // 2
    three = heads * 3 * HD
    qpad = qz.shape[1]
    f32, bf = jnp.float32, jnp.bfloat16
    MESH = pl.DeviceIdType.MESH
    i = lax.axis_index("gx")
    me = lax.axis_index("gy")
    core = i % 2
    plane = i // 2
    sib = plane * 2 + (1 - core)
    opp = (1 - plane) * 2 + core
    dia = (1 - plane) * 2 + (1 - core)
    odd = me % 2
    place = (1 - odd) * (me // 2) + odd * (parts - 1 - me // 2)

    def index_of(spot):
        spot = (spot + 2 * parts) % parts
        back = spot // half
        return (1 - back) * (2 * spot) + back * (2 * (parts - 1 - spot) + 1)

    right, left = index_of(place + 1), index_of(place - 1)
    used = [0]
    started = []

    def take(number):
        first = used[0]
        used[0] += number
        assert used[0] <= sems
        return first

    def remote(src, dst, send, recv, **where):
        return pltpu.make_async_remote_copy(
            src_ref=src,
            dst_ref=dst,
            send_sem=ssem.at[send],
            recv_sem=rsem.at[recv],
            device_id=where,
            device_id_type=MESH,
        )

    def launch(copy):
        copy.start()
        started.append(copy)

    sent_rows = up_to(count, 16)
    chunks = 4

    def span(chunk):
        return chunk * tile, min((chunk + 1) * tile, sent_rows) - chunk * tile

    def piece(chunk):
        return pl.ds(*span(chunk))

    def first_way(chunk, way):
        return (chunk < chunks // 2) == (way == 0)

    class Ring:
        def __init__(self, buf, height=None):
            self.buf, self.height = buf, height
            self.chunks = chunks if height is None else 2
            self.base = take(2 * half * self.chunks)

        def has(self, way, step, chunk):
            return step < half - 1 or (chunk < self.chunks // 2) == (way == 0)

        def copy(self, way, step, chunk):
            owner = index_of(place - step if way == 0 else place + step)
            if self.height is None:
                ref = self.buf.at[owner, piece(chunk)]
            else:
                ref = self.buf.at[owner, pl.ds(chunk * self.height // 2, self.height // 2)]
            sem = self.base + (way * half + step) * self.chunks + chunk
            return remote(ref, ref, sem, sem, gy=right if way == 0 else left)

        def order(self):
            for chunk in range(self.chunks):
                yield 0, chunk
                yield 1, self.chunks - 1 - chunk

        def start_chunk(self, chunk):
            for way in range(2):
                if self.has(way, 0, chunk):
                    launch(self.copy(way, 0, chunk))

        def start(self):
            for way, chunk in self.order():
                if self.has(way, 0, chunk):
                    launch(self.copy(way, 0, chunk))

        def advance(self, step):
            for way, chunk in self.order():
                if self.has(way, step, chunk):
                    self.copy(way, step, chunk).wait_recv()
                    if step + 1 < half and self.has(way, step + 1, chunk):
                        launch(self.copy(way, step + 1, chunk))

        def last(self, chunk):
            for way in range(2):
                if self.has(way, half - 1, chunk):
                    self.copy(way, half - 1, chunk).wait_recv()

    class Scatter:
        def __init__(self, slot, lhs, weight_rows, join, multiply):
            self.send, self.recv = rs_send.at[slot], rs_recv.at[slot]
            self.lhs, self.weight_rows, self.join, self.multiply = lhs, weight_rows, join, multiply
            self.base = take(2 * half * chunks)
            self.scr = tscr

        def has(self, way, step, chunk):
            return 0 <= step < half and (step > 0 or first_way(chunk, way))

        def copy(self, way, step, chunk):
            sem = self.base + (way * half + step) * chunks + chunk
            return remote(
                self.send.at[way, step, piece(chunk)],
                self.recv.at[way, step, piece(chunk)],
                sem,
                sem,
                gy=right if way == 0 else left,
            )

        def weight(self, step):
            first = self.weight_rows(index_of(place + half - step))
            if 0 < step < half:
                second = self.weight_rows(index_of(place - half + step))
                return jnp.concatenate([first, second], axis=self.join)
            return first

        def term(self, step):
            weight = self.weight(step)
            wide = weight.shape[self.join]

            @pl.loop(0, 2)
            def _(number):
                at = pl.ds(pl.multiple_of(number * mid_row, mid_row), mid_row)
                self.scr[at, 0:wide] = self.multiply(self.lhs[at, :], weight)

        def send_one(self, way, step, chunk, value):
            if self.has(way, step - 1, chunk):
                self.copy(way, step - 1, chunk).wait_recv()
                value = value + self.recv[way, step - 1, piece(chunk), :].astype(f32)
            self.send[way, step, piece(chunk), :] = value.astype(bf)
            launch(self.copy(way, step, chunk))

        def open_chunk(self, chunk):
            start, size = span(chunk)
            value = self.multiply(self.lhs[start : start + size, :], self.weight(0))
            self.send_one(0 if first_way(chunk, 0) else 1, 0, chunk, value)

        def put(self, step):
            lanes = (0, 0 if step == 0 else width)
            for at in range(chunks):
                for way in range(2):
                    chunk = (at + chunks // 2) % chunks if way == 0 else at
                    if self.has(way, step, chunk):
                        lane = lanes[way]
                        self.send_one(
                            way, step, chunk, self.scr[piece(chunk), lane : lane + width]
                        )

        def step(self, step):
            self.term(step)
            self.put(step)

        def total(self, chunk):
            value = self.scr[piece(chunk), 0:width]
            for way in range(2):
                self.copy(way, half - 1, chunk).wait_recv()
                value = value + self.recv[way, half - 1, piece(chunk), :].astype(f32)
            return value

        def finish(self):
            pieces = [self.total(chunk) for chunk in range(chunks)]
            if sent_rows < rows_pad:
                pieces.append(jnp.zeros((rows_pad - sent_rows, width), f32))
            return jnp.concatenate(pieces, axis=0)

    class Gather:
        def __init__(self, view):
            self.view, self.base = view, take(3)

        def copy(self, which):
            shard = opp if which == 2 else i
            to = opp if which == 1 else sib
            ref = self.view(shard)
            return remote(ref, ref, self.base + which, self.base + which, gx=to)

        def start(self):
            launch(self.copy(1))
            launch(self.copy(0))

        def forward(self):
            self.copy(1).wait_recv()
            launch(self.copy(2))

        def finish(self):
            self.copy(0).wait_recv()
            self.copy(2).wait_recv()

    class RowSum:
        def __init__(self, term, from_sib, sent, from_opp, out):
            self.refs = (term, from_sib, sent, from_opp, out)
            self.base = take(2)

        def first(self):
            term, from_sib = self.refs[:2]
            return remote(term.at[1 - core], from_sib, self.base, self.base, gx=sib)

        def second(self):
            sent, from_opp = self.refs[2:4]
            return remote(sent, from_opp, self.base + 1, self.base + 1, gx=opp)

        def start(self):
            launch(self.first())

        def cross(self):
            term, from_sib, sent = self.refs[:3]
            self.first().wait_recv()
            sent[...] = (
                term[core, 1 - plane].astype(f32) + from_sib[1 - plane].astype(f32)
            ).astype(bf)
            launch(self.second())

        def finish(self):
            term, from_sib, _, from_opp, out = self.refs
            self.second().wait_recv()
            out[...] = (
                term[core, plane].astype(f32)
                + from_sib[plane].astype(f32)
                + from_opp[...].astype(f32)
            )

    ring_tok, ring_cot, ring_att, ring_grad = Ring(tg), Ring(cg), Ring(ag), Ring(hg)
    quarter = full // 4
    ring_proj = Ring(projg.at[i], quarter)
    gat_qkv = Gather(lambda shard: wqkv.at[pl.ds(pl.multiple_of(shard * quarter, quarter), quarter)])
    gat_fc1 = Gather(lambda shard: wfc1.at[pl.ds(pl.multiple_of(shard * quarter, quarter), quarter)])
    gat_proj = Gather(lambda shard: projg.at[shard])
    sum_qkv = RowSum(tq, tqs, tqc, tqx, gqkv_ref)
    sum_proj = RowSum(tp, tps, tpc, tpx, gproj_ref)
    sum_fc1 = RowSum(t1, t1s, t1c, t1x, gfc1_ref)

    class Spread:
        def __init__(self, src, view, number):
            self.src, self.view = src, view
            self.sends, self.recvs = take(parts), take(parts)

        def start(self):
            for step in range(1, parts):
                to = (me + step) % parts
                launch(
                    remote(self.src(to), self.view(me), self.sends + step, self.recvs + me, gy=to)
                )

        def wait(self, other):
            remote(self.src(other), self.view(other), self.sends, self.recvs + other, gy=other).wait_recv()

        def finish(self):
            for step in range(1, parts):
                self.wait((me + step) % parts)

    all_vecs = Spread(lambda to: vec_ref, lambda who: vecs.at[who], 0)
    all_stats = [
        Spread(lambda to, k=k: st_mine.at[k], lambda who, k=k: st_all.at[k, who], 0) for k in range(2)
    ]

    barrier = pltpu.get_barrier_semaphore()
    for step in range(1, parts):
        pl.semaphore_signal(
            barrier, inc=1, device_id={"gy": (me + step) % parts}, device_id_type=MESH
        )
    for to in (sib, opp, dia):
        pl.semaphore_signal(barrier, inc=1, device_id={"gx": to}, device_id_type=MESH)
    whole_rows = count // 16 * 16

    def take_rows(dest, src):
        dest[me, 0:whole_rows, :] = src[0:whole_rows, :]
        dest[me, whole_rows:rows_pad, :] = jnp.zeros((rows_pad - whole_rows, width), bf)
        if count > whole_rows:
            dest[me, whole_rows:count, :] = src[whole_rows:count, :]

    take_rows(tg, tok_ref)
    own_vectors = (
        gain1_ref,
        shift1_ref,
        bproj_ref,
        satt_ref,
        gain2_ref,
        shift2_ref,
        smlp_ref,
        bfc2_ref,
    )
    for at, ref in enumerate(own_vectors):
        vec_ref[at : at + 1, :] = ref[...].reshape(1, width)
    wqkv[pl.ds(pl.multiple_of(i * quarter, quarter), quarter), :] = qkv_ref[...]
    pl.semaphore_wait(barrier, parts + 2)

    ring_tok.start()
    gat_qkv.start()
    all_vecs.start()
    if sent_rows < rows_pad:
        for ref in (tg, cg, ag, hg):
            for at in range(parts):
                ref[at, sent_rows:rows_pad, :] = jnp.zeros((rows_pad - sent_rows, width), bf)
    vecs[me] = vec_ref[...]
    take_rows(cg, cot_ref)
    projg[i, me] = proj_ref[...]
    wfc1[pl.ds(pl.multiple_of(i * quarter, quarter), quarter), :] = fc1_ref[...]
    ring_tok.advance(0)
    lines = fc2_ref.shape[0] // 2
    part = lines // 2
    fc2_cross = take(2)
    crosses = [
        remote(
            fc2_ref.at[pl.ds(pl.multiple_of(block * lines + (1 - plane) * part, part), part)],
            fc2x.at[block],
            fc2_cross + block,
            fc2_cross + block,
            gx=opp,
        )
        for block in range(2)
    ]
    gat_qkv.forward()
    for cross in crosses:
        launch(cross)
    ring_tok.advance(1)
    gat_fc1.start()
    ring_tok.advance(2)
    ring_proj.start()
    gat_qkv.finish()
    ring_tok.advance(3) if half > 3 else None
    for step in range(4, half):
        ring_tok.advance(step)
    is_owner = core == (me // 2) % 2
    spread_send, spread_recv = take(4), take(parts)

    def fc2_copy(block):
        if block < 2:
            source = fc2_ref.at[pl.ds(pl.multiple_of(block * lines + plane * part, part), part)]
        else:
            source = fc2x.at[block - 2]
        target = 2 * (i if block < 2 else opp) + block % 2
        return target, source, remote(
            source, fc2h.at[plane, me], spread_send + block, spread_recv + me, gy=target
        )

    def spread_fc2():
        for cross in crosses:
            cross.wait_recv()
        for block in range(4):
            target, source, copy = fc2_copy(block)

            @pl.when(target != me)
            def _():
                copy.start()

            @pl.when(target == me)
            def _():
                fc2h[plane, me] = source[...]

    pass_sem = take(3)
    fc2_sib = remote(fc2h.at[plane], fc2h.at[plane], pass_sem, pass_sem, gx=sib)
    fc2_opp = remote(fc2h.at[plane], fc2h.at[plane], pass_sem + 1, pass_sem + 1, gx=opp)
    fc2_far = remote(fc2h.at[1 - plane], fc2h.at[1 - plane], pass_sem + 2, pass_sem + 2, gx=sib)

    def pass_fc2():
        @pl.when(is_owner)
        def _():
            for step in range(1, parts):
                other = (me + step) % parts
                ref = fc2h.at[plane, other]
                remote(ref, ref, spread_send, spread_recv + other, gy=other).wait_recv()
            fc2_opp.start()
            fc2_sib.start()

    def forward_fc2():
        @pl.when(is_owner)
        def _():
            fc2_opp.wait_recv()
            fc2_far.start()

    def finish_fc2():
        @pl.when(jnp.logical_not(is_owner))
        def _():
            fc2_sib.wait_recv()
            fc2_far.wait_recv()

        for at in range(parts):
            for piece in range(2):
                wfc2[piece * part : (piece + 1) * part, at * width : (at + 1) * width] = fc2h[piece, at]

    spread_fc2()
    ring_cot.start()
    all_vecs.finish()

    GAIN1, SHIFT1, BPROJ, SATT, GAIN2, SHIFT2, SMLP = range(7)
    FC2B = 7

    def vec_block(block, which):
        return vecs[block, which : which + 1, :]

    def row_tile(number, size=tile):
        return pl.ds(pl.multiple_of(number * size, size), size)

    def normalise(blocks, gain, shift, rows, slot, dest):
        acc = blocks[0]
        for block in blocks[1:]:
            acc = acc + block
        row_mean = jnp.sum(acc, axis=1, keepdims=True) * (1.0 / full)
        blocks = [block - row_mean for block in blocks]
        acc = blocks[0] * blocks[0]
        for block in blocks[1:]:
            acc = acc + block * block
        inv = lax.rsqrt(jnp.sum(acc, axis=1, keepdims=True) * (1.0 / full) + EPS)
        for at in range(parts):
            value = blocks[at] * inv * vec_block(at, gain) + vec_block(at, shift)
            dest[rows, at * width : (at + 1) * width] = value.astype(bf)
        stat[slot, rows, :] = row_mean
        stat[slot + 1, rows, :] = inv

    @pl.loop(0, 4)
    def _(number):
        rows = row_tile(number)
        normalise([tg[at, rows, :].astype(f32) for at in range(parts)], GAIN1, SHIFT1, rows, 0, nb)

    qv_row = qv_ref[...].reshape(1, heads * 2 * HD)
    blank = jnp.zeros((1, HD), f32)
    pieces = []
    for head in range(heads):
        at = head * 2 * HD
        pieces += [qv_row[:, at : at + HD], blank, qv_row[:, at + HD : at + 2 * HD]]
    qkv_bias = jnp.concatenate(pieces, axis=1)
    lane = lax.broadcasted_iota(jnp.int32, (1, three), 1)
    qkv_scale = jnp.where(lane % (3 * HD) < HD, HD ** (-0.5), 1.0).astype(f32)

    @pl.loop(0, 2)
    def _(number):
        rows = row_tile(number, mid_row)
        mixed = dot_nn(nb[rows, :], wqkv[...])
        mixf[rows, :] = mixed
        qkvb[rows, :] = ((mixed + qkv_bias) * qkv_scale).astype(bf)

    kv_sem = take(1)
    kv_copy = remote(qkvb, qkvo, kv_sem, kv_sem, gx=sib)
    launch(kv_copy)
    ring_proj.advance(0)
    ring_cot.advance(0)
    gat_fc1.forward()
    zero_half = jnp.zeros((qpad - rows_pad, 2 * HD), bf)
    for head in range(heads):
        at = head * 3 * HD
        query = qkvb[:, at : at + HD]
        qz[head, 0:rows_pad, :] = jnp.concatenate([query, jnp.zeros_like(query)], axis=1)
        qz[head, rows_pad:qpad, :] = zero_half
        kvc[head, 0:rows_pad, :] = qkvb[:, at + HD : at + 3 * HD]
    kv_copy.wait_recv()
    for head in range(heads):
        at = head * 3 * HD
        kvc[head, rows_pad : 2 * rows_pad, :] = qkvo[:, at + HD : at + 3 * HD]
        kvt[head] = jnp.transpose(kvc[head])
    ring_proj.advance(1)

    lo = count // 8 * 8
    qtile = 256
    qtiles = qpad // qtile

    def mask_keys(scores):
        pieces = []
        for base in (0, rows_pad):
            pieces.append(scores[base : base + lo])
            edge = scores[base + lo : base + rows_pad]
            index = lax.broadcasted_iota(jnp.int32, edge.shape, 0) + lo
            pieces.append(jnp.where(index < count, edge, -1e30))
        return jnp.concatenate(pieces, axis=0)

    def attend_tile(number):
        cols = slice(number * qtile, (number + 1) * qtile)
        for head in range(heads):
            scores = mask_keys(dot_nt(kvc[head], qz[head, cols, :]))
            top = jnp.max(scores, axis=0, keepdims=True)
            exponent = jnp.exp(scores - top)
            total = jnp.sum(exponent, axis=0, keepdims=True)
            probs = (exponent * (1.0 / total)).astype(bf)
            pt[head, :, cols] = probs
            result = dot_nn(kvt[head, HD : 2 * HD, :], probs).astype(bf)
            att[head * HD : (head + 1) * HD, cols] = result
        stop = min((number + 1) * qtile, rows_pad)
        got = jnp.transpose(att[:, cols])
        ag[me, number * qtile : stop, :] = got[0 : stop - number * qtile]

    sent_chunks = 0
    for number in range(qtiles):
        attend_tile(number)
        if number == 0:
            ring_proj.advance(2)
            gat_fc1.finish()
            for step in range(3, half):
                ring_proj.advance(step)
            gat_proj.start()
        if number == 1:
            ring_cot.advance(1)
        while sent_chunks < chunks and min(qpad, (number + 1) * qtile) >= sum(span(sent_chunks)):
            ring_att.start_chunk(sent_chunks)
            sent_chunks += 1
    pass_fc2()
    ring_att.advance(0)
    gat_proj.forward()
    ring_cot.advance(2)
    ring_att.advance(1)
    forward_fc2()
    for step in range(3, half):
        ring_cot.advance(step)

    @pl.loop(0, 4)
    def _(number):
        rows = row_tile(number)
        for at in range(parts):
            gm[rows, at * width : (at + 1) * width] = (
                cg[at, rows, :].astype(f32) * vec_block(at, SMLP)
            ).astype(bf)

    ring_att.advance(2)
    gat_proj.finish()
    for shard in range(4):
        for at in range(parts):
            wproj[shard * quarter : (shard + 1) * quarter, at * width : (at + 1) * width] = projg[shard, at]

    def weigh(which, weight):
        whole = jnp.concatenate([vec_block(at, which) for at in range(parts)], axis=1)
        high, low = split_high(jnp.broadcast_to(whole, (16, full)))
        return (dot_nn(high, weight) + dot_nn(low, weight))[0:1]

    gain_fc1 = weigh(GAIN2, wfc1[...])
    shift_fc1 = weigh(SHIFT2, wfc1[...])
    gain_qkv = weigh(GAIN1, wqkv[...])
    shift_qkv = weigh(SHIFT1, wqkv[...])
    for step in range(3, half - 1):
        ring_att.advance(step)
    finish_fc2()
    fc1_bias = bfc1_ref[...].reshape(1, hidden_width)
    cs_acc[...] = jnp.zeros_like(cs_acc)

    @pl.loop(0, 2)
    def _(number):
        rows = row_tile(number, mid_row)
        gh[rows, :] = dot_nt(gm[rows, :], wfc2[...])

    def fc1_rows(who):
        return wfc1[pl.ds(pl.multiple_of(who * width, width), width), :]

    scat_two = Scatter(0, gpb, fc1_rows, 0, dot_nt)

    def middle_tile(chunk):
        rows = slice(chunk * tile, (chunk + 1) * tile)
        whole = jnp.concatenate([ag[at, rows, :] for at in range(parts)], axis=1)
        result = dot_nn(whole, wproj[...])
        blocks = []
        for at in range(parts):
            attn = result[:, at * width : (at + 1) * width] + vec_block(at, BPROJ)
            ao[at, rows, :] = attn
            blocks.append(tg[at, rows, :].astype(f32) + vec_block(at, SATT) * attn)
        normalise(blocks, GAIN2, SHIFT2, rows, 2, nt)

    def mlp_tile(chunk):
        rows = slice(chunk * tile, (chunk + 1) * tile)
        raw = dot_nn(nt[rows, :], wfc1[...])
        act = raw + fc1_bias
        cdf = normal_cdf(act)
        hid[rows, :] = (act * cdf).astype(bf)
        slope = cdf + act * jnp.exp(-0.5 * act * act) * INV_ROOT_TAU
        grad = gh[rows, :] * slope
        cs_acc[...] += jnp.sum(grad.reshape(tile // 8, 8, hidden_width), axis=0)
        gpb[rows, :] = grad.astype(bf)
        prod[rows, 0:hidden_width] = (grad * (raw - shift_fc1)).astype(bf)

    for chunk in (0, 3, 1, 2):
        ring_att.last(chunk)
        middle_tile(chunk)
        mlp_tile(chunk)
        scat_two.open_chunk(chunk)

    def row_sums(slot, weights, grads, products):
        wide = grads.shape[1]
        high, low = split_high(jnp.broadcast_to(weights, (8, wide)))
        ones = jnp.ones((8, wide), bf)
        first = dot_nt(high, grads) + dot_nt(low, grads)
        second = dot_nt(ones, products)
        st_mine[slot, 0:1, 0:rows_pad] = first[0:1]
        st_mine[slot, 1:2, 0:rows_pad] = second[0:1]
        all_stats[slot].start()
        st_all[slot, me] = st_mine[slot]

    def total_sums(slot):
        all_stats[slot].finish()
        total = st_all[slot, 0]
        for at in range(1, parts):
            total = total + st_all[slot, at]
        st_sum[...] = jnp.zeros_like(st_sum)
        st_sum[0:2, :] = total
        turned = jnp.transpose(st_sum[...])
        return turned[0:rows_pad, 0:1] * (1.0 / full), turned[0:rows_pad, 1:2] * (1.0 / full)

    st_mine[...] = jnp.zeros_like(st_mine)
    row_sums(0, gain_fc1, gpb[...], prod[:, 0:hidden_width])
    for step in range(1, half):
        scat_two.step(step)

    def fc2_cols(who):
        return wfc2[:, pl.ds(pl.multiple_of(who * width, width), width)]

    scat_mlp = Scatter(1, hid, fc2_cols, 1, dot_nn)
    scat_mlp.step(0)

    def fc2_grad(number):
        result = dot_tn(hid[...], gm[:, number * 256 : (number + 1) * 256]).astype(bf)
        for piece in range(2):
            for side in range(2):
                t2[piece, 2 * number + side] = result[
                    piece * part : (piece + 1) * part, side * width : (side + 1) * width
                ]

    for number in range(parts // 2):
        fc2_grad(number)
    sib_sem = take(1)
    t2_pass = remote(t2, t2s, sib_sem, sib_sem, gx=sib)

    @pl.when(jnp.logical_not(is_owner))
    def _():
        t2_pass.start()

    scat_two.term(half)
    first, second = total_sums(0)
    satt_own = vecs[me, SATT : SATT + 1, :]
    gain_own = vecs[me, GAIN2 : GAIN2 + 1, :]

    def col_sum(value):
        return jnp.sum(value, axis=0, keepdims=True)

    sm[...] = jnp.zeros_like(sm)
    for chunk in range(chunks):
        start, size = span(chunk)
        rows = slice(start, start + size)
        grad_two = scat_two.total(chunk)
        attn_own = ao[me, rows, :]
        mid_value = tg[me, rows, :].astype(f32) + satt_own * attn_own
        mid_own[rows, :] = mid_value
        inv_two = stat[3, rows, :]
        normed = (mid_value - stat[2, rows, :]) * inv_two
        grad_mid = cg[me, rows, :].astype(f32) + inv_two * (
            grad_two * gain_own - first[rows] - normed * second[rows]
        )
        gmid[rows, :] = grad_mid
        grad_attn = grad_mid * satt_own
        hg[me, rows, :] = grad_attn.astype(bf)
        ring_grad.start_chunk(chunk)
        sm[5:6, :] += col_sum(grad_attn)
        sm[6:7, :] += col_sum(grad_mid * attn_own)
        sm[7:8, :] += col_sum(grad_two * normed)
        sm[8:9, :] += col_sum(grad_two)
    if sent_rows < rows_pad:
        for ref in (mid_own, gmid):
            ref[sent_rows:rows_pad, :] = jnp.zeros((rows_pad - sent_rows, width), f32)
    fc1_sum = col_sum(cs_acc[...])
    for at in range(hidden_width // width):
        sm[16 + at : 17 + at, :] = fc1_sum[:, at * width : (at + 1) * width]

    def rows_grad(dest, left_of, grads):
        for shard in range(4):
            dest[shard % 2, shard // 2] = dot_tn(left_of(shard), grads).astype(bf)

    rows_grad(t1, lambda shard: nt[:, shard * quarter : (shard + 1) * quarter], gpb[...])
    sum_fc1.start()
    ring_grad.advance(0)
    blocks_in = quarter // width
    rows_grad(
        tp,
        lambda shard: jnp.concatenate(
            [ag[shard * blocks_in + b] for b in range(blocks_in)], axis=1
        ),
        hg[me],
    )
    sum_proj.start()
    sum_fc1.cross()

    t2_recv = take(parts)
    t2_send = take(parts)

    def t2_copy(step):
        to = (me + step) % parts
        return remote(t2d.at[to], t2r.at[me], t2_send + step, t2_recv + me, gy=to)

    plane_sem = take(1)
    t2_plane = remote(t2c, t2o, plane_sem, plane_sem, gx=opp)

    @pl.when(is_owner)
    def _():
        t2_pass.wait_recv()
        for at in range(parts):
            t2c[at] = (t2[1 - plane, at].astype(f32) + t2s[1 - plane, at].astype(f32)).astype(bf)
        t2_plane.start()

    ring_grad.advance(1)
    scat_mlp.step(1)
    sum_proj.cross()
    ring_grad.advance(2)
    for step in range(3, half):
        ring_grad.advance(step)
    own_rows = pl.ds(pl.multiple_of(me * width, width), width)

    @pl.loop(0, 4)
    def _(number):
        rows = row_tile(number)
        whole = jnp.concatenate([hg[at, rows, :] for at in range(parts)], axis=1)
        gat[rows, :] = dot_nt(whole, wproj[own_rows, :]).astype(bf)

    gat[rows_pad:qpad, :] = jnp.zeros((qpad - rows_pad, 2 * HD), bf)
    gatt = jnp.transpose(gat[...])
    delta_all = gatt.astype(f32) * att[...].astype(f32)
    for head in range(heads):
        value = gat[:, head * HD : (head + 1) * HD]
        dz[head] = jnp.concatenate([jnp.zeros_like(value), value], axis=1)
    deltas = [
        jnp.sum(delta_all[head * HD : (head + 1) * HD], axis=0, keepdims=True) for head in range(heads)
    ]
    dkv[...] = jnp.zeros_like(dkv)

    def attend_back(number, side):
        cols = slice(number * qtile, (number + 1) * qtile)
        keys = slice(side * rows_pad, (side + 1) * rows_pad)
        for head in range(heads):
            probs = pt[head, keys, cols]
            query, grad = qz[head, cols, :], dz[head, cols, :]
            slope = dot_nt(kvc[head, keys, :], grad)
            scores = (probs.astype(f32) * (slope - deltas[head][:, cols])).astype(bf)
            dkv[head, keys, :] += dot_nn(probs, grad) + dot_nn(scores, query)
            part_query = dot_nn(kvt[head, 0:HD, keys], scores)
            here = slice(head * HD, (head + 1) * HD)
            if side == 1:
                dqf[here, cols] = part_query
            else:
                dqf[here, cols] += part_query

    def spread_t2():
        @pl.when(is_owner)
        def _():
            t2_plane.wait_recv()
            for at in range(parts):
                t2d[at] = (
                    t2[plane, at].astype(f32) + t2s[plane, at].astype(f32) + t2o[at].astype(f32)
                ).astype(bf)
            for step in range(1, parts):
                t2_copy(step).start()
            t2r[me] = t2d[me]

    for number in range(qtiles):
        attend_back(number, 1)
        if number == 0:
            scat_mlp.step(2)
        if number == 1:
            spread_t2()
    for head in range(heads):
        dks[head] = dkv[head, rows_pad : 2 * rows_pad, :].astype(bf)
    dk_sem = take(1)
    dk_copy = remote(dks, dkr, dk_sem, dk_sem, gx=sib)
    launch(dk_copy)
    for number in range(qtiles):
        attend_back(number, 0)
        if number == 0:
            for step in range(3, half):
                scat_mlp.step(step)

    grad_query = jnp.transpose(dqf[...])[0:rows_pad] * (HD ** (-0.5))
    sm[0:1, :] = col_sum(grad_query)
    dk_copy.wait_recv()
    pieces = []
    value_sums = []
    for head in range(heads):
        own = dkv[head, 0:rows_pad, :] + dkr[head].astype(f32)
        value_sums.append(col_sum(own))
        pieces += [grad_query[:, head * HD : (head + 1) * HD], own]
    for head in range(heads):
        sm[1 + head : 2 + head, :] = value_sums[head]
    mixed_grad = jnp.concatenate(pieces, axis=1)
    gmx[...] = mixed_grad.astype(bf)
    prod[:, 0:three] = (mixed_grad * (mixf[...] - shift_qkv)).astype(bf)

    def qkv_rows(who):
        return wqkv[pl.ds(pl.multiple_of(who * width, width), width), :]

    scat_one = Scatter(2, gmx, qkv_rows, 0, dot_nt)
    scat_one.step(0)
    row_sums(1, gain_qkv, gmx[...], prod[:, 0:three])
    rows_grad(tq, lambda shard: nb[:, shard * quarter : (shard + 1) * quarter], gmx[...])
    sum_qkv.start()
    scat_one.step(1)

    scat_mlp.term(half)
    mlp_out = scat_mlp.finish() + vecs[me, FC2B : FC2B + 1, :]
    smlp_own = vecs[me, SMLP : SMLP + 1, :]
    up = cg[me].astype(f32)
    out_ref[...] = (mid_own[...] + smlp_own * mlp_out)[0:count]
    sm[9:10, :] = col_sum(up * smlp_own)
    sm[10:11, :] = col_sum(up * mlp_out)
    sum_qkv.cross()
    for step in range(2, half):
        scat_one.step(step)
    sum_fc1.finish()
    sum_proj.finish()

    for step in range(4):
        source = (step // 2) * (parts // 2) + 2 * core + step % 2

        @pl.when(source != me)
        def _():
            remote(t2d.at[me], t2r.at[source], t2_send, t2_recv + source, gy=source).wait_recv()

    x_sem = take(1)
    t2_cross = remote(t2r.at[pl.ds(2 * opp, 2)], t2x, x_sem, x_sem, gx=opp)
    launch(t2_cross)
    scat_one.term(half)
    t2_cross.wait_recv()
    for block in range(2):
        for at, value in ((plane, t2r[2 * i + block]), (1 - plane, t2x[block])):
            rows = pl.ds(pl.multiple_of(block * lines + at * part, part), part)
            gfc2_ref[rows, :] = value.astype(f32)
    sum_qkv.finish()

    grad_one = scat_one.finish()
    first, second = total_sums(1)
    inv_one = stat[1]
    normed = (tg[me].astype(f32) - stat[0]) * inv_one
    gain_own = vecs[me, GAIN1 : GAIN1 + 1, :]
    gin_ref[...] = (gmid[...] + inv_one * (grad_one * gain_own - first - normed * second))[0:count]
    sm[3:4, :] = col_sum(grad_one * normed)
    sm[4:5, :] = col_sum(grad_one)
    sma[i] = sm[...]
    small_sem = take(3)
    copies = [
        remote(sm, sma.at[i], small_sem + n, small_sem + n, gx=to)
        for n, to in enumerate((sib, opp, dia))
    ]
    for copy in copies:
        launch(copy)
    for copy in copies:
        copy.wait_recv()
    small_ref[...] = sma[0] + sma[1] + sma[2] + sma[3]

    for copy in started:
        copy.wait_send()
    for block in range(4):
        target, _, copy = fc2_copy(block)

        @pl.when(target != me)
        def _():
            copy.wait_send()

    @pl.when(is_owner)
    def _():
        fc2_opp.wait_send()
        fc2_sib.wait_send()
        fc2_far.wait_send()
        t2_plane.wait_send()
        for step in range(1, parts):
            t2_copy(step).wait_send()

    @pl.when(jnp.logical_not(is_owner))
    def _():
        t2_pass.wait_send()


def emit_kernel(heads, hidden_width, small_ref, *refs):
    sources, results = refs[:6], refs[6:22]
    for source, result in zip(sources, results):
        result[...] = source[...]
    qv_ref, fc1_ref = results[6:8]
    width = small_ref.shape[1]
    for head in range(heads):
        row = jnp.concatenate(
            [small_ref[0:1, head * HD : (head + 1) * HD], small_ref[1 + head : 2 + head, HD : 2 * HD]],
            axis=1,
        )
        qv_ref[head * 2 * HD : (head + 1) * 2 * HD] = row.reshape(2 * HD)
    for at in range(hidden_width // width):
        fc1_ref[at * width : (at + 1) * width] = small_ref[16 + at : 17 + at, :].reshape(width)
    for at, ref in enumerate(results[8:]):
        ref[...] = small_ref[3 + at : 4 + at, :].reshape(width)


def on_device(*args):
    (
        tokens,
        cotangent,
        norm1_gain,
        norm1_shift,
        qkv_weight,
        qv_bias,
        proj_weight,
        proj_bias,
        scale_attn,
        norm2_gain,
        norm2_shift,
        fc1_weight,
        fc1_bias,
        fc2_weight,
        fc2_bias,
        scale_mlp,
    ) = args
    parts, rows_over = lax.axis_size("gy"), lax.axis_size("gx")
    count, width = tokens.shape
    heads = qkv_weight.shape[1] // (3 * HD)
    hidden_width = fc1_weight.shape[1]
    if (
        rows_over != 4
        or parts != 8
        or width != 128
        or heads != 2
        or IMGS != 1
        or hidden_width % 256
    ):
        return on_device_plain(*args)
    full = parts * width
    rows = up_to(count, 64)
    qpad = up_to(rows, 256)
    three = heads * 3 * HD
    quarter = full // 4
    lines = fc2_weight.shape[0] // 2
    half = parts // 2
    bf, f32 = jnp.bfloat16, jnp.float32
    wide = max(three, hidden_width)
    stat_wide = up_to(rows, 256)
    V = pltpu.VMEM
    scratch = [
        V((parts, rows, width), bf),
        V((parts, rows, width), bf),
        V((parts, rows, width), bf),
        V((parts, rows, width), bf),
        V((parts, 8, width), f32),
        V((full, three), bf),
        V((full, hidden_width), bf),
        V((4, parts, quarter, width), bf),
        V((full, full), bf),
        V((2, lines // 2, width), bf),
        V((2, parts, lines // 2, width), bf),
        V((lines, full), bf),
        V((rows, full), bf),
        V((rows, full), bf),
        V((rows, full), bf),
        V((4, rows, 1), f32),
        V((rows, three), f32),
        V((rows, three), bf),
        V((rows, three), bf),
        V((heads, 2 * rows, 2 * HD), bf),
        V((heads, 2 * HD, 2 * rows), bf),
        V((heads, qpad, 2 * HD), bf),
        V((heads, qpad, 2 * HD), bf),
        V((heads, 2 * rows, qpad), bf),
        V((heads * HD, qpad), bf),
        V((8, width), f32),
        V((parts, rows, width), f32),
        V((rows, hidden_width), f32),
        V((rows, hidden_width), bf),
        V((rows, hidden_width), bf),
        V((rows, wide), bf),
        V((rows, 2 * width), f32),
        V((3, 2, half, rows, width), bf),
        V((3, 2, half, rows, width), bf),
        V((2, 2, stat_wide), f32),
        V((2, parts, 2, stat_wide), f32),
        V((8, stat_wide), f32),
        V((rows, width), f32),
        V((rows, width), f32),
        V((qpad, width), bf),
        V((heads, 2 * rows, 2 * HD), f32),
        V((heads, rows, 2 * HD), bf),
        V((heads, rows, 2 * HD), bf),
        V((heads * HD, qpad), f32),
        V((rows, three), bf),
        V((2, 2, quarter, three), bf),
        V((2, quarter, three), bf),
        V((quarter, three), bf),
        V((quarter, three), bf),
        V((2, 2, quarter, width), bf),
        V((2, quarter, width), bf),
        V((quarter, width), bf),
        V((quarter, width), bf),
        V((2, 2, quarter, hidden_width), bf),
        V((2, quarter, hidden_width), bf),
        V((quarter, hidden_width), bf),
        V((quarter, hidden_width), bf),
        V((2, parts, lines // 2, width), bf),
        V((2, parts, lines // 2, width), bf),
        V((parts, lines // 2, width), bf),
        V((parts, lines // 2, width), bf),
        V((parts, lines // 2, width), bf),
        V((parts, lines // 2, width), bf),
        V((2, lines // 2, width), bf),
        V((24, width), f32),
        V((4, 24, width), f32),
        V((8, hidden_width), f32),
        pltpu.SemaphoreType.DMA((SEMS,)),
        pltpu.SemaphoreType.DMA((SEMS,)),
    ]
    vmem = pl.BlockSpec(memory_space=pltpu.VMEM)
    results = pl.pallas_call(
        functools.partial(mega_kernel, parts, count, heads, hidden_width, SEMS),
        out_shape=[
            jax.ShapeDtypeStruct((count, width), f32),
            jax.ShapeDtypeStruct((count, width), f32),
            jax.ShapeDtypeStruct((24, width), f32),
            jax.ShapeDtypeStruct((quarter, three), f32),
            jax.ShapeDtypeStruct((quarter, width), f32),
            jax.ShapeDtypeStruct((quarter, hidden_width), f32),
            jax.ShapeDtypeStruct((2 * lines, width), f32),
        ],
        in_specs=[vmem] * 16,
        out_specs=[vmem] * 7,
        scratch_shapes=scratch,
        compiler_params=pltpu.CompilerParams(
            collective_id=3, has_side_effects=True, vmem_limit_bytes=VMEM_BYTES
        ),
    )(
        tokens,
        cotangent,
        norm1_gain,
        norm1_shift,
        qkv_weight,
        qv_bias,
        proj_weight,
        proj_bias,
        scale_attn,
        norm2_gain,
        norm2_shift,
        fc1_weight,
        fc1_bias,
        fc2_weight,
        fc2_bias,
        scale_mlp,
    )
    output, grad_in, small, grad_qkv, grad_proj, grad_fc1, grad_fc2 = results
    line = jax.ShapeDtypeStruct((width,), f32)
    large = [output, grad_in, grad_qkv, grad_proj, grad_fc1, grad_fc2]
    written = pl.pallas_call(
        functools.partial(emit_kernel, heads, hidden_width),
        out_shape=[jax.ShapeDtypeStruct(array.shape, f32) for array in large]
        + [
            jax.ShapeDtypeStruct((heads * 2 * HD,), f32),
            jax.ShapeDtypeStruct((hidden_width,), f32),
        ]
        + [line] * 8,
        in_specs=[vmem] * 7,
        out_specs=[vmem] * 16,
    )(small, *large)
    output, grad_in, grad_qkv, grad_proj, grad_fc1, grad_fc2, grad_qv, grad_fc1_bias = written[:8]
    lines_out = written[8:]
    return (
        output,
        grad_in,
        lines_out[0],
        lines_out[1],
        grad_qkv,
        grad_qv,
        grad_proj,
        lines_out[2],
        lines_out[3],
        lines_out[4],
        lines_out[5],
        grad_fc1,
        grad_fc1_bias,
        grad_fc2,
        lines_out[6],
        lines_out[7],
    )


def solution(mesh):
    return jax.shard_map(
        on_device,
        mesh=mesh,
        in_specs=(
            P("gx", "gy"),
            P("gx", "gy"),
            P("gy"),
            P("gy"),
            P("gx", "gy"),
            P("gy"),
            P("gx", "gy"),
            P("gy"),
            P("gy"),
            P("gy"),
            P("gy"),
            P("gx", "gy"),
            P("gy"),
            P("gx", "gy"),
            P("gy"),
            P("gy"),
        ),
        out_specs=(
            P("gx", "gy"),
            P("gx", "gy"),
            P("gy"),
            P("gy"),
            P("gx", "gy"),
            P("gy"),
            P("gx", "gy"),
            P("gy"),
            P("gy"),
            P("gy"),
            P("gy"),
            P("gx", "gy"),
            P("gy"),
            P("gx", "gy"),
            P("gy"),
            P("gy"),
        ),
        check_vma=False,
    )
```

```python
import functools

import jax
import jax.numpy as jnp
from jax import lax
from jax.experimental import pallas as pl
from jax.experimental.pallas import tpu as pltpu
from jax.sharding import PartitionSpec as P

D = 1024
HD = 64
IMGS = 1


EPS = 1e-06
ROOT_HALF = 0.7071067811865476
INV_ROOT_TAU = 0.3989422804014327
SEMS = 400
VMEM_BYTES = 62 * 1024 * 1024


def from_partner(block, axis, bit):
    count = lax.axis_size(axis)
    route = []
    for low in range(count):
        high = low | 1 << bit
        if high != low and high < count:
            route += [(low, high), (high, low)]
    return lax.ppermute(block, axis, route)


def normal_cdf(values):
    return 0.5 * (1.0 + jax.scipy.special.erf(values * ROOT_HALF))


def gelu_exact(values):
    return values * normal_cdf(values)


def gelu_slope(values):
    return normal_cdf(values) + values * jnp.exp(-0.5 * values * values) * INV_ROOT_TAU


def norm_full(rows, gain, shift):
    row_mean = jnp.mean(rows, axis=1, keepdims=True)
    inv_std = lax.rsqrt(jnp.mean(rows * rows, axis=1, keepdims=True) - row_mean * row_mean + EPS)
    normed = (rows - row_mean) * inv_std
    return (normed, inv_std, (normed * gain + shift).astype(jnp.bfloat16))


def gather_columns(block):
    return lax.all_gather(block, "gy", axis=1, tiled=True)


def ring_kernel(parts, block_ref, out_ref, send_sem, recv_sem):
    half = parts // 2

    def index_of(place):
        back = place // half
        return (1 - back) * (2 * place) + back * (2 * (parts - 1 - place) + 1)

    me = lax.axis_index("gy")
    odd = me % 2
    place = (1 - odd) * (me // 2) + odd * (parts - 1 - me // 2)
    sides = (index_of((place + 1) % parts), index_of((place + parts - 1) % parts))
    barrier = pltpu.get_barrier_semaphore()
    for side in sides:
        pl.semaphore_signal(
            barrier, inc=1, device_id={"gy": side}, device_id_type=pl.DeviceIdType.MESH
        )
    pl.semaphore_wait(barrier, 2)
    copies = []
    for step in range(half):
        owners = (
            index_of((place + parts - step) % parts),
            index_of((place + step) % parts),
        )
        started = []
        for way in range(2):
            if way == 1 and step == half - 1:
                continue
            copy = pltpu.make_async_remote_copy(
                src_ref=block_ref if step == 0 else out_ref.at[owners[way]],
                dst_ref=out_ref.at[owners[way]],
                send_sem=send_sem.at[way, step],
                recv_sem=recv_sem.at[way, step],
                device_id={"gy": sides[way]},
                device_id_type=pl.DeviceIdType.MESH,
            )
            copy.start()
            started.append(copy)
        if step == 0:
            out_ref[me] = block_ref[...]
        for copy in started:
            copy.wait_recv()
        copies += started
    for copy in copies:
        copy.wait_send()


def ring_columns(block, call):
    parts = lax.axis_size("gy")
    count, width = block.shape
    if parts % 2 or parts < 4:
        return gather_columns(block)
    got = pl.pallas_call(
        functools.partial(ring_kernel, parts),
        out_shape=jax.ShapeDtypeStruct((parts, count, width), block.dtype),
        in_specs=[pl.BlockSpec(memory_space=pltpu.VMEM)],
        out_specs=pl.BlockSpec(memory_space=pltpu.VMEM),
        scratch_shapes=[
            pltpu.SemaphoreType.DMA((2, parts // 2)),
            pltpu.SemaphoreType.DMA((2, parts // 2)),
        ],
        compiler_params=pltpu.CompilerParams(collective_id=call, has_side_effects=True),
    )(block)
    return jnp.transpose(got, (1, 0, 2)).reshape(count, parts * width)


def spread_columns(block):
    parts = lax.axis_size("gy")
    got = lax.all_to_all(
        jnp.broadcast_to(block[None], (parts,) + block.shape), "gy", 0, 0, tiled=True
    )
    return jnp.transpose(got, (1, 0, 2)).reshape(block.shape[0], parts * block.shape[1])


def column_blocks(block):
    parts = lax.axis_size("gy")
    count, full = block.shape
    return jnp.transpose(block.reshape(count, parts, full // parts), (1, 0, 2))


def scatter_sum(blocks, axis):
    got = lax.all_to_all(blocks, axis, 0, 0, tiled=True)
    return jnp.sum(got.astype(jnp.float32), axis=0)


def own_columns(block, width):
    return lax.dynamic_slice_in_dim(block, lax.axis_index("gy") * width, width, axis=1)


def sum_rows(term):
    parts = lax.axis_size("gx")
    blocks = term.reshape(parts, term.shape[0] // parts, term.shape[1])
    return scatter_sum(blocks, "gx")


def weight_grad_rows(saved, grad_out):
    term = jnp.einsum("tk,tn->kn", saved, grad_out, preferred_element_type=jnp.float32)
    return lax.psum_scatter(
        term.astype(jnp.bfloat16), "gx", scatter_dimension=0, tiled=True
    ).astype(jnp.float32)


def weight_grad(saved, grad_out):
    term = jnp.einsum("tk,tn->kn", saved, grad_out, preferred_element_type=jnp.float32)
    return sum_rows(term.astype(jnp.bfloat16))


def lanes_of(column, width):
    count = column.shape[0]
    lines = -(-count // width)
    return jnp.pad(column, (0, lines * width - count)).reshape(lines, width)


def back_norm(grad_out, weight, normed, normed_own, inv_std, gain, gain_own):
    parts = lax.axis_size("gy")
    count, full = normed.shape
    width = full // parts
    term = jnp.einsum("tn,kn->tk", grad_out, weight, preferred_element_type=jnp.float32)
    scaled = term * gain
    first = lanes_of(jnp.sum(scaled, axis=1), width)
    second = lanes_of(jnp.sum(scaled * normed, axis=1), width)
    lines = first.shape[0]
    sums = jnp.concatenate([first, second], axis=0).astype(jnp.bfloat16)
    blocks = column_blocks(term.astype(jnp.bfloat16))
    sent = jnp.concatenate(
        [blocks, jnp.broadcast_to(sums[None], (parts,) + sums.shape)], axis=1
    )
    back = scatter_sum(sent, "gy")
    grad_normed = back[:count]
    first = back[count : count + lines].reshape(-1)[:count, None]
    second = back[count + lines :].reshape(-1)[:count, None]
    grad_rows = inv_std * (
        grad_normed * gain_own - first / full - normed_own * (second / full)
    )
    return (
        grad_rows,
        jnp.sum(grad_normed * normed_own, axis=0),
        jnp.sum(grad_normed, axis=0),
    )


def on_device_plain(
    tokens,
    cotangent,
    norm1_gain,
    norm1_shift,
    qkv_weight,
    qv_bias,
    proj_weight,
    proj_bias,
    scale_attn,
    norm2_gain,
    norm2_shift,
    fc1_weight,
    fc1_bias,
    fc2_weight,
    fc2_bias,
    scale_mlp,
):
    count = tokens.shape[0]
    half_len = count // IMGS
    heads_here = qkv_weight.shape[1] // (3 * HD)
    factor = HD ** (-0.5)
    width = tokens.shape[1]
    full_tokens = ring_columns(tokens, 0)
    vectors = spread_columns(
        jnp.stack([norm1_gain, norm1_shift, proj_bias, scale_attn, norm2_gain, norm2_shift, scale_mlp])
    )
    gain_one, shift_one, bias_proj, full_scale_attn, gain_two, shift_two, full_scale_mlp = vectors
    full_qkv = lax.all_gather(qkv_weight, "gx", axis=0, tiled=True)
    all_proj = lax.all_gather(ring_columns(proj_weight, 1), "gx", axis=0, tiled=True)
    full_fc1 = lax.all_gather(fc1_weight, "gx", axis=0, tiled=True)
    full_fc2 = lax.all_gather(fc2_weight, "gx", axis=0, tiled=True)
    rows_fc2 = lax.all_to_all(full_fc2, "gy", split_axis=0, concat_axis=1, tiled=True)
    full_cotangent = gather_columns(cotangent)
    inputs = full_tokens.astype(jnp.float32)
    normed_one, inv_one, norm_one = norm_full(inputs, gain_one, shift_one)
    mixed = jnp.dot(norm_one, full_qkv, preferred_element_type=jnp.float32)
    mixed = mixed.reshape(count, heads_here, 3, HD)
    biases = qv_bias.reshape(heads_here, 2, HD)
    queries = (mixed[:, :, 0] + biases[:, 0]).astype(jnp.bfloat16)
    keys = mixed[:, :, 1].astype(jnp.bfloat16)
    values = (mixed[:, :, 2] + biases[:, 1]).astype(jnp.bfloat16)
    lower = lax.axis_index("gx") % 2 == 0
    pair_kv = jnp.concatenate([keys, values], axis=2).reshape(count, heads_here * 2 * HD)
    other_kv = from_partner(pair_kv, "gx", 0)
    first_kv = jnp.where(lower, pair_kv, other_kv)
    second_kv = jnp.where(lower, other_kv, pair_kv)
    image_shape = (IMGS, half_len, heads_here, 2 * HD)
    both_kv = jnp.concatenate(
        [first_kv.reshape(image_shape), second_kv.reshape(image_shape)], axis=1
    )
    key_all = both_kv[..., :HD]
    value_all = both_kv[..., HD:]
    query_img = queries.reshape(IMGS, half_len, heads_here, HD)
    scores = (
        jnp.einsum("iqhe,ikhe->ihqk", query_img, key_all, preferred_element_type=jnp.float32)
        * factor
    )
    row_max = jnp.max(scores, axis=3, keepdims=True)
    exponent = jnp.exp(scores - row_max)
    totals = jnp.sum(exponent, axis=3, keepdims=True)
    log_total = row_max + jnp.log(totals)
    probs = (exponent / totals).astype(jnp.bfloat16)
    attended_img = jnp.einsum(
        "ihqk,ikhe->iqhe", probs, value_all, preferred_element_type=jnp.float32
    ).astype(jnp.bfloat16)
    attended = attended_img.reshape(count, heads_here * HD)
    full_attended = ring_columns(attended, 0)
    attn_out = jnp.dot(full_attended, all_proj, preferred_element_type=jnp.float32) + bias_proj
    middle = inputs + full_scale_attn * attn_out
    normed_two, inv_two, norm_two = norm_full(middle, gain_two, shift_two)
    pre_act = jnp.dot(norm_two, full_fc1, preferred_element_type=jnp.float32) + fc1_bias
    hidden = gelu_exact(pre_act).astype(jnp.bfloat16)
    upstream = cotangent.astype(jnp.float32)
    grad_mlp = upstream * scale_mlp
    grad_fc2_bias = jnp.sum(grad_mlp, axis=0)
    full_grad_mlp_b = (full_cotangent.astype(jnp.float32) * full_scale_mlp).astype(jnp.bfloat16)
    grad_hidden = jnp.einsum(
        "tn,kn->tk", full_grad_mlp_b, rows_fc2, preferred_element_type=jnp.float32
    )
    grad_pre = grad_hidden * gelu_slope(pre_act)
    grad_fc1_bias = jnp.sum(grad_pre, axis=0)
    grad_pre_b = grad_pre.astype(jnp.bfloat16)
    own_two = own_columns(normed_two, width)
    grad_rows, grad_gain_two, grad_shift_two = back_norm(
        grad_pre_b, full_fc1, normed_two, own_two, inv_two, gain_two, norm2_gain
    )
    grad_middle = upstream + grad_rows
    grad_scale_attn = jnp.sum(grad_middle * own_columns(attn_out, width), axis=0)
    grad_attn = grad_middle * scale_attn
    grad_proj_bias = jnp.sum(grad_attn, axis=0)
    grad_attn_b = grad_attn.astype(jnp.bfloat16)
    full_grad_attn_b = ring_columns(grad_attn_b, 0)
    own_rows_proj = lax.dynamic_slice_in_dim(
        all_proj, lax.axis_index("gy") * width, width, axis=0
    )
    grad_attended = jnp.einsum(
        "tn,kn->tk", full_grad_attn_b, own_rows_proj, preferred_element_type=jnp.float32
    ).astype(jnp.bfloat16)
    mlp_term = jnp.dot(hidden, rows_fc2, preferred_element_type=jnp.float32)
    mlp_out = (
        lax.psum_scatter(
            column_blocks(mlp_term.astype(jnp.bfloat16)), "gy", scatter_dimension=0, tiled=False
        ).astype(jnp.float32)
        + fc2_bias
    )
    output = own_columns(middle, width) + scale_mlp * mlp_out
    grad_scale_mlp = jnp.sum(upstream * mlp_out, axis=0)
    fc2_term = jnp.einsum(
        "tk,tn->kn", hidden, full_grad_mlp_b, preferred_element_type=jnp.float32
    )
    fc2_blocks = lax.all_to_all(column_blocks(fc2_term.astype(jnp.bfloat16)), "gy", 0, 0, tiled=True)
    grad_fc2 = sum_rows(fc2_blocks.reshape(-1, width))
    grad_fc1 = weight_grad_rows(norm_two, grad_pre_b)
    grad_proj = weight_grad_rows(full_attended, grad_attn_b)
    grad_att_img = grad_attended.reshape(IMGS, half_len, heads_here, HD)
    recomputed = jnp.exp(scores - log_total)
    probs_b = recomputed.astype(jnp.bfloat16)
    grad_value_all = jnp.einsum(
        "ihqk,iqhe->ikhe", probs_b, grad_att_img, preferred_element_type=jnp.float32
    )
    grad_probs = jnp.einsum(
        "iqhe,ikhe->ihqk", grad_att_img, value_all, preferred_element_type=jnp.float32
    )
    delta = jnp.sum(grad_att_img.astype(jnp.float32) * attended_img.astype(jnp.float32), axis=3)
    grad_scores = recomputed * (grad_probs - jnp.transpose(delta, (0, 2, 1))[..., None])
    grad_scores_b = grad_scores.astype(jnp.bfloat16)
    grad_query = (
        jnp.einsum("ihqk,ikhe->iqhe", grad_scores_b, key_all, preferred_element_type=jnp.float32)
        * factor
    )
    grad_key_all = (
        jnp.einsum("ihqk,iqhe->ikhe", grad_scores_b, query_img, preferred_element_type=jnp.float32)
        * factor
    )
    grad_kv_all = jnp.concatenate([grad_key_all, grad_value_all], axis=3)
    first_part = grad_kv_all[:, :half_len].reshape(count, heads_here * 2 * HD)
    second_part = grad_kv_all[:, half_len:].reshape(count, heads_here * 2 * HD)
    own_part = jnp.where(lower, first_part, second_part)
    sent_part = jnp.where(lower, second_part, first_part)
    grad_kv = own_part + from_partner(sent_part.astype(jnp.bfloat16), "gx", 0).astype(
        sent_part.dtype
    )
    grad_kv = grad_kv.reshape(count, heads_here, 2, HD)
    grad_query = grad_query.reshape(count, heads_here, HD)
    grad_qv_bias = jnp.stack(
        [jnp.sum(grad_query, axis=0), jnp.sum(grad_kv[:, :, 1], axis=0)], axis=1
    ).reshape(heads_here * 2 * HD)
    grad_mixed = (
        jnp.stack([grad_query, grad_kv[:, :, 0], grad_kv[:, :, 1]], axis=2)
        .astype(jnp.bfloat16)
        .reshape(count, heads_here * 3 * HD)
    )
    grad_qkv = weight_grad(norm_one, grad_mixed)
    own_one = own_columns(normed_one, width)
    grad_rows, grad_gain_one, grad_shift_one = back_norm(
        grad_mixed, full_qkv, normed_one, own_one, inv_one, gain_one, norm1_gain
    )
    grad_input = grad_middle + grad_rows
    smalls = lax.psum(
        (
            grad_gain_one,
            grad_shift_one,
            grad_qv_bias,
            grad_proj_bias,
            grad_scale_attn,
            grad_gain_two,
            grad_shift_two,
            grad_fc1_bias,
            grad_fc2_bias,
            grad_scale_mlp,
        ),
        "gx",
    )
    return (
        output,
        grad_input,
        smalls[0],
        smalls[1],
        grad_qkv,
        smalls[2],
        grad_proj,
        smalls[3],
        smalls[4],
        smalls[5],
        smalls[6],
        grad_fc1,
        smalls[7],
        grad_fc2,
        smalls[8],
        smalls[9],
    )


def up_to(value, step):
    return -(-value // step) * step


def dot_nn(a, b):
    return lax.dot_general(a, b, (((1,), (0,)), ((), ())), preferred_element_type=jnp.float32)


def dot_nt(a, b):
    return lax.dot_general(a, b, (((1,), (1,)), ((), ())), preferred_element_type=jnp.float32)


def dot_tn(a, b):
    return lax.dot_general(a, b, (((0,), (0,)), ((), ())), preferred_element_type=jnp.float32)


def split_high(values):
    high = values.astype(jnp.bfloat16)
    return high, (values - high.astype(jnp.float32)).astype(jnp.bfloat16)


def mega_kernel(
    parts,
    count,
    heads,
    hidden_width,
    sems,
    tok_ref,
    cot_ref,
    gain1_ref,
    shift1_ref,
    qkv_ref,
    qv_ref,
    proj_ref,
    bproj_ref,
    satt_ref,
    gain2_ref,
    shift2_ref,
    fc1_ref,
    bfc1_ref,
    fc2_ref,
    bfc2_ref,
    smlp_ref,
    out_ref,
    gin_ref,
    small_ref,
    gqkv_ref,
    gproj_ref,
    gfc1_ref,
    gfc2_ref,
    tg,
    cg,
    ag,
    hg,
    vecs,
    wqkv,
    wfc1,
    projg,
    wproj,
    fc2x,
    fc2h,
    wfc2,
    nb,
    nt,
    gm,
    stat,
    mixf,
    qkvb,
    qkvo,
    kvc,
    kvt,
    qz,
    dz,
    pt,
    att,
    vec_ref,
    ao,
    gh,
    hid,
    gpb,
    prod,
    tscr,
    rs_send,
    rs_recv,
    st_mine,
    st_all,
    st_sum,
    mid_own,
    gmid,
    gat,
    dkv,
    dks,
    dkr,
    dqf,
    gmx,
    tq,
    tqs,
    tqc,
    tqx,
    tp,
    tps,
    tpc,
    tpx,
    t1,
    t1s,
    t1c,
    t1x,
    t2,
    t2s,
    t2c,
    t2o,
    t2d,
    t2r,
    t2x,
    sm,
    sma,
    cs_acc,
    ssem,
    rsem,
):
    width = 128
    full = parts * width
    half = parts // 2
    rows_pad = tg.shape[1]
    tile = rows_pad // 4
    mid_row = rows_pad // 2
    three = heads * 3 * HD
    qpad = qz.shape[1]
    f32, bf = jnp.float32, jnp.bfloat16
    MESH = pl.DeviceIdType.MESH
    i = lax.axis_index("gx")
    me = lax.axis_index("gy")
    core = i % 2
    plane = i // 2
    sib = plane * 2 + (1 - core)
    opp = (1 - plane) * 2 + core
    dia = (1 - plane) * 2 + (1 - core)
    odd = me % 2
    place = (1 - odd) * (me // 2) + odd * (parts - 1 - me // 2)

    def index_of(spot):
        spot = (spot + 2 * parts) % parts
        back = spot // half
        return (1 - back) * (2 * spot) + back * (2 * (parts - 1 - spot) + 1)

    right, left = index_of(place + 1), index_of(place - 1)
    used = [0]
    started = []

    def take(number):
        first = used[0]
        used[0] += number
        assert used[0] <= sems
        return first

    def remote(src, dst, send, recv, **where):
        return pltpu.make_async_remote_copy(
            src_ref=src,
            dst_ref=dst,
            send_sem=ssem.at[send],
            recv_sem=rsem.at[recv],
            device_id=where,
            device_id_type=MESH,
        )

    def launch(copy):
        copy.start()
        started.append(copy)

    sent_rows = up_to(count, 16)
    chunks = 4

    def span(chunk):
        return chunk * tile, min((chunk + 1) * tile, sent_rows) - chunk * tile

    def piece(chunk):
        return pl.ds(*span(chunk))

    def first_way(chunk, way):
        return (chunk < chunks // 2) == (way == 0)

    class Ring:
        def __init__(self, buf, height=None):
            self.buf, self.height = buf, height
            self.chunks = chunks if height is None else 2
            self.base = take(2 * half * self.chunks)

        def has(self, way, step, chunk):
            return step < half - 1 or (chunk < self.chunks // 2) == (way == 0)

        def copy(self, way, step, chunk):
            owner = index_of(place - step if way == 0 else place + step)
            if self.height is None:
                ref = self.buf.at[owner, piece(chunk)]
            else:
                ref = self.buf.at[owner, pl.ds(chunk * self.height // 2, self.height // 2)]
            sem = self.base + (way * half + step) * self.chunks + chunk
            return remote(ref, ref, sem, sem, gy=right if way == 0 else left)

        def order(self):
            for chunk in range(self.chunks):
                yield 0, chunk
                yield 1, self.chunks - 1 - chunk

        def start_chunk(self, chunk):
            for way in range(2):
                if self.has(way, 0, chunk):
                    launch(self.copy(way, 0, chunk))

        def start(self):
            for way, chunk in self.order():
                if self.has(way, 0, chunk):
                    launch(self.copy(way, 0, chunk))

        def advance(self, step):
            for way, chunk in self.order():
                if self.has(way, step, chunk):
                    self.copy(way, step, chunk).wait_recv()
                    if step + 1 < half and self.has(way, step + 1, chunk):
                        launch(self.copy(way, step + 1, chunk))

        def last(self, chunk):
            for way in range(2):
                if self.has(way, half - 1, chunk):
                    self.copy(way, half - 1, chunk).wait_recv()

    class Scatter:
        def __init__(self, slot, lhs, weight_rows, join, multiply):
            self.send, self.recv = rs_send.at[slot], rs_recv.at[slot]
            self.lhs, self.weight_rows, self.join, self.multiply = lhs, weight_rows, join, multiply
            self.base = take(2 * half * chunks)
            self.scr = tscr

        def has(self, way, step, chunk):
            return 0 <= step < half and (step > 0 or first_way(chunk, way))

        def copy(self, way, step, chunk):
            sem = self.base + (way * half + step) * chunks + chunk
            return remote(
                self.send.at[way, step, piece(chunk)],
                self.recv.at[way, step, piece(chunk)],
                sem,
                sem,
                gy=right if way == 0 else left,
            )

        def weight(self, step):
            first = self.weight_rows(index_of(place + half - step))
            if 0 < step < half:
                second = self.weight_rows(index_of(place - half + step))
                return jnp.concatenate([first, second], axis=self.join)
            return first

        def term(self, step):
            weight = self.weight(step)
            wide = weight.shape[self.join]

            @pl.loop(0, 2)
            def _(number):
                at = pl.ds(pl.multiple_of(number * mid_row, mid_row), mid_row)
                self.scr[at, 0:wide] = self.multiply(self.lhs[at, :], weight)

        def send_one(self, way, step, chunk, value):
            if self.has(way, step - 1, chunk):
                self.copy(way, step - 1, chunk).wait_recv()
                value = value + self.recv[way, step - 1, piece(chunk), :].astype(f32)
            self.send[way, step, piece(chunk), :] = value.astype(bf)
            launch(self.copy(way, step, chunk))

        def open_chunk(self, chunk):
            start, size = span(chunk)
            value = self.multiply(self.lhs[start : start + size, :], self.weight(0))
            self.send_one(0 if first_way(chunk, 0) else 1, 0, chunk, value)

        def put(self, step):
            lanes = (0, 0 if step == 0 else width)
            for at in range(chunks):
                for way in range(2):
                    chunk = (at + chunks // 2) % chunks if way == 0 else at
                    if self.has(way, step, chunk):
                        lane = lanes[way]
                        self.send_one(
                            way, step, chunk, self.scr[piece(chunk), lane : lane + width]
                        )

        def step(self, step):
            self.term(step)
            self.put(step)

        def total(self, chunk):
            value = self.scr[piece(chunk), 0:width]
            for way in range(2):
                self.copy(way, half - 1, chunk).wait_recv()
                value = value + self.recv[way, half - 1, piece(chunk), :].astype(f32)
            return value

        def finish(self):
            pieces = [self.total(chunk) for chunk in range(chunks)]
            if sent_rows < rows_pad:
                pieces.append(jnp.zeros((rows_pad - sent_rows, width), f32))
            return jnp.concatenate(pieces, axis=0)

    class Gather:
        def __init__(self, view):
            self.view, self.base = view, take(3)

        def copy(self, which):
            shard = opp if which == 2 else i
            to = opp if which == 1 else sib
            ref = self.view(shard)
            return remote(ref, ref, self.base + which, self.base + which, gx=to)

        def start(self):
            launch(self.copy(1))
            launch(self.copy(0))

        def forward(self):
            self.copy(1).wait_recv()
            launch(self.copy(2))

        def finish(self):
            self.copy(0).wait_recv()
            self.copy(2).wait_recv()

    class RowSum:
        def __init__(self, term, from_sib, sent, from_opp, out):
            self.refs = (term, from_sib, sent, from_opp, out)
            self.base = take(2)

        def first(self):
            term, from_sib = self.refs[:2]
            return remote(term.at[1 - core], from_sib, self.base, self.base, gx=sib)

        def second(self):
            sent, from_opp = self.refs[2:4]
            return remote(sent, from_opp, self.base + 1, self.base + 1, gx=opp)

        def start(self):
            launch(self.first())

        def cross(self):
            term, from_sib, sent = self.refs[:3]
            self.first().wait_recv()
            sent[...] = (
                term[core, 1 - plane].astype(f32) + from_sib[1 - plane].astype(f32)
            ).astype(bf)
            launch(self.second())

        def finish(self):
            term, from_sib, _, from_opp, out = self.refs
            self.second().wait_recv()
            out[...] = (
                term[core, plane].astype(f32)
                + from_sib[plane].astype(f32)
                + from_opp[...].astype(f32)
            )

    ring_tok, ring_cot, ring_att, ring_grad = Ring(tg), Ring(cg), Ring(ag), Ring(hg)
    quarter = full // 4
    ring_proj = Ring(projg.at[i], quarter)
    gat_qkv = Gather(lambda shard: wqkv.at[pl.ds(pl.multiple_of(shard * quarter, quarter), quarter)])
    gat_fc1 = Gather(lambda shard: wfc1.at[pl.ds(pl.multiple_of(shard * quarter, quarter), quarter)])
    gat_proj = Gather(lambda shard: projg.at[shard])
    sum_qkv = RowSum(tq, tqs, tqc, tqx, gqkv_ref)
    sum_proj = RowSum(tp, tps, tpc, tpx, gproj_ref)
    sum_fc1 = RowSum(t1, t1s, t1c, t1x, gfc1_ref)

    class Spread:
        def __init__(self, src, view, number):
            self.src, self.view = src, view
            self.sends, self.recvs = take(parts), take(parts)

        def start(self):
            for step in range(1, parts):
                to = (me + step) % parts
                launch(
                    remote(self.src(to), self.view(me), self.sends + step, self.recvs + me, gy=to)
                )

        def wait(self, other):
            remote(self.src(other), self.view(other), self.sends, self.recvs + other, gy=other).wait_recv()

        def finish(self):
            for step in range(1, parts):
                self.wait((me + step) % parts)

    all_vecs = Spread(lambda to: vec_ref, lambda who: vecs.at[who], 0)
    all_stats = [
        Spread(lambda to, k=k: st_mine.at[k], lambda who, k=k: st_all.at[k, who], 0) for k in range(2)
    ]

    barrier = pltpu.get_barrier_semaphore()
    for step in range(1, parts):
        pl.semaphore_signal(
            barrier, inc=1, device_id={"gy": (me + step) % parts}, device_id_type=MESH
        )
    for to in (sib, opp, dia):
        pl.semaphore_signal(barrier, inc=1, device_id={"gx": to}, device_id_type=MESH)
    whole_rows = count // 16 * 16

    def take_rows(dest, src):
        dest[me, 0:whole_rows, :] = src[0:whole_rows, :]
        dest[me, whole_rows:rows_pad, :] = jnp.zeros((rows_pad - whole_rows, width), bf)
        if count > whole_rows:
            dest[me, whole_rows:count, :] = src[whole_rows:count, :]

    take_rows(tg, tok_ref)
    own_vectors = (
        gain1_ref,
        shift1_ref,
        bproj_ref,
        satt_ref,
        gain2_ref,
        shift2_ref,
        smlp_ref,
        bfc2_ref,
    )
    for at, ref in enumerate(own_vectors):
        vec_ref[at : at + 1, :] = ref[...].reshape(1, width)
    wqkv[pl.ds(pl.multiple_of(i * quarter, quarter), quarter), :] = qkv_ref[...]
    pl.semaphore_wait(barrier, parts + 2)

    ring_tok.start()
    gat_qkv.start()
    all_vecs.start()
    if sent_rows < rows_pad:
        for ref in (tg, cg, ag, hg):
            for at in range(parts):
                ref[at, sent_rows:rows_pad, :] = jnp.zeros((rows_pad - sent_rows, width), bf)
    vecs[me] = vec_ref[...]
    take_rows(cg, cot_ref)
    projg[i, me] = proj_ref[...]
    wfc1[pl.ds(pl.multiple_of(i * quarter, quarter), quarter), :] = fc1_ref[...]
    ring_tok.advance(0)
    lines = fc2_ref.shape[0] // 2
    part = lines // 2
    fc2_cross = take(2)
    crosses = [
        remote(
            fc2_ref.at[pl.ds(pl.multiple_of(block * lines + (1 - plane) * part, part), part)],
            fc2x.at[block],
            fc2_cross + block,
            fc2_cross + block,
            gx=opp,
        )
        for block in range(2)
    ]
    gat_qkv.forward()
    for cross in crosses:
        launch(cross)
    ring_tok.advance(1)
    gat_fc1.start()
    ring_tok.advance(2)
    ring_proj.start()
    gat_qkv.finish()
    ring_tok.advance(3) if half > 3 else None
    for step in range(4, half):
        ring_tok.advance(step)
    is_owner = core == (me // 2) % 2
    spread_send, spread_recv = take(4), take(parts)

    def fc2_copy(block):
        if block < 2:
            source = fc2_ref.at[pl.ds(pl.multiple_of(block * lines + plane * part, part), part)]
        else:
            source = fc2x.at[block - 2]
        target = 2 * (i if block < 2 else opp) + block % 2
        return target, source, remote(
            source, fc2h.at[plane, me], spread_send + block, spread_recv + me, gy=target
        )

    def spread_fc2():
        for cross in crosses:
            cross.wait_recv()
        for block in range(4):
            target, source, copy = fc2_copy(block)

            @pl.when(target != me)
            def _():
                copy.start()

            @pl.when(target == me)
            def _():
                fc2h[plane, me] = source[...]

    pass_sem = take(3)
    fc2_sib = remote(fc2h.at[plane], fc2h.at[plane], pass_sem, pass_sem, gx=sib)
    fc2_opp = remote(fc2h.at[plane], fc2h.at[plane], pass_sem + 1, pass_sem + 1, gx=opp)
    fc2_far = remote(fc2h.at[1 - plane], fc2h.at[1 - plane], pass_sem + 2, pass_sem + 2, gx=sib)

    def pass_fc2():
        @pl.when(is_owner)
        def _():
            for step in range(1, parts):
                other = (me + step) % parts
                ref = fc2h.at[plane, other]
                remote(ref, ref, spread_send, spread_recv + other, gy=other).wait_recv()
            fc2_opp.start()
            fc2_sib.start()

    def forward_fc2():
        @pl.when(is_owner)
        def _():
            fc2_opp.wait_recv()
            fc2_far.start()

    def finish_fc2():
        @pl.when(jnp.logical_not(is_owner))
        def _():
            fc2_sib.wait_recv()
            fc2_far.wait_recv()

        for at in range(parts):
            for piece in range(2):
                wfc2[piece * part : (piece + 1) * part, at * width : (at + 1) * width] = fc2h[piece, at]

    ring_cot.start()
    all_vecs.finish()

    GAIN1, SHIFT1, BPROJ, SATT, GAIN2, SHIFT2, SMLP = range(7)
    FC2B = 7

    def vec_block(block, which):
        return vecs[block, which : which + 1, :]

    def row_tile(number, size=tile):
        return pl.ds(pl.multiple_of(number * size, size), size)

    def normalise(blocks, gain, shift, rows, slot, dest):
        acc = blocks[0]
        for block in blocks[1:]:
            acc = acc + block
        row_mean = jnp.sum(acc, axis=1, keepdims=True) * (1.0 / full)
        blocks = [block - row_mean for block in blocks]
        acc = blocks[0] * blocks[0]
        for block in blocks[1:]:
            acc = acc + block * block
        inv = lax.rsqrt(jnp.sum(acc, axis=1, keepdims=True) * (1.0 / full) + EPS)
        for at in range(parts):
            value = blocks[at] * inv * vec_block(at, gain) + vec_block(at, shift)
            dest[rows, at * width : (at + 1) * width] = value.astype(bf)
        stat[slot, rows, :] = row_mean
        stat[slot + 1, rows, :] = inv

    @pl.loop(0, 4)
    def _(number):
        rows = row_tile(number)
        normalise([tg[at, rows, :].astype(f32) for at in range(parts)], GAIN1, SHIFT1, rows, 0, nb)

    qv_row = qv_ref[...].reshape(1, heads * 2 * HD)
    blank = jnp.zeros((1, HD), f32)
    pieces = []
    for head in range(heads):
        at = head * 2 * HD
        pieces += [qv_row[:, at : at + HD], blank, qv_row[:, at + HD : at + 2 * HD]]
    qkv_bias = jnp.concatenate(pieces, axis=1)
    lane = lax.broadcasted_iota(jnp.int32, (1, three), 1)
    qkv_scale = jnp.where(lane % (3 * HD) < HD, HD ** (-0.5), 1.0).astype(f32)

    @pl.loop(0, 2)
    def _(number):
        rows = row_tile(number, mid_row)
        mixed = dot_nn(nb[rows, :], wqkv[...])
        mixf[rows, :] = mixed
        qkvb[rows, :] = ((mixed + qkv_bias) * qkv_scale).astype(bf)

    kv_sem = take(1)
    kv_copy = remote(qkvb, qkvo, kv_sem, kv_sem, gx=sib)
    launch(kv_copy)
    ring_proj.advance(0)
    ring_proj.advance(1)
    ring_cot.advance(0)
    gat_fc1.forward()
    zero_half = jnp.zeros((qpad - rows_pad, 2 * HD), bf)
    for head in range(heads):
        at = head * 3 * HD
        query = qkvb[:, at : at + HD]
        qz[head, 0:rows_pad, :] = jnp.concatenate([query, jnp.zeros_like(query)], axis=1)
        qz[head, rows_pad:qpad, :] = zero_half
        kvc[head, 0:rows_pad, :] = qkvb[:, at + HD : at + 3 * HD]
    kv_copy.wait_recv()
    for head in range(heads):
        at = head * 3 * HD
        kvc[head, rows_pad : 2 * rows_pad, :] = qkvo[:, at + HD : at + 3 * HD]
        kvt[head] = jnp.transpose(kvc[head])
    ring_proj.advance(2)

    lo = count // 8 * 8
    qtile = 256
    qtiles = qpad // qtile

    def mask_keys(scores):
        pieces = []
        for base in (0, rows_pad):
            pieces.append(scores[base : base + lo])
            edge = scores[base + lo : base + rows_pad]
            index = lax.broadcasted_iota(jnp.int32, edge.shape, 0) + lo
            pieces.append(jnp.where(index < count, edge, -1e30))
        return jnp.concatenate(pieces, axis=0)

    def attend_tile(number):
        cols = slice(number * qtile, (number + 1) * qtile)
        for head in range(heads):
            scores = mask_keys(dot_nt(kvc[head], qz[head, cols, :]))
            top = jnp.max(scores, axis=0, keepdims=True)
            exponent = jnp.exp(scores - top)
            total = jnp.sum(exponent, axis=0, keepdims=True)
            probs = (exponent * (1.0 / total)).astype(bf)
            pt[head, :, cols] = probs
            result = dot_nn(kvt[head, HD : 2 * HD, :], probs).astype(bf)
            att[head * HD : (head + 1) * HD, cols] = result
        stop = min((number + 1) * qtile, rows_pad)
        got = jnp.transpose(att[:, cols])
        ag[me, number * qtile : stop, :] = got[0 : stop - number * qtile]

    sent_chunks = 0
    for number in range(qtiles):
        attend_tile(number)
        if number == 0:
            spread_fc2()
            gat_fc1.finish()
            for step in range(3, half):
                ring_proj.advance(step)
            gat_proj.start()
        if number == 1:
            ring_cot.advance(1)
        while sent_chunks < chunks and min(qpad, (number + 1) * qtile) >= sum(span(sent_chunks)):
            ring_att.start_chunk(sent_chunks)
            sent_chunks += 1
    pass_fc2()
    ring_att.advance(0)
    gat_proj.forward()
    ring_cot.advance(2)
    ring_att.advance(1)
    forward_fc2()
    for step in range(3, half):
        ring_cot.advance(step)

    @pl.loop(0, 4)
    def _(number):
        rows = row_tile(number)
        for at in range(parts):
            gm[rows, at * width : (at + 1) * width] = (
                cg[at, rows, :].astype(f32) * vec_block(at, SMLP)
            ).astype(bf)

    ring_att.advance(2)
    gat_proj.finish()
    for shard in range(4):
        for at in range(parts):
            wproj[shard * quarter : (shard + 1) * quarter, at * width : (at + 1) * width] = projg[shard, at]

    def weigh(which, weight):
        whole = jnp.concatenate([vec_block(at, which) for at in range(parts)], axis=1)
        high, low = split_high(jnp.broadcast_to(whole, (16, full)))
        return (dot_nn(high, weight) + dot_nn(low, weight))[0:1]

    gain_fc1 = weigh(GAIN2, wfc1[...])
    shift_fc1 = weigh(SHIFT2, wfc1[...])
    gain_qkv = weigh(GAIN1, wqkv[...])
    shift_qkv = weigh(SHIFT1, wqkv[...])
    for step in range(3, half - 1):
        ring_att.advance(step)
    finish_fc2()
    fc1_bias = bfc1_ref[...].reshape(1, hidden_width)
    cs_acc[...] = jnp.zeros_like(cs_acc)

    @pl.loop(0, 2)
    def _(number):
        rows = row_tile(number, mid_row)
        gh[rows, :] = dot_nt(gm[rows, :], wfc2[...])

    def fc1_rows(who):
        return wfc1[pl.ds(pl.multiple_of(who * width, width), width), :]

    scat_two = Scatter(0, gpb, fc1_rows, 0, dot_nt)

    def middle_tile(chunk):
        rows = slice(chunk * tile, (chunk + 1) * tile)
        whole = jnp.concatenate([ag[at, rows, :] for at in range(parts)], axis=1)
        result = dot_nn(whole, wproj[...])
        blocks = []
        for at in range(parts):
            attn = result[:, at * width : (at + 1) * width] + vec_block(at, BPROJ)
            ao[at, rows, :] = attn
            blocks.append(tg[at, rows, :].astype(f32) + vec_block(at, SATT) * attn)
        normalise(blocks, GAIN2, SHIFT2, rows, 2, nt)

    def mlp_tile(chunk):
        rows = slice(chunk * tile, (chunk + 1) * tile)
        raw = dot_nn(nt[rows, :], wfc1[...])
        act = raw + fc1_bias
        cdf = normal_cdf(act)
        hid[rows, :] = (act * cdf).astype(bf)
        slope = cdf + act * jnp.exp(-0.5 * act * act) * INV_ROOT_TAU
        grad = gh[rows, :] * slope
        cs_acc[...] += jnp.sum(grad.reshape(tile // 8, 8, hidden_width), axis=0)
        gpb[rows, :] = grad.astype(bf)
        prod[rows, 0:hidden_width] = (grad * (raw - shift_fc1)).astype(bf)

    for chunk in (0, 3, 1, 2):
        ring_att.last(chunk)
        middle_tile(chunk)
        mlp_tile(chunk)
        scat_two.open_chunk(chunk)

    def row_sums(slot, weights, grads, products):
        wide = grads.shape[1]
        high, low = split_high(jnp.broadcast_to(weights, (8, wide)))
        ones = jnp.ones((8, wide), bf)
        first = dot_nt(high, grads) + dot_nt(low, grads)
        second = dot_nt(ones, products)
        st_mine[slot, 0:1, 0:rows_pad] = first[0:1]
        st_mine[slot, 1:2, 0:rows_pad] = second[0:1]
        all_stats[slot].start()
        st_all[slot, me] = st_mine[slot]

    def total_sums(slot):
        all_stats[slot].finish()
        total = st_all[slot, 0]
        for at in range(1, parts):
            total = total + st_all[slot, at]
        st_sum[...] = jnp.zeros_like(st_sum)
        st_sum[0:2, :] = total
        turned = jnp.transpose(st_sum[...])
        return turned[0:rows_pad, 0:1] * (1.0 / full), turned[0:rows_pad, 1:2] * (1.0 / full)

    st_mine[...] = jnp.zeros_like(st_mine)
    row_sums(0, gain_fc1, gpb[...], prod[:, 0:hidden_width])
    def fc2_cols(who):
        return wfc2[:, pl.ds(pl.multiple_of(who * width, width), width)]

    scat_mlp = Scatter(1, hid, fc2_cols, 1, dot_nn)

    for step in range(1, half):
        scat_two.step(step)
        if step == 1:
            scat_mlp.step(0)
    scat_mlp.step(1)

    def fc2_grad(number):
        result = dot_tn(hid[...], gm[:, number * 256 : (number + 1) * 256]).astype(bf)
        for piece in range(2):
            for side in range(2):
                t2[piece, 2 * number + side] = result[
                    piece * part : (piece + 1) * part, side * width : (side + 1) * width
                ]

    for number in range(parts // 2):
        fc2_grad(number)
    sib_sem = take(1)
    t2_pass = remote(t2, t2s, sib_sem, sib_sem, gx=sib)

    @pl.when(jnp.logical_not(is_owner))
    def _():
        t2_pass.start()

    scat_two.term(half)
    first, second = total_sums(0)
    satt_own = vecs[me, SATT : SATT + 1, :]
    gain_own = vecs[me, GAIN2 : GAIN2 + 1, :]

    def col_sum(value):
        return jnp.sum(value, axis=0, keepdims=True)

    sm[...] = jnp.zeros_like(sm)
    for chunk in range(chunks):
        start, size = span(chunk)
        rows = slice(start, start + size)
        grad_two = scat_two.total(chunk)
        attn_own = ao[me, rows, :]
        mid_value = tg[me, rows, :].astype(f32) + satt_own * attn_own
        mid_own[rows, :] = mid_value
        inv_two = stat[3, rows, :]
        normed = (mid_value - stat[2, rows, :]) * inv_two
        grad_mid = cg[me, rows, :].astype(f32) + inv_two * (
            grad_two * gain_own - first[rows] - normed * second[rows]
        )
        gmid[rows, :] = grad_mid
        grad_attn = grad_mid * satt_own
        hg[me, rows, :] = grad_attn.astype(bf)
        ring_grad.start_chunk(chunk)
        sm[5:6, :] += col_sum(grad_attn)
        sm[6:7, :] += col_sum(grad_mid * attn_own)
        sm[7:8, :] += col_sum(grad_two * normed)
        sm[8:9, :] += col_sum(grad_two)
    if sent_rows < rows_pad:
        for ref in (mid_own, gmid):
            ref[sent_rows:rows_pad, :] = jnp.zeros((rows_pad - sent_rows, width), f32)
    fc1_sum = col_sum(cs_acc[...])
    for at in range(hidden_width // width):
        sm[16 + at : 17 + at, :] = fc1_sum[:, at * width : (at + 1) * width]

    scat_mlp.step(2)

    def rows_grad(dest, left_of, grads):
        for shard in range(4):
            dest[shard % 2, shard // 2] = dot_tn(left_of(shard), grads).astype(bf)

    rows_grad(t1, lambda shard: nt[:, shard * quarter : (shard + 1) * quarter], gpb[...])
    sum_fc1.start()
    ring_grad.advance(0)
    blocks_in = quarter // width
    rows_grad(
        tp,
        lambda shard: jnp.concatenate(
            [ag[shard * blocks_in + b] for b in range(blocks_in)], axis=1
        ),
        hg[me],
    )
    sum_proj.start()
    sum_fc1.cross()

    t2_recv = take(parts)
    t2_send = take(parts)

    def t2_copy(step):
        to = (me + step) % parts
        return remote(t2d.at[to], t2r.at[me], t2_send + step, t2_recv + me, gy=to)

    plane_sem = take(1)
    t2_plane = remote(t2c, t2o, plane_sem, plane_sem, gx=opp)

    @pl.when(is_owner)
    def _():
        t2_pass.wait_recv()
        for at in range(parts):
            t2c[at] = (t2[1 - plane, at].astype(f32) + t2s[1 - plane, at].astype(f32)).astype(bf)
        t2_plane.start()

    ring_grad.advance(1)
    sum_proj.cross()
    ring_grad.advance(2)
    for step in range(3, half):
        ring_grad.advance(step)
    own_rows = pl.ds(pl.multiple_of(me * width, width), width)

    @pl.loop(0, 4)
    def _(number):
        rows = row_tile(number)
        whole = jnp.concatenate([hg[at, rows, :] for at in range(parts)], axis=1)
        gat[rows, :] = dot_nt(whole, wproj[own_rows, :]).astype(bf)

    gat[rows_pad:qpad, :] = jnp.zeros((qpad - rows_pad, 2 * HD), bf)
    for step in range(3, half):
        scat_mlp.step(step)
    gatt = jnp.transpose(gat[...])
    delta_all = gatt.astype(f32) * att[...].astype(f32)
    for head in range(heads):
        value = gat[:, head * HD : (head + 1) * HD]
        dz[head] = jnp.concatenate([jnp.zeros_like(value), value], axis=1)
    deltas = [
        jnp.sum(delta_all[head * HD : (head + 1) * HD], axis=0, keepdims=True) for head in range(heads)
    ]
    dkv[...] = jnp.zeros_like(dkv)

    def attend_back(number, side):
        cols = slice(number * qtile, (number + 1) * qtile)
        keys = slice(side * rows_pad, (side + 1) * rows_pad)
        for head in range(heads):
            probs = pt[head, keys, cols]
            query, grad = qz[head, cols, :], dz[head, cols, :]
            slope = dot_nt(kvc[head, keys, :], grad)
            scores = (probs.astype(f32) * (slope - deltas[head][:, cols])).astype(bf)
            dkv[head, keys, :] += dot_nn(probs, grad) + dot_nn(scores, query)
            part_query = dot_nn(kvt[head, 0:HD, keys], scores)
            here = slice(head * HD, (head + 1) * HD)
            if side == 1:
                dqf[here, cols] = part_query
            else:
                dqf[here, cols] += part_query

    def spread_t2():
        @pl.when(is_owner)
        def _():
            t2_plane.wait_recv()
            for at in range(parts):
                t2d[at] = (
                    t2[plane, at].astype(f32) + t2s[plane, at].astype(f32) + t2o[at].astype(f32)
                ).astype(bf)
            for step in range(1, parts):
                t2_copy(step).start()
            t2r[me] = t2d[me]

    for number in range(qtiles):
        attend_back(number, 1)
        if number == 1:
            spread_t2()
    for head in range(heads):
        dks[head] = dkv[head, rows_pad : 2 * rows_pad, :].astype(bf)
    dk_sem = take(1)
    dk_copy = remote(dks, dkr, dk_sem, dk_sem, gx=sib)
    launch(dk_copy)
    for number in range(qtiles):
        attend_back(number, 0)

    grad_query = jnp.transpose(dqf[...])[0:rows_pad] * (HD ** (-0.5))
    sm[0:1, :] = col_sum(grad_query)
    dk_copy.wait_recv()
    pieces = []
    value_sums = []
    for head in range(heads):
        own = dkv[head, 0:rows_pad, :] + dkr[head].astype(f32)
        value_sums.append(col_sum(own))
        pieces += [grad_query[:, head * HD : (head + 1) * HD], own]
    for head in range(heads):
        sm[1 + head : 2 + head, :] = value_sums[head]
    mixed_grad = jnp.concatenate(pieces, axis=1)
    gmx[...] = mixed_grad.astype(bf)
    prod[:, 0:three] = (mixed_grad * (mixf[...] - shift_qkv)).astype(bf)

    def qkv_rows(who):
        return wqkv[pl.ds(pl.multiple_of(who * width, width), width), :]

    scat_one = Scatter(2, gmx, qkv_rows, 0, dot_nt)
    scat_one.step(0)
    row_sums(1, gain_qkv, gmx[...], prod[:, 0:three])
    rows_grad(tq, lambda shard: nb[:, shard * quarter : (shard + 1) * quarter], gmx[...])
    sum_qkv.start()
    scat_one.step(1)

    scat_mlp.term(half)
    mlp_out = scat_mlp.finish() + vecs[me, FC2B : FC2B + 1, :]
    smlp_own = vecs[me, SMLP : SMLP + 1, :]
    up = cg[me].astype(f32)
    out_ref[...] = (mid_own[...] + smlp_own * mlp_out)[0:count]
    sm[9:10, :] = col_sum(up * smlp_own)
    sm[10:11, :] = col_sum(up * mlp_out)
    sum_qkv.cross()
    for step in range(2, half):
        scat_one.step(step)
    sum_fc1.finish()
    sum_proj.finish()

    for step in range(4):
        source = (step // 2) * (parts // 2) + 2 * core + step % 2

        @pl.when(source != me)
        def _():
            remote(t2d.at[me], t2r.at[source], t2_send, t2_recv + source, gy=source).wait_recv()

    x_sem = take(1)
    t2_cross = remote(t2r.at[pl.ds(2 * opp, 2)], t2x, x_sem, x_sem, gx=opp)
    launch(t2_cross)
    scat_one.term(half)
    t2_cross.wait_recv()
    for block in range(2):
        for at, value in ((plane, t2r[2 * i + block]), (1 - plane, t2x[block])):
            rows = pl.ds(pl.multiple_of(block * lines + at * part, part), part)
            gfc2_ref[rows, :] = value.astype(f32)
    sum_qkv.finish()

    grad_one = scat_one.finish()
    first, second = total_sums(1)
    inv_one = stat[1]
    normed = (tg[me].astype(f32) - stat[0]) * inv_one
    gain_own = vecs[me, GAIN1 : GAIN1 + 1, :]
    gin_ref[...] = (gmid[...] + inv_one * (grad_one * gain_own - first - normed * second))[0:count]
    sm[3:4, :] = col_sum(grad_one * normed)
    sm[4:5, :] = col_sum(grad_one)
    sma[i] = sm[...]
    small_sem = take(3)
    copies = [
        remote(sm, sma.at[i], small_sem + n, small_sem + n, gx=to)
        for n, to in enumerate((sib, opp, dia))
    ]
    for copy in copies:
        launch(copy)
    for copy in copies:
        copy.wait_recv()
    small_ref[...] = sma[0] + sma[1] + sma[2] + sma[3]

    for copy in started:
        copy.wait_send()
    for block in range(4):
        target, _, copy = fc2_copy(block)

        @pl.when(target != me)
        def _():
            copy.wait_send()

    @pl.when(is_owner)
    def _():
        fc2_opp.wait_send()
        fc2_sib.wait_send()
        fc2_far.wait_send()
        t2_plane.wait_send()
        for step in range(1, parts):
            t2_copy(step).wait_send()

    @pl.when(jnp.logical_not(is_owner))
    def _():
        t2_pass.wait_send()


def emit_kernel(heads, hidden_width, small_ref, *refs):
    sources, results = refs[:6], refs[6:22]
    for source, result in zip(sources, results):
        result[...] = source[...]
    qv_ref, fc1_ref = results[6:8]
    width = small_ref.shape[1]
    for head in range(heads):
        row = jnp.concatenate(
            [small_ref[0:1, head * HD : (head + 1) * HD], small_ref[1 + head : 2 + head, HD : 2 * HD]],
            axis=1,
        )
        qv_ref[head * 2 * HD : (head + 1) * 2 * HD] = row.reshape(2 * HD)
    for at in range(hidden_width // width):
        fc1_ref[at * width : (at + 1) * width] = small_ref[16 + at : 17 + at, :].reshape(width)
    for at, ref in enumerate(results[8:]):
        ref[...] = small_ref[3 + at : 4 + at, :].reshape(width)


def on_device(*args):
    (
        tokens,
        cotangent,
        norm1_gain,
        norm1_shift,
        qkv_weight,
        qv_bias,
        proj_weight,
        proj_bias,
        scale_attn,
        norm2_gain,
        norm2_shift,
        fc1_weight,
        fc1_bias,
        fc2_weight,
        fc2_bias,
        scale_mlp,
    ) = args
    parts, rows_over = lax.axis_size("gy"), lax.axis_size("gx")
    count, width = tokens.shape
    heads = qkv_weight.shape[1] // (3 * HD)
    hidden_width = fc1_weight.shape[1]
    if (
        rows_over != 4
        or parts != 8
        or width != 128
        or heads != 2
        or IMGS != 1
        or hidden_width % 256
    ):
        return on_device_plain(*args)
    full = parts * width
    rows = up_to(count, 64)
    qpad = up_to(rows, 256)
    three = heads * 3 * HD
    quarter = full // 4
    lines = fc2_weight.shape[0] // 2
    half = parts // 2
    bf, f32 = jnp.bfloat16, jnp.float32
    wide = max(three, hidden_width)
    stat_wide = up_to(rows, 256)
    V = pltpu.VMEM
    scratch = [
        V((parts, rows, width), bf),
        V((parts, rows, width), bf),
        V((parts, rows, width), bf),
        V((parts, rows, width), bf),
        V((parts, 8, width), f32),
        V((full, three), bf),
        V((full, hidden_width), bf),
        V((4, parts, quarter, width), bf),
        V((full, full), bf),
        V((2, lines // 2, width), bf),
        V((2, parts, lines // 2, width), bf),
        V((lines, full), bf),
        V((rows, full), bf),
        V((rows, full), bf),
        V((rows, full), bf),
        V((4, rows, 1), f32),
        V((rows, three), f32),
        V((rows, three), bf),
        V((rows, three), bf),
        V((heads, 2 * rows, 2 * HD), bf),
        V((heads, 2 * HD, 2 * rows), bf),
        V((heads, qpad, 2 * HD), bf),
        V((heads, qpad, 2 * HD), bf),
        V((heads, 2 * rows, qpad), bf),
        V((heads * HD, qpad), bf),
        V((8, width), f32),
        V((parts, rows, width), f32),
        V((rows, hidden_width), f32),
        V((rows, hidden_width), bf),
        V((rows, hidden_width), bf),
        V((rows, wide), bf),
        V((rows, 2 * width), f32),
        V((3, 2, half, rows, width), bf),
        V((3, 2, half, rows, width), bf),
        V((2, 2, stat_wide), f32),
        V((2, parts, 2, stat_wide), f32),
        V((8, stat_wide), f32),
        V((rows, width), f32),
        V((rows, width), f32),
        V((qpad, width), bf),
        V((heads, 2 * rows, 2 * HD), f32),
        V((heads, rows, 2 * HD), bf),
        V((heads, rows, 2 * HD), bf),
        V((heads * HD, qpad), f32),
        V((rows, three), bf),
        V((2, 2, quarter, three), bf),
        V((2, quarter, three), bf),
        V((quarter, three), bf),
        V((quarter, three), bf),
        V((2, 2, quarter, width), bf),
        V((2, quarter, width), bf),
        V((quarter, width), bf),
        V((quarter, width), bf),
        V((2, 2, quarter, hidden_width), bf),
        V((2, quarter, hidden_width), bf),
        V((quarter, hidden_width), bf),
        V((quarter, hidden_width), bf),
        V((2, parts, lines // 2, width), bf),
        V((2, parts, lines // 2, width), bf),
        V((parts, lines // 2, width), bf),
        V((parts, lines // 2, width), bf),
        V((parts, lines // 2, width), bf),
        V((parts, lines // 2, width), bf),
        V((2, lines // 2, width), bf),
        V((24, width), f32),
        V((4, 24, width), f32),
        V((8, hidden_width), f32),
        pltpu.SemaphoreType.DMA((SEMS,)),
        pltpu.SemaphoreType.DMA((SEMS,)),
    ]
    vmem = pl.BlockSpec(memory_space=pltpu.VMEM)
    results = pl.pallas_call(
        functools.partial(mega_kernel, parts, count, heads, hidden_width, SEMS),
        out_shape=[
            jax.ShapeDtypeStruct((count, width), f32),
            jax.ShapeDtypeStruct((count, width), f32),
            jax.ShapeDtypeStruct((24, width), f32),
            jax.ShapeDtypeStruct((quarter, three), f32),
            jax.ShapeDtypeStruct((quarter, width), f32),
            jax.ShapeDtypeStruct((quarter, hidden_width), f32),
            jax.ShapeDtypeStruct((2 * lines, width), f32),
        ],
        in_specs=[vmem] * 16,
        out_specs=[vmem] * 7,
        scratch_shapes=scratch,
        compiler_params=pltpu.CompilerParams(
            collective_id=3, has_side_effects=True, vmem_limit_bytes=VMEM_BYTES
        ),
    )(
        tokens,
        cotangent,
        norm1_gain,
        norm1_shift,
        qkv_weight,
        qv_bias,
        proj_weight,
        proj_bias,
        scale_attn,
        norm2_gain,
        norm2_shift,
        fc1_weight,
        fc1_bias,
        fc2_weight,
        fc2_bias,
        scale_mlp,
    )
    output, grad_in, small, grad_qkv, grad_proj, grad_fc1, grad_fc2 = results
    line = jax.ShapeDtypeStruct((width,), f32)
    large = [output, grad_in, grad_qkv, grad_proj, grad_fc1, grad_fc2]
    written = pl.pallas_call(
        functools.partial(emit_kernel, heads, hidden_width),
        out_shape=[jax.ShapeDtypeStruct(array.shape, f32) for array in large]
        + [
            jax.ShapeDtypeStruct((heads * 2 * HD,), f32),
            jax.ShapeDtypeStruct((hidden_width,), f32),
        ]
        + [line] * 8,
        in_specs=[vmem] * 7,
        out_specs=[vmem] * 16,
    )(small, *large)
    output, grad_in, grad_qkv, grad_proj, grad_fc1, grad_fc2, grad_qv, grad_fc1_bias = written[:8]
    lines_out = written[8:]
    return (
        output,
        grad_in,
        lines_out[0],
        lines_out[1],
        grad_qkv,
        grad_qv,
        grad_proj,
        lines_out[2],
        lines_out[3],
        lines_out[4],
        lines_out[5],
        grad_fc1,
        grad_fc1_bias,
        grad_fc2,
        lines_out[6],
        lines_out[7],
    )


def solution(mesh):
    return jax.shard_map(
        on_device,
        mesh=mesh,
        in_specs=(
            P("gx", "gy"),
            P("gx", "gy"),
            P("gy"),
            P("gy"),
            P("gx", "gy"),
            P("gy"),
            P("gx", "gy"),
            P("gy"),
            P("gy"),
            P("gy"),
            P("gy"),
            P("gx", "gy"),
            P("gy"),
            P("gx", "gy"),
            P("gy"),
            P("gy"),
        ),
        out_specs=(
            P("gx", "gy"),
            P("gx", "gy"),
            P("gy"),
            P("gy"),
            P("gx", "gy"),
            P("gy"),
            P("gx", "gy"),
            P("gy"),
            P("gy"),
            P("gy"),
            P("gy"),
            P("gx", "gy"),
            P("gy"),
            P("gx", "gy"),
            P("gy"),
            P("gy"),
        ),
        check_vma=False,
    )
```

```python
import functools

import jax
import jax.numpy as jnp
from jax import lax
from jax.experimental import pallas as pl
from jax.experimental.pallas import tpu as pltpu
from jax.sharding import PartitionSpec as P

D = 1024
HD = 64
IMGS = 1


EPS = 1e-06
ROOT_HALF = 0.7071067811865476
INV_ROOT_TAU = 0.3989422804014327
SEMS = 400
VMEM_BYTES = 62 * 1024 * 1024


def from_partner(block, axis, bit):
    count = lax.axis_size(axis)
    route = []
    for low in range(count):
        high = low | 1 << bit
        if high != low and high < count:
            route += [(low, high), (high, low)]
    return lax.ppermute(block, axis, route)


def normal_cdf(values):
    return 0.5 * (1.0 + jax.scipy.special.erf(values * ROOT_HALF))


def gelu_exact(values):
    return values * normal_cdf(values)


def gelu_slope(values):
    return normal_cdf(values) + values * jnp.exp(-0.5 * values * values) * INV_ROOT_TAU


def norm_full(rows, gain, shift):
    row_mean = jnp.mean(rows, axis=1, keepdims=True)
    inv_std = lax.rsqrt(jnp.mean(rows * rows, axis=1, keepdims=True) - row_mean * row_mean + EPS)
    normed = (rows - row_mean) * inv_std
    return (normed, inv_std, (normed * gain + shift).astype(jnp.bfloat16))


def gather_columns(block):
    return lax.all_gather(block, "gy", axis=1, tiled=True)


def ring_kernel(parts, block_ref, out_ref, send_sem, recv_sem):
    half = parts // 2

    def index_of(place):
        back = place // half
        return (1 - back) * (2 * place) + back * (2 * (parts - 1 - place) + 1)

    me = lax.axis_index("gy")
    odd = me % 2
    place = (1 - odd) * (me // 2) + odd * (parts - 1 - me // 2)
    sides = (index_of((place + 1) % parts), index_of((place + parts - 1) % parts))
    barrier = pltpu.get_barrier_semaphore()
    for side in sides:
        pl.semaphore_signal(
            barrier, inc=1, device_id={"gy": side}, device_id_type=pl.DeviceIdType.MESH
        )
    pl.semaphore_wait(barrier, 2)
    copies = []
    for step in range(half):
        owners = (
            index_of((place + parts - step) % parts),
            index_of((place + step) % parts),
        )
        started = []
        for way in range(2):
            if way == 1 and step == half - 1:
                continue
            copy = pltpu.make_async_remote_copy(
                src_ref=block_ref if step == 0 else out_ref.at[owners[way]],
                dst_ref=out_ref.at[owners[way]],
                send_sem=send_sem.at[way, step],
                recv_sem=recv_sem.at[way, step],
                device_id={"gy": sides[way]},
                device_id_type=pl.DeviceIdType.MESH,
            )
            copy.start()
            started.append(copy)
        if step == 0:
            out_ref[me] = block_ref[...]
        for copy in started:
            copy.wait_recv()
        copies += started
    for copy in copies:
        copy.wait_send()


def ring_columns(block, call):
    parts = lax.axis_size("gy")
    count, width = block.shape
    if parts % 2 or parts < 4:
        return gather_columns(block)
    got = pl.pallas_call(
        functools.partial(ring_kernel, parts),
        out_shape=jax.ShapeDtypeStruct((parts, count, width), block.dtype),
        in_specs=[pl.BlockSpec(memory_space=pltpu.VMEM)],
        out_specs=pl.BlockSpec(memory_space=pltpu.VMEM),
        scratch_shapes=[
            pltpu.SemaphoreType.DMA((2, parts // 2)),
            pltpu.SemaphoreType.DMA((2, parts // 2)),
        ],
        compiler_params=pltpu.CompilerParams(collective_id=call, has_side_effects=True),
    )(block)
    return jnp.transpose(got, (1, 0, 2)).reshape(count, parts * width)


def spread_columns(block):
    parts = lax.axis_size("gy")
    got = lax.all_to_all(
        jnp.broadcast_to(block[None], (parts,) + block.shape), "gy", 0, 0, tiled=True
    )
    return jnp.transpose(got, (1, 0, 2)).reshape(block.shape[0], parts * block.shape[1])


def column_blocks(block):
    parts = lax.axis_size("gy")
    count, full = block.shape
    return jnp.transpose(block.reshape(count, parts, full // parts), (1, 0, 2))


def scatter_sum(blocks, axis):
    got = lax.all_to_all(blocks, axis, 0, 0, tiled=True)
    return jnp.sum(got.astype(jnp.float32), axis=0)


def own_columns(block, width):
    return lax.dynamic_slice_in_dim(block, lax.axis_index("gy") * width, width, axis=1)


def sum_rows(term):
    parts = lax.axis_size("gx")
    blocks = term.reshape(parts, term.shape[0] // parts, term.shape[1])
    return scatter_sum(blocks, "gx")


def weight_grad_rows(saved, grad_out):
    term = jnp.einsum("tk,tn->kn", saved, grad_out, preferred_element_type=jnp.float32)
    return lax.psum_scatter(
        term.astype(jnp.bfloat16), "gx", scatter_dimension=0, tiled=True
    ).astype(jnp.float32)


def weight_grad(saved, grad_out):
    term = jnp.einsum("tk,tn->kn", saved, grad_out, preferred_element_type=jnp.float32)
    return sum_rows(term.astype(jnp.bfloat16))


def lanes_of(column, width):
    count = column.shape[0]
    lines = -(-count // width)
    return jnp.pad(column, (0, lines * width - count)).reshape(lines, width)


def back_norm(grad_out, weight, normed, normed_own, inv_std, gain, gain_own):
    parts = lax.axis_size("gy")
    count, full = normed.shape
    width = full // parts
    term = jnp.einsum("tn,kn->tk", grad_out, weight, preferred_element_type=jnp.float32)
    scaled = term * gain
    first = lanes_of(jnp.sum(scaled, axis=1), width)
    second = lanes_of(jnp.sum(scaled * normed, axis=1), width)
    lines = first.shape[0]
    sums = jnp.concatenate([first, second], axis=0).astype(jnp.bfloat16)
    blocks = column_blocks(term.astype(jnp.bfloat16))
    sent = jnp.concatenate(
        [blocks, jnp.broadcast_to(sums[None], (parts,) + sums.shape)], axis=1
    )
    back = scatter_sum(sent, "gy")
    grad_normed = back[:count]
    first = back[count : count + lines].reshape(-1)[:count, None]
    second = back[count + lines :].reshape(-1)[:count, None]
    grad_rows = inv_std * (
        grad_normed * gain_own - first / full - normed_own * (second / full)
    )
    return (
        grad_rows,
        jnp.sum(grad_normed * normed_own, axis=0),
        jnp.sum(grad_normed, axis=0),
    )


def on_device_plain(
    tokens,
    cotangent,
    norm1_gain,
    norm1_shift,
    qkv_weight,
    qv_bias,
    proj_weight,
    proj_bias,
    scale_attn,
    norm2_gain,
    norm2_shift,
    fc1_weight,
    fc1_bias,
    fc2_weight,
    fc2_bias,
    scale_mlp,
):
    count = tokens.shape[0]
    half_len = count // IMGS
    heads_here = qkv_weight.shape[1] // (3 * HD)
    factor = HD ** (-0.5)
    width = tokens.shape[1]
    full_tokens = ring_columns(tokens, 0)
    vectors = spread_columns(
        jnp.stack([norm1_gain, norm1_shift, proj_bias, scale_attn, norm2_gain, norm2_shift, scale_mlp])
    )
    gain_one, shift_one, bias_proj, full_scale_attn, gain_two, shift_two, full_scale_mlp = vectors
    full_qkv = lax.all_gather(qkv_weight, "gx", axis=0, tiled=True)
    all_proj = lax.all_gather(ring_columns(proj_weight, 1), "gx", axis=0, tiled=True)
    full_fc1 = lax.all_gather(fc1_weight, "gx", axis=0, tiled=True)
    full_fc2 = lax.all_gather(fc2_weight, "gx", axis=0, tiled=True)
    rows_fc2 = lax.all_to_all(full_fc2, "gy", split_axis=0, concat_axis=1, tiled=True)
    full_cotangent = gather_columns(cotangent)
    inputs = full_tokens.astype(jnp.float32)
    normed_one, inv_one, norm_one = norm_full(inputs, gain_one, shift_one)
    mixed = jnp.dot(norm_one, full_qkv, preferred_element_type=jnp.float32)
    mixed = mixed.reshape(count, heads_here, 3, HD)
    biases = qv_bias.reshape(heads_here, 2, HD)
    queries = (mixed[:, :, 0] + biases[:, 0]).astype(jnp.bfloat16)
    keys = mixed[:, :, 1].astype(jnp.bfloat16)
    values = (mixed[:, :, 2] + biases[:, 1]).astype(jnp.bfloat16)
    lower = lax.axis_index("gx") % 2 == 0
    pair_kv = jnp.concatenate([keys, values], axis=2).reshape(count, heads_here * 2 * HD)
    other_kv = from_partner(pair_kv, "gx", 0)
    first_kv = jnp.where(lower, pair_kv, other_kv)
    second_kv = jnp.where(lower, other_kv, pair_kv)
    image_shape = (IMGS, half_len, heads_here, 2 * HD)
    both_kv = jnp.concatenate(
        [first_kv.reshape(image_shape), second_kv.reshape(image_shape)], axis=1
    )
    key_all = both_kv[..., :HD]
    value_all = both_kv[..., HD:]
    query_img = queries.reshape(IMGS, half_len, heads_here, HD)
    scores = (
        jnp.einsum("iqhe,ikhe->ihqk", query_img, key_all, preferred_element_type=jnp.float32)
        * factor
    )
    row_max = jnp.max(scores, axis=3, keepdims=True)
    exponent = jnp.exp(scores - row_max)
    totals = jnp.sum(exponent, axis=3, keepdims=True)
    log_total = row_max + jnp.log(totals)
    probs = (exponent / totals).astype(jnp.bfloat16)
    attended_img = jnp.einsum(
        "ihqk,ikhe->iqhe", probs, value_all, preferred_element_type=jnp.float32
    ).astype(jnp.bfloat16)
    attended = attended_img.reshape(count, heads_here * HD)
    full_attended = ring_columns(attended, 0)
    attn_out = jnp.dot(full_attended, all_proj, preferred_element_type=jnp.float32) + bias_proj
    middle = inputs + full_scale_attn * attn_out
    normed_two, inv_two, norm_two = norm_full(middle, gain_two, shift_two)
    pre_act = jnp.dot(norm_two, full_fc1, preferred_element_type=jnp.float32) + fc1_bias
    hidden = gelu_exact(pre_act).astype(jnp.bfloat16)
    upstream = cotangent.astype(jnp.float32)
    grad_mlp = upstream * scale_mlp
    grad_fc2_bias = jnp.sum(grad_mlp, axis=0)
    full_grad_mlp_b = (full_cotangent.astype(jnp.float32) * full_scale_mlp).astype(jnp.bfloat16)
    grad_hidden = jnp.einsum(
        "tn,kn->tk", full_grad_mlp_b, rows_fc2, preferred_element_type=jnp.float32
    )
    grad_pre = grad_hidden * gelu_slope(pre_act)
    grad_fc1_bias = jnp.sum(grad_pre, axis=0)
    grad_pre_b = grad_pre.astype(jnp.bfloat16)
    own_two = own_columns(normed_two, width)
    grad_rows, grad_gain_two, grad_shift_two = back_norm(
        grad_pre_b, full_fc1, normed_two, own_two, inv_two, gain_two, norm2_gain
    )
    grad_middle = upstream + grad_rows
    grad_scale_attn = jnp.sum(grad_middle * own_columns(attn_out, width), axis=0)
    grad_attn = grad_middle * scale_attn
    grad_proj_bias = jnp.sum(grad_attn, axis=0)
    grad_attn_b = grad_attn.astype(jnp.bfloat16)
    full_grad_attn_b = ring_columns(grad_attn_b, 0)
    own_rows_proj = lax.dynamic_slice_in_dim(
        all_proj, lax.axis_index("gy") * width, width, axis=0
    )
    grad_attended = jnp.einsum(
        "tn,kn->tk", full_grad_attn_b, own_rows_proj, preferred_element_type=jnp.float32
    ).astype(jnp.bfloat16)
    mlp_term = jnp.dot(hidden, rows_fc2, preferred_element_type=jnp.float32)
    mlp_out = (
        lax.psum_scatter(
            column_blocks(mlp_term.astype(jnp.bfloat16)), "gy", scatter_dimension=0, tiled=False
        ).astype(jnp.float32)
        + fc2_bias
    )
    output = own_columns(middle, width) + scale_mlp * mlp_out
    grad_scale_mlp = jnp.sum(upstream * mlp_out, axis=0)
    fc2_term = jnp.einsum(
        "tk,tn->kn", hidden, full_grad_mlp_b, preferred_element_type=jnp.float32
    )
    fc2_blocks = lax.all_to_all(column_blocks(fc2_term.astype(jnp.bfloat16)), "gy", 0, 0, tiled=True)
    grad_fc2 = sum_rows(fc2_blocks.reshape(-1, width))
    grad_fc1 = weight_grad_rows(norm_two, grad_pre_b)
    grad_proj = weight_grad_rows(full_attended, grad_attn_b)
    grad_att_img = grad_attended.reshape(IMGS, half_len, heads_here, HD)
    recomputed = jnp.exp(scores - log_total)
    probs_b = recomputed.astype(jnp.bfloat16)
    grad_value_all = jnp.einsum(
        "ihqk,iqhe->ikhe", probs_b, grad_att_img, preferred_element_type=jnp.float32
    )
    grad_probs = jnp.einsum(
        "iqhe,ikhe->ihqk", grad_att_img, value_all, preferred_element_type=jnp.float32
    )
    delta = jnp.sum(grad_att_img.astype(jnp.float32) * attended_img.astype(jnp.float32), axis=3)
    grad_scores = recomputed * (grad_probs - jnp.transpose(delta, (0, 2, 1))[..., None])
    grad_scores_b = grad_scores.astype(jnp.bfloat16)
    grad_query = (
        jnp.einsum("ihqk,ikhe->iqhe", grad_scores_b, key_all, preferred_element_type=jnp.float32)
        * factor
    )
    grad_key_all = (
        jnp.einsum("ihqk,iqhe->ikhe", grad_scores_b, query_img, preferred_element_type=jnp.float32)
        * factor
    )
    grad_kv_all = jnp.concatenate([grad_key_all, grad_value_all], axis=3)
    first_part = grad_kv_all[:, :half_len].reshape(count, heads_here * 2 * HD)
    second_part = grad_kv_all[:, half_len:].reshape(count, heads_here * 2 * HD)
    own_part = jnp.where(lower, first_part, second_part)
    sent_part = jnp.where(lower, second_part, first_part)
    grad_kv = own_part + from_partner(sent_part.astype(jnp.bfloat16), "gx", 0).astype(
        sent_part.dtype
    )
    grad_kv = grad_kv.reshape(count, heads_here, 2, HD)
    grad_query = grad_query.reshape(count, heads_here, HD)
    grad_qv_bias = jnp.stack(
        [jnp.sum(grad_query, axis=0), jnp.sum(grad_kv[:, :, 1], axis=0)], axis=1
    ).reshape(heads_here * 2 * HD)
    grad_mixed = (
        jnp.stack([grad_query, grad_kv[:, :, 0], grad_kv[:, :, 1]], axis=2)
        .astype(jnp.bfloat16)
        .reshape(count, heads_here * 3 * HD)
    )
    grad_qkv = weight_grad(norm_one, grad_mixed)
    own_one = own_columns(normed_one, width)
    grad_rows, grad_gain_one, grad_shift_one = back_norm(
        grad_mixed, full_qkv, normed_one, own_one, inv_one, gain_one, norm1_gain
    )
    grad_input = grad_middle + grad_rows
    smalls = lax.psum(
        (
            grad_gain_one,
            grad_shift_one,
            grad_qv_bias,
            grad_proj_bias,
            grad_scale_attn,
            grad_gain_two,
            grad_shift_two,
            grad_fc1_bias,
            grad_fc2_bias,
            grad_scale_mlp,
        ),
        "gx",
    )
    return (
        output,
        grad_input,
        smalls[0],
        smalls[1],
        grad_qkv,
        smalls[2],
        grad_proj,
        smalls[3],
        smalls[4],
        smalls[5],
        smalls[6],
        grad_fc1,
        smalls[7],
        grad_fc2,
        smalls[8],
        smalls[9],
    )


def up_to(value, step):
    return -(-value // step) * step


def dot_nn(a, b):
    return lax.dot_general(a, b, (((1,), (0,)), ((), ())), preferred_element_type=jnp.float32)


def dot_nt(a, b):
    return lax.dot_general(a, b, (((1,), (1,)), ((), ())), preferred_element_type=jnp.float32)


def dot_tn(a, b):
    return lax.dot_general(a, b, (((0,), (0,)), ((), ())), preferred_element_type=jnp.float32)


def split_high(values):
    high = values.astype(jnp.bfloat16)
    return high, (values - high.astype(jnp.float32)).astype(jnp.bfloat16)


def mega_kernel(
    parts,
    count,
    heads,
    hidden_width,
    sems,
    tok_ref,
    cot_ref,
    gain1_ref,
    shift1_ref,
    qkv_ref,
    qv_ref,
    proj_ref,
    bproj_ref,
    satt_ref,
    gain2_ref,
    shift2_ref,
    fc1_ref,
    bfc1_ref,
    fc2_ref,
    bfc2_ref,
    smlp_ref,
    out_ref,
    gin_ref,
    small_ref,
    gqkv_ref,
    gproj_ref,
    gfc1_ref,
    gfc2_ref,
    tg,
    cg,
    ag,
    hg,
    vecs,
    wqkv,
    wfc1,
    projg,
    wproj,
    fc2x,
    fc2h,
    wfc2,
    nb,
    nt,
    gm,
    stat,
    mixf,
    qkvb,
    qkvo,
    kvc,
    kvt,
    qz,
    dz,
    pt,
    att,
    vec_ref,
    ao,
    gh,
    hid,
    gpb,
    prod,
    tscr,
    rs_send,
    rs_recv,
    st_mine,
    st_all,
    st_sum,
    mid_own,
    gmid,
    gat,
    dkv,
    dks,
    dkr,
    dqf,
    gmx,
    tq,
    tqs,
    tqc,
    tqx,
    tp,
    tps,
    tpc,
    tpx,
    t1,
    t1s,
    t1c,
    t1x,
    t2,
    t2s,
    t2c,
    t2o,
    t2d,
    t2r,
    t2x,
    sm,
    sma,
    cs_acc,
    ssem,
    rsem,
):
    width = 128
    full = parts * width
    half = parts // 2
    rows_pad = tg.shape[1]
    tile = rows_pad // 4
    mid_row = rows_pad // 2
    three = heads * 3 * HD
    qpad = qz.shape[1]
    f32, bf = jnp.float32, jnp.bfloat16
    MESH = pl.DeviceIdType.MESH
    i = lax.axis_index("gx")
    me = lax.axis_index("gy")
    core = i % 2
    plane = i // 2
    sib = plane * 2 + (1 - core)
    opp = (1 - plane) * 2 + core
    dia = (1 - plane) * 2 + (1 - core)
    odd = me % 2
    place = (1 - odd) * (me // 2) + odd * (parts - 1 - me // 2)

    def index_of(spot):
        spot = (spot + 2 * parts) % parts
        back = spot // half
        return (1 - back) * (2 * spot) + back * (2 * (parts - 1 - spot) + 1)

    right, left = index_of(place + 1), index_of(place - 1)
    used = [0]
    started = []

    def take(number):
        first = used[0]
        used[0] += number
        assert used[0] <= sems
        return first

    def remote(src, dst, send, recv, **where):
        return pltpu.make_async_remote_copy(
            src_ref=src,
            dst_ref=dst,
            send_sem=ssem.at[send],
            recv_sem=rsem.at[recv],
            device_id=where,
            device_id_type=MESH,
        )

    def launch(copy):
        copy.start()
        started.append(copy)

    sent_rows = up_to(count, 16)
    chunks = 4

    def span(chunk):
        return chunk * tile, min((chunk + 1) * tile, sent_rows) - chunk * tile

    def piece(chunk):
        return pl.ds(*span(chunk))

    def first_way(chunk, way):
        return (chunk < chunks // 2) == (way == 0)

    class Ring:
        def __init__(self, buf, height=None):
            self.buf, self.height = buf, height
            self.chunks = chunks if height is None else 2
            self.base = take(2 * half * self.chunks)

        def has(self, way, step, chunk):
            return step < half - 1 or (chunk < self.chunks // 2) == (way == 0)

        def copy(self, way, step, chunk):
            owner = index_of(place - step if way == 0 else place + step)
            if self.height is None:
                ref = self.buf.at[owner, piece(chunk)]
            else:
                ref = self.buf.at[owner, pl.ds(chunk * self.height // 2, self.height // 2)]
            sem = self.base + (way * half + step) * self.chunks + chunk
            return remote(ref, ref, sem, sem, gy=right if way == 0 else left)

        def order(self):
            for chunk in range(self.chunks):
                yield 0, chunk
                yield 1, self.chunks - 1 - chunk

        def start_chunk(self, chunk):
            for way in range(2):
                if self.has(way, 0, chunk):
                    launch(self.copy(way, 0, chunk))

        def start(self):
            for way, chunk in self.order():
                if self.has(way, 0, chunk):
                    launch(self.copy(way, 0, chunk))

        def advance(self, step):
            for way, chunk in self.order():
                if self.has(way, step, chunk):
                    self.copy(way, step, chunk).wait_recv()
                    if step + 1 < half and self.has(way, step + 1, chunk):
                        launch(self.copy(way, step + 1, chunk))

        def last(self, chunk):
            for way in range(2):
                if self.has(way, half - 1, chunk):
                    self.copy(way, half - 1, chunk).wait_recv()

    class Scatter:
        def __init__(self, slot, lhs, weight_rows, join, multiply):
            self.send, self.recv = rs_send.at[slot], rs_recv.at[slot]
            self.lhs, self.weight_rows, self.join, self.multiply = lhs, weight_rows, join, multiply
            self.base = take(2 * half * chunks)
            self.scr = tscr

        def has(self, way, step, chunk):
            return 0 <= step < half and (step > 0 or first_way(chunk, way))

        def copy(self, way, step, chunk):
            sem = self.base + (way * half + step) * chunks + chunk
            return remote(
                self.send.at[way, step, piece(chunk)],
                self.recv.at[way, step, piece(chunk)],
                sem,
                sem,
                gy=right if way == 0 else left,
            )

        def weight(self, step):
            first = self.weight_rows(index_of(place + half - step))
            if 0 < step < half:
                second = self.weight_rows(index_of(place - half + step))
                return jnp.concatenate([first, second], axis=self.join)
            return first

        def term(self, step):
            weight = self.weight(step)
            wide = weight.shape[self.join]

            @pl.loop(0, 2)
            def _(number):
                at = pl.ds(pl.multiple_of(number * mid_row, mid_row), mid_row)
                self.scr[at, 0:wide] = self.multiply(self.lhs[at, :], weight)

        def send_one(self, way, step, chunk, value):
            if self.has(way, step - 1, chunk):
                self.copy(way, step - 1, chunk).wait_recv()
                value = value + self.recv[way, step - 1, piece(chunk), :].astype(f32)
            self.send[way, step, piece(chunk), :] = value.astype(bf)
            launch(self.copy(way, step, chunk))

        def open_chunk(self, chunk):
            start, size = span(chunk)
            value = self.multiply(self.lhs[start : start + size, :], self.weight(0))
            self.send_one(0 if first_way(chunk, 0) else 1, 0, chunk, value)

        def put(self, step):
            lanes = (0, 0 if step == 0 else width)
            for at in range(chunks):
                for way in range(2):
                    chunk = (at + chunks // 2) % chunks if way == 0 else at
                    if self.has(way, step, chunk):
                        lane = lanes[way]
                        self.send_one(
                            way, step, chunk, self.scr[piece(chunk), lane : lane + width]
                        )

        def step(self, step):
            self.term(step)
            self.put(step)

        def total(self, chunk):
            value = self.scr[piece(chunk), 0:width]
            for way in range(2):
                self.copy(way, half - 1, chunk).wait_recv()
                value = value + self.recv[way, half - 1, piece(chunk), :].astype(f32)
            return value

        def finish(self):
            pieces = [self.total(chunk) for chunk in range(chunks)]
            if sent_rows < rows_pad:
                pieces.append(jnp.zeros((rows_pad - sent_rows, width), f32))
            return jnp.concatenate(pieces, axis=0)

    class Gather:
        def __init__(self, view):
            self.view, self.base = view, take(3)

        def copy(self, which):
            shard = opp if which == 2 else i
            to = opp if which == 1 else sib
            ref = self.view(shard)
            return remote(ref, ref, self.base + which, self.base + which, gx=to)

        def start(self):
            launch(self.copy(1))
            launch(self.copy(0))

        def forward(self):
            self.copy(1).wait_recv()
            launch(self.copy(2))

        def finish(self):
            self.copy(0).wait_recv()
            self.copy(2).wait_recv()

    class RowSum:
        def __init__(self, term, from_sib, sent, from_opp, out):
            self.refs = (term, from_sib, sent, from_opp, out)
            self.base = take(2)

        def first(self):
            term, from_sib = self.refs[:2]
            return remote(term.at[1 - core], from_sib, self.base, self.base, gx=sib)

        def second(self):
            sent, from_opp = self.refs[2:4]
            return remote(sent, from_opp, self.base + 1, self.base + 1, gx=opp)

        def start(self):
            launch(self.first())

        def cross(self):
            term, from_sib, sent = self.refs[:3]
            self.first().wait_recv()
            sent[...] = (
                term[core, 1 - plane].astype(f32) + from_sib[1 - plane].astype(f32)
            ).astype(bf)
            launch(self.second())

        def finish(self):
            term, from_sib, _, from_opp, out = self.refs
            self.second().wait_recv()
            out[...] = (
                term[core, plane].astype(f32)
                + from_sib[plane].astype(f32)
                + from_opp[...].astype(f32)
            )

    ring_tok, ring_cot, ring_att, ring_grad = Ring(tg), Ring(cg), Ring(ag), Ring(hg)
    quarter = full // 4
    ring_proj = Ring(projg.at[i], quarter)
    gat_qkv = Gather(lambda shard: wqkv.at[pl.ds(pl.multiple_of(shard * quarter, quarter), quarter)])
    gat_fc1 = Gather(lambda shard: wfc1.at[pl.ds(pl.multiple_of(shard * quarter, quarter), quarter)])
    gat_proj = Gather(lambda shard: projg.at[shard])
    sum_qkv = RowSum(tq, tqs, tqc, tqx, gqkv_ref)
    sum_proj = RowSum(tp, tps, tpc, tpx, gproj_ref)
    sum_fc1 = RowSum(t1, t1s, t1c, t1x, gfc1_ref)

    class Spread:
        def __init__(self, src, view, number):
            self.src, self.view = src, view
            self.sends, self.recvs = take(parts), take(parts)

        def start(self):
            for step in range(1, parts):
                to = (me + step) % parts
                launch(
                    remote(self.src(to), self.view(me), self.sends + step, self.recvs + me, gy=to)
                )

        def wait(self, other):
            remote(self.src(other), self.view(other), self.sends, self.recvs + other, gy=other).wait_recv()

        def finish(self):
            for step in range(1, parts):
                self.wait((me + step) % parts)

    all_vecs = Spread(lambda to: vec_ref, lambda who: vecs.at[who], 0)
    all_stats = [
        Spread(lambda to, k=k: st_mine.at[k], lambda who, k=k: st_all.at[k, who], 0) for k in range(2)
    ]

    barrier = pltpu.get_barrier_semaphore()
    for step in range(1, parts):
        pl.semaphore_signal(
            barrier, inc=1, device_id={"gy": (me + step) % parts}, device_id_type=MESH
        )
    for to in (sib, opp, dia):
        pl.semaphore_signal(barrier, inc=1, device_id={"gx": to}, device_id_type=MESH)
    def take_rows(dest, src):
        value = src[...].astype(f32)
        if count < rows_pad:
            value = jnp.concatenate([value, jnp.zeros((rows_pad - count, width), f32)], axis=0)
        dest[me] = value.astype(bf)

    take_rows(tg, tok_ref)
    own_vectors = (
        gain1_ref,
        shift1_ref,
        bproj_ref,
        satt_ref,
        gain2_ref,
        shift2_ref,
        smlp_ref,
        bfc2_ref,
    )
    for at, ref in enumerate(own_vectors):
        vec_ref[at : at + 1, :] = ref[...].reshape(1, width)
    wqkv[pl.ds(pl.multiple_of(i * quarter, quarter), quarter), :] = qkv_ref[...]
    pl.semaphore_wait(barrier, parts + 2)

    ring_tok.start()
    gat_qkv.start()
    all_vecs.start()
    if sent_rows < rows_pad:
        for ref in (tg, cg, ag, hg):
            for at in range(parts):
                ref[at, sent_rows:rows_pad, :] = jnp.zeros((rows_pad - sent_rows, width), bf)
    vecs[me] = vec_ref[...]
    take_rows(cg, cot_ref)
    projg[i, me] = proj_ref[...]
    wfc1[pl.ds(pl.multiple_of(i * quarter, quarter), quarter), :] = fc1_ref[...]
    ring_tok.advance(0)
    lines = fc2_ref.shape[0] // 2
    part = lines // 2
    fc2_cross = take(2)
    crosses = [
        remote(
            fc2_ref.at[pl.ds(pl.multiple_of(block * lines + (1 - plane) * part, part), part)],
            fc2x.at[block],
            fc2_cross + block,
            fc2_cross + block,
            gx=opp,
        )
        for block in range(2)
    ]
    gat_qkv.forward()
    for cross in crosses:
        launch(cross)
    ring_tok.advance(1)
    gat_fc1.start()
    ring_tok.advance(2)
    ring_proj.start()
    gat_qkv.finish()
    ring_tok.advance(3) if half > 3 else None
    for step in range(4, half):
        ring_tok.advance(step)
    is_owner = core == (me // 2) % 2
    spread_send, spread_recv = take(4), take(parts)

    def fc2_copy(block):
        if block < 2:
            source = fc2_ref.at[pl.ds(pl.multiple_of(block * lines + plane * part, part), part)]
        else:
            source = fc2x.at[block - 2]
        target = 2 * (i if block < 2 else opp) + block % 2
        return target, source, remote(
            source, fc2h.at[plane, me], spread_send + block, spread_recv + me, gy=target
        )

    def spread_fc2():
        for cross in crosses:
            cross.wait_recv()
        for block in range(4):
            target, source, copy = fc2_copy(block)

            @pl.when(target != me)
            def _():
                copy.start()

            @pl.when(target == me)
            def _():
                fc2h[plane, me] = source[...]

    pass_sem = take(3)
    fc2_sib = remote(fc2h.at[plane], fc2h.at[plane], pass_sem, pass_sem, gx=sib)
    fc2_opp = remote(fc2h.at[plane], fc2h.at[plane], pass_sem + 1, pass_sem + 1, gx=opp)
    fc2_far = remote(fc2h.at[1 - plane], fc2h.at[1 - plane], pass_sem + 2, pass_sem + 2, gx=sib)

    def pass_fc2():
        @pl.when(is_owner)
        def _():
            for step in range(1, parts):
                other = (me + step) % parts
                ref = fc2h.at[plane, other]
                remote(ref, ref, spread_send, spread_recv + other, gy=other).wait_recv()
            fc2_opp.start()
            fc2_sib.start()

    def forward_fc2():
        @pl.when(is_owner)
        def _():
            fc2_opp.wait_recv()
            fc2_far.start()

    def finish_fc2():
        @pl.when(jnp.logical_not(is_owner))
        def _():
            fc2_sib.wait_recv()
            fc2_far.wait_recv()

        for at in range(parts):
            for piece in range(2):
                wfc2[piece * part : (piece + 1) * part, at * width : (at + 1) * width] = fc2h[piece, at]

    ring_cot.start()
    all_vecs.finish()

    GAIN1, SHIFT1, BPROJ, SATT, GAIN2, SHIFT2, SMLP = range(7)
    FC2B = 7

    def vec_block(block, which):
        return vecs[block, which : which + 1, :]

    def row_tile(number, size=tile):
        return pl.ds(pl.multiple_of(number * size, size), size)

    def normalise(blocks, gain, shift, rows, slot, dest):
        acc = blocks[0]
        for block in blocks[1:]:
            acc = acc + block
        row_mean = jnp.sum(acc, axis=1, keepdims=True) * (1.0 / full)
        blocks = [block - row_mean for block in blocks]
        acc = blocks[0] * blocks[0]
        for block in blocks[1:]:
            acc = acc + block * block
        inv = lax.rsqrt(jnp.sum(acc, axis=1, keepdims=True) * (1.0 / full) + EPS)
        for at in range(parts):
            value = blocks[at] * inv * vec_block(at, gain) + vec_block(at, shift)
            dest[rows, at * width : (at + 1) * width] = value.astype(bf)
        stat[slot, rows, :] = row_mean
        stat[slot + 1, rows, :] = inv

    @pl.loop(0, 4)
    def _(number):
        rows = row_tile(number)
        normalise([tg[at, rows, :].astype(f32) for at in range(parts)], GAIN1, SHIFT1, rows, 0, nb)

    qv_row = qv_ref[...].reshape(1, heads * 2 * HD)
    blank = jnp.zeros((1, HD), f32)
    pieces = []
    for head in range(heads):
        at = head * 2 * HD
        pieces += [qv_row[:, at : at + HD], blank, qv_row[:, at + HD : at + 2 * HD]]
    qkv_bias = jnp.concatenate(pieces, axis=1)
    lane = lax.broadcasted_iota(jnp.int32, (1, three), 1)
    qkv_scale = jnp.where(lane % (3 * HD) < HD, HD ** (-0.5), 1.0).astype(f32)

    @pl.loop(0, 2)
    def _(number):
        rows = row_tile(number, mid_row)
        mixed = dot_nn(nb[rows, :], wqkv[...])
        mixf[rows, :] = mixed
        qkvb[rows, :] = ((mixed + qkv_bias) * qkv_scale).astype(bf)

    kv_sem = take(1)
    kv_copy = remote(qkvb, qkvo, kv_sem, kv_sem, gx=sib)
    launch(kv_copy)
    ring_proj.advance(0)
    ring_proj.advance(1)
    ring_cot.advance(0)
    gat_fc1.forward()
    zero_half = jnp.zeros((qpad - rows_pad, 2 * HD), bf)
    for head in range(heads):
        at = head * 3 * HD
        query = qkvb[:, at : at + HD]
        qz[head, 0:rows_pad, :] = jnp.concatenate([query, jnp.zeros_like(query)], axis=1)
        qz[head, rows_pad:qpad, :] = zero_half
        kvc[head, 0:rows_pad, :] = qkvb[:, at + HD : at + 3 * HD]
    kv_copy.wait_recv()
    for head in range(heads):
        at = head * 3 * HD
        kvc[head, rows_pad : 2 * rows_pad, :] = qkvo[:, at + HD : at + 3 * HD]
        kvt[head] = jnp.transpose(kvc[head])
    ring_proj.advance(2)

    lo = count // 8 * 8
    qtile = 256
    qtiles = qpad // qtile

    def mask_keys(scores):
        pieces = []
        for base in (0, rows_pad):
            pieces.append(scores[base : base + lo])
            edge = scores[base + lo : base + rows_pad]
            index = lax.broadcasted_iota(jnp.int32, edge.shape, 0) + lo
            pieces.append(jnp.where(index < count, edge, -1e30))
        return jnp.concatenate(pieces, axis=0)

    def attend_tile(number):
        cols = slice(number * qtile, (number + 1) * qtile)
        for head in range(heads):
            scores = mask_keys(dot_nt(kvc[head], qz[head, cols, :]))
            top = jnp.max(scores, axis=0, keepdims=True)
            exponent = jnp.exp(scores - top)
            total = jnp.sum(exponent, axis=0, keepdims=True)
            probs = (exponent * (1.0 / total)).astype(bf)
            pt[head, :, cols] = probs
            result = dot_nn(kvt[head, HD : 2 * HD, :], probs).astype(bf)
            att[head * HD : (head + 1) * HD, cols] = result
        stop = min((number + 1) * qtile, rows_pad)
        got = jnp.transpose(att[:, cols])
        ag[me, number * qtile : stop, :] = got[0 : stop - number * qtile]

    sent_chunks = 0
    for number in range(qtiles):
        attend_tile(number)
        if number == 0:
            spread_fc2()
            gat_fc1.finish()
            for step in range(3, half):
                ring_proj.advance(step)
            gat_proj.start()
        if number == 1:
            ring_cot.advance(1)
        while sent_chunks < chunks and min(qpad, (number + 1) * qtile) >= sum(span(sent_chunks)):
            ring_att.start_chunk(sent_chunks)
            sent_chunks += 1
    pass_fc2()
    ring_att.advance(0)
    gat_proj.forward()
    ring_cot.advance(2)
    ring_att.advance(1)
    forward_fc2()
    for step in range(3, half):
        ring_cot.advance(step)

    @pl.loop(0, 4)
    def _(number):
        rows = row_tile(number)
        for at in range(parts):
            gm[rows, at * width : (at + 1) * width] = (
                cg[at, rows, :].astype(f32) * vec_block(at, SMLP)
            ).astype(bf)

    ring_att.advance(2)
    gat_proj.finish()
    for shard in range(4):
        for at in range(parts):
            wproj[shard * quarter : (shard + 1) * quarter, at * width : (at + 1) * width] = projg[shard, at]

    def weigh(which, weight):
        whole = jnp.concatenate([vec_block(at, which) for at in range(parts)], axis=1)
        high, low = split_high(jnp.broadcast_to(whole, (16, full)))
        return (dot_nn(high, weight) + dot_nn(low, weight))[0:1]

    gain_fc1 = weigh(GAIN2, wfc1[...])
    shift_fc1 = weigh(SHIFT2, wfc1[...])
    gain_qkv = weigh(GAIN1, wqkv[...])
    shift_qkv = weigh(SHIFT1, wqkv[...])
    for step in range(3, half - 1):
        ring_att.advance(step)
    finish_fc2()
    fc1_bias = bfc1_ref[...].reshape(1, hidden_width)
    cs_acc[...] = jnp.zeros_like(cs_acc)

    @pl.loop(0, 2)
    def _(number):
        rows = row_tile(number, mid_row)
        gh[rows, :] = dot_nt(gm[rows, :], wfc2[...])

    def fc1_rows(who):
        return wfc1[pl.ds(pl.multiple_of(who * width, width), width), :]

    scat_two = Scatter(0, gpb, fc1_rows, 0, dot_nt)

    def middle_tile(chunk):
        rows = slice(chunk * tile, (chunk + 1) * tile)
        whole = jnp.concatenate([ag[at, rows, :] for at in range(parts)], axis=1)
        result = dot_nn(whole, wproj[...])
        blocks = []
        for at in range(parts):
            attn = result[:, at * width : (at + 1) * width] + vec_block(at, BPROJ)
            ao[at, rows, :] = attn
            blocks.append(tg[at, rows, :].astype(f32) + vec_block(at, SATT) * attn)
        normalise(blocks, GAIN2, SHIFT2, rows, 2, nt)

    def mlp_tile(chunk):
        rows = slice(chunk * tile, (chunk + 1) * tile)
        raw = dot_nn(nt[rows, :], wfc1[...])
        act = raw + fc1_bias
        cdf = normal_cdf(act)
        hid[rows, :] = (act * cdf).astype(bf)
        slope = cdf + act * jnp.exp(-0.5 * act * act) * INV_ROOT_TAU
        grad = gh[rows, :] * slope
        cs_acc[...] += jnp.sum(grad.reshape(tile // 8, 8, hidden_width), axis=0)
        gpb[rows, :] = grad.astype(bf)
        prod[rows, 0:hidden_width] = (grad * (raw - shift_fc1)).astype(bf)

    for chunk in (0, 3, 1, 2):
        ring_att.last(chunk)
        middle_tile(chunk)
        mlp_tile(chunk)
        scat_two.open_chunk(chunk)

    def row_sums(slot, weights, grads, products):
        wide = grads.shape[1]
        high, low = split_high(jnp.broadcast_to(weights, (8, wide)))
        ones = jnp.ones((8, wide), bf)
        first = dot_nt(high, grads) + dot_nt(low, grads)
        second = dot_nt(ones, products)
        st_mine[slot, 0:1, 0:rows_pad] = first[0:1]
        st_mine[slot, 1:2, 0:rows_pad] = second[0:1]
        all_stats[slot].start()
        st_all[slot, me] = st_mine[slot]

    def total_sums(slot):
        all_stats[slot].finish()
        total = st_all[slot, 0]
        for at in range(1, parts):
            total = total + st_all[slot, at]
        st_sum[...] = jnp.zeros_like(st_sum)
        st_sum[0:2, :] = total
        turned = jnp.transpose(st_sum[...])
        return turned[0:rows_pad, 0:1] * (1.0 / full), turned[0:rows_pad, 1:2] * (1.0 / full)

    st_mine[...] = jnp.zeros_like(st_mine)
    row_sums(0, gain_fc1, gpb[...], prod[:, 0:hidden_width])
    def fc2_cols(who):
        return wfc2[:, pl.ds(pl.multiple_of(who * width, width), width)]

    scat_mlp = Scatter(1, hid, fc2_cols, 1, dot_nn)

    for step in range(1, half):
        scat_two.step(step)
        if step == 1:
            scat_mlp.step(0)
    scat_mlp.step(1)

    def fc2_grad(number):
        result = dot_tn(hid[...], gm[:, number * 256 : (number + 1) * 256]).astype(bf)
        for piece in range(2):
            for side in range(2):
                t2[piece, 2 * number + side] = result[
                    piece * part : (piece + 1) * part, side * width : (side + 1) * width
                ]

    for number in range(parts // 2):
        fc2_grad(number)
    sib_sem = take(1)
    t2_pass = remote(t2, t2s, sib_sem, sib_sem, gx=sib)

    @pl.when(jnp.logical_not(is_owner))
    def _():
        t2_pass.start()

    scat_two.term(half)
    first, second = total_sums(0)
    satt_own = vecs[me, SATT : SATT + 1, :]
    gain_own = vecs[me, GAIN2 : GAIN2 + 1, :]

    def col_sum(value):
        return jnp.sum(value, axis=0, keepdims=True)

    sm[...] = jnp.zeros_like(sm)
    for chunk in range(chunks):
        start, size = span(chunk)
        rows = slice(start, start + size)
        grad_two = scat_two.total(chunk)
        attn_own = ao[me, rows, :]
        mid_value = tg[me, rows, :].astype(f32) + satt_own * attn_own
        mid_own[rows, :] = mid_value
        inv_two = stat[3, rows, :]
        normed = (mid_value - stat[2, rows, :]) * inv_two
        grad_mid = cg[me, rows, :].astype(f32) + inv_two * (
            grad_two * gain_own - first[rows] - normed * second[rows]
        )
        gmid[rows, :] = grad_mid
        grad_attn = grad_mid * satt_own
        hg[me, rows, :] = grad_attn.astype(bf)
        ring_grad.start_chunk(chunk)
        sm[5:6, :] += col_sum(grad_attn)
        sm[6:7, :] += col_sum(grad_mid * attn_own)
        sm[7:8, :] += col_sum(grad_two * normed)
        sm[8:9, :] += col_sum(grad_two)
    if sent_rows < rows_pad:
        for ref in (mid_own, gmid):
            ref[sent_rows:rows_pad, :] = jnp.zeros((rows_pad - sent_rows, width), f32)
    fc1_sum = col_sum(cs_acc[...])
    for at in range(hidden_width // width):
        sm[16 + at : 17 + at, :] = fc1_sum[:, at * width : (at + 1) * width]

    scat_mlp.step(2)

    def rows_grad(dest, left_of, grads):
        for shard in range(4):
            dest[shard % 2, shard // 2] = dot_tn(left_of(shard), grads).astype(bf)

    rows_grad(t1, lambda shard: nt[:, shard * quarter : (shard + 1) * quarter], gpb[...])
    sum_fc1.start()
    ring_grad.advance(0)
    blocks_in = quarter // width
    rows_grad(
        tp,
        lambda shard: jnp.concatenate(
            [ag[shard * blocks_in + b] for b in range(blocks_in)], axis=1
        ),
        hg[me],
    )
    sum_proj.start()
    sum_fc1.cross()

    t2_recv = take(parts)
    t2_send = take(parts)

    def t2_copy(step):
        to = (me + step) % parts
        return remote(t2d.at[to], t2r.at[me], t2_send + step, t2_recv + me, gy=to)

    plane_sem = take(1)
    t2_plane = remote(t2c, t2o, plane_sem, plane_sem, gx=opp)

    @pl.when(is_owner)
    def _():
        t2_pass.wait_recv()
        for at in range(parts):
            t2c[at] = (t2[1 - plane, at].astype(f32) + t2s[1 - plane, at].astype(f32)).astype(bf)
        t2_plane.start()

    ring_grad.advance(1)
    sum_proj.cross()
    ring_grad.advance(2)
    for step in range(3, half):
        ring_grad.advance(step)
    own_rows = pl.ds(pl.multiple_of(me * width, width), width)

    @pl.loop(0, 4)
    def _(number):
        rows = row_tile(number)
        whole = jnp.concatenate([hg[at, rows, :] for at in range(parts)], axis=1)
        gat[rows, :] = dot_nt(whole, wproj[own_rows, :]).astype(bf)

    gat[rows_pad:qpad, :] = jnp.zeros((qpad - rows_pad, 2 * HD), bf)
    for step in range(3, half):
        scat_mlp.step(step)
    gatt = jnp.transpose(gat[...])
    delta_all = gatt.astype(f32) * att[...].astype(f32)
    for head in range(heads):
        value = gat[:, head * HD : (head + 1) * HD]
        dz[head] = jnp.concatenate([jnp.zeros_like(value), value], axis=1)
    deltas = [
        jnp.sum(delta_all[head * HD : (head + 1) * HD], axis=0, keepdims=True) for head in range(heads)
    ]
    dkv[...] = jnp.zeros_like(dkv)

    def attend_back(number, side):
        cols = slice(number * qtile, (number + 1) * qtile)
        keys = slice(side * rows_pad, (side + 1) * rows_pad)
        for head in range(heads):
            probs = pt[head, keys, cols]
            query, grad = qz[head, cols, :], dz[head, cols, :]
            slope = dot_nt(kvc[head, keys, :], grad)
            scores = (probs.astype(f32) * (slope - deltas[head][:, cols])).astype(bf)
            dkv[head, keys, :] += dot_nn(probs, grad) + dot_nn(scores, query)
            part_query = dot_nn(kvt[head, 0:HD, keys], scores)
            here = slice(head * HD, (head + 1) * HD)
            if side == 1:
                dqf[here, cols] = part_query
            else:
                dqf[here, cols] += part_query

    def spread_t2():
        @pl.when(is_owner)
        def _():
            t2_plane.wait_recv()
            for at in range(parts):
                t2d[at] = (
                    t2[plane, at].astype(f32) + t2s[plane, at].astype(f32) + t2o[at].astype(f32)
                ).astype(bf)
            for step in range(1, parts):
                t2_copy(step).start()
            t2r[me] = t2d[me]

    for number in range(qtiles):
        attend_back(number, 1)
        if number == 1:
            spread_t2()
    for head in range(heads):
        dks[head] = dkv[head, rows_pad : 2 * rows_pad, :].astype(bf)
    dk_sem = take(1)
    dk_copy = remote(dks, dkr, dk_sem, dk_sem, gx=sib)
    launch(dk_copy)
    for number in range(qtiles):
        attend_back(number, 0)

    grad_query = jnp.transpose(dqf[...])[0:rows_pad] * (HD ** (-0.5))
    sm[0:1, :] = col_sum(grad_query)
    dk_copy.wait_recv()
    pieces = []
    value_sums = []
    for head in range(heads):
        own = dkv[head, 0:rows_pad, :] + dkr[head].astype(f32)
        value_sums.append(col_sum(own))
        pieces += [grad_query[:, head * HD : (head + 1) * HD], own]
    for head in range(heads):
        sm[1 + head : 2 + head, :] = value_sums[head]
    mixed_grad = jnp.concatenate(pieces, axis=1)
    gmx[...] = mixed_grad.astype(bf)
    prod[:, 0:three] = (mixed_grad * (mixf[...] - shift_qkv)).astype(bf)

    def qkv_rows(who):
        return wqkv[pl.ds(pl.multiple_of(who * width, width), width), :]

    scat_one = Scatter(2, gmx, qkv_rows, 0, dot_nt)
    scat_one.step(0)
    row_sums(1, gain_qkv, gmx[...], prod[:, 0:three])
    rows_grad(tq, lambda shard: nb[:, shard * quarter : (shard + 1) * quarter], gmx[...])
    sum_qkv.start()
    scat_one.step(1)

    scat_mlp.term(half)
    mlp_out = scat_mlp.finish() + vecs[me, FC2B : FC2B + 1, :]
    smlp_own = vecs[me, SMLP : SMLP + 1, :]
    up = cg[me].astype(f32)
    out_ref[...] = (mid_own[...] + smlp_own * mlp_out)[0:count]
    sm[9:10, :] = col_sum(up * smlp_own)
    sm[10:11, :] = col_sum(up * mlp_out)
    sum_qkv.cross()
    for step in range(2, half):
        scat_one.step(step)
    sum_fc1.finish()
    sum_proj.finish()

    for step in range(4):
        source = (step // 2) * (parts // 2) + 2 * core + step % 2

        @pl.when(source != me)
        def _():
            remote(t2d.at[me], t2r.at[source], t2_send, t2_recv + source, gy=source).wait_recv()

    x_sem = take(1)
    t2_cross = remote(t2r.at[pl.ds(2 * opp, 2)], t2x, x_sem, x_sem, gx=opp)
    launch(t2_cross)
    scat_one.term(half)
    t2_cross.wait_recv()
    for block in range(2):
        for at, value in ((plane, t2r[2 * i + block]), (1 - plane, t2x[block])):
            rows = pl.ds(pl.multiple_of(block * lines + at * part, part), part)
            gfc2_ref[rows, :] = value.astype(f32)
    sum_qkv.finish()

    grad_one = scat_one.finish()
    first, second = total_sums(1)
    inv_one = stat[1]
    normed = (tg[me].astype(f32) - stat[0]) * inv_one
    gain_own = vecs[me, GAIN1 : GAIN1 + 1, :]
    gin_ref[...] = (gmid[...] + inv_one * (grad_one * gain_own - first - normed * second))[0:count]
    sm[3:4, :] = col_sum(grad_one * normed)
    sm[4:5, :] = col_sum(grad_one)
    sma[i] = sm[...]
    small_sem = take(3)
    copies = [
        remote(sm, sma.at[i], small_sem + n, small_sem + n, gx=to)
        for n, to in enumerate((sib, opp, dia))
    ]
    for copy in copies:
        launch(copy)
    for copy in copies:
        copy.wait_recv()
    small_ref[...] = sma[0] + sma[1] + sma[2] + sma[3]

    for copy in started:
        copy.wait_send()
    for block in range(4):
        target, _, copy = fc2_copy(block)

        @pl.when(target != me)
        def _():
            copy.wait_send()

    @pl.when(is_owner)
    def _():
        fc2_opp.wait_send()
        fc2_sib.wait_send()
        fc2_far.wait_send()
        t2_plane.wait_send()
        for step in range(1, parts):
            t2_copy(step).wait_send()

    @pl.when(jnp.logical_not(is_owner))
    def _():
        t2_pass.wait_send()


def emit_kernel(heads, hidden_width, small_ref, *refs):
    sources, results = refs[:6], refs[6:22]
    for source, result in zip(sources, results):
        result[...] = source[...]
    qv_ref, fc1_ref = results[6:8]
    width = small_ref.shape[1]
    for head in range(heads):
        row = jnp.concatenate(
            [small_ref[0:1, head * HD : (head + 1) * HD], small_ref[1 + head : 2 + head, HD : 2 * HD]],
            axis=1,
        )
        qv_ref[head * 2 * HD : (head + 1) * 2 * HD] = row.reshape(2 * HD)
    for at in range(hidden_width // width):
        fc1_ref[at * width : (at + 1) * width] = small_ref[16 + at : 17 + at, :].reshape(width)
    for at, ref in enumerate(results[8:]):
        ref[...] = small_ref[3 + at : 4 + at, :].reshape(width)


def on_device(*args):
    (
        tokens,
        cotangent,
        norm1_gain,
        norm1_shift,
        qkv_weight,
        qv_bias,
        proj_weight,
        proj_bias,
        scale_attn,
        norm2_gain,
        norm2_shift,
        fc1_weight,
        fc1_bias,
        fc2_weight,
        fc2_bias,
        scale_mlp,
    ) = args
    parts, rows_over = lax.axis_size("gy"), lax.axis_size("gx")
    count, width = tokens.shape
    heads = qkv_weight.shape[1] // (3 * HD)
    hidden_width = fc1_weight.shape[1]
    if (
        rows_over != 4
        or parts != 8
        or width != 128
        or heads != 2
        or IMGS != 1
        or hidden_width % 256
    ):
        return on_device_plain(*args)
    full = parts * width
    rows = up_to(count, 64)
    qpad = up_to(rows, 256)
    three = heads * 3 * HD
    quarter = full // 4
    lines = fc2_weight.shape[0] // 2
    half = parts // 2
    bf, f32 = jnp.bfloat16, jnp.float32
    wide = max(three, hidden_width)
    stat_wide = up_to(rows, 256)
    V = pltpu.VMEM
    scratch = [
        V((parts, rows, width), bf),
        V((parts, rows, width), bf),
        V((parts, rows, width), bf),
        V((parts, rows, width), bf),
        V((parts, 8, width), f32),
        V((full, three), bf),
        V((full, hidden_width), bf),
        V((4, parts, quarter, width), bf),
        V((full, full), bf),
        V((2, lines // 2, width), bf),
        V((2, parts, lines // 2, width), bf),
        V((lines, full), bf),
        V((rows, full), bf),
        V((rows, full), bf),
        V((rows, full), bf),
        V((4, rows, 1), f32),
        V((rows, three), f32),
        V((rows, three), bf),
        V((rows, three), bf),
        V((heads, 2 * rows, 2 * HD), bf),
        V((heads, 2 * HD, 2 * rows), bf),
        V((heads, qpad, 2 * HD), bf),
        V((heads, qpad, 2 * HD), bf),
        V((heads, 2 * rows, qpad), bf),
        V((heads * HD, qpad), bf),
        V((8, width), f32),
        V((parts, rows, width), f32),
        V((rows, hidden_width), f32),
        V((rows, hidden_width), bf),
        V((rows, hidden_width), bf),
        V((rows, wide), bf),
        V((rows, 2 * width), f32),
        V((3, 2, half, rows, width), bf),
        V((3, 2, half, rows, width), bf),
        V((2, 2, stat_wide), f32),
        V((2, parts, 2, stat_wide), f32),
        V((8, stat_wide), f32),
        V((rows, width), f32),
        V((rows, width), f32),
        V((qpad, width), bf),
        V((heads, 2 * rows, 2 * HD), f32),
        V((heads, rows, 2 * HD), bf),
        V((heads, rows, 2 * HD), bf),
        V((heads * HD, qpad), f32),
        V((rows, three), bf),
        V((2, 2, quarter, three), bf),
        V((2, quarter, three), bf),
        V((quarter, three), bf),
        V((quarter, three), bf),
        V((2, 2, quarter, width), bf),
        V((2, quarter, width), bf),
        V((quarter, width), bf),
        V((quarter, width), bf),
        V((2, 2, quarter, hidden_width), bf),
        V((2, quarter, hidden_width), bf),
        V((quarter, hidden_width), bf),
        V((quarter, hidden_width), bf),
        V((2, parts, lines // 2, width), bf),
        V((2, parts, lines // 2, width), bf),
        V((parts, lines // 2, width), bf),
        V((parts, lines // 2, width), bf),
        V((parts, lines // 2, width), bf),
        V((parts, lines // 2, width), bf),
        V((2, lines // 2, width), bf),
        V((24, width), f32),
        V((4, 24, width), f32),
        V((8, hidden_width), f32),
        pltpu.SemaphoreType.DMA((SEMS,)),
        pltpu.SemaphoreType.DMA((SEMS,)),
    ]
    vmem = pl.BlockSpec(memory_space=pltpu.VMEM)
    results = pl.pallas_call(
        functools.partial(mega_kernel, parts, count, heads, hidden_width, SEMS),
        out_shape=[
            jax.ShapeDtypeStruct((count, width), f32),
            jax.ShapeDtypeStruct((count, width), f32),
            jax.ShapeDtypeStruct((24, width), f32),
            jax.ShapeDtypeStruct((quarter, three), f32),
            jax.ShapeDtypeStruct((quarter, width), f32),
            jax.ShapeDtypeStruct((quarter, hidden_width), f32),
            jax.ShapeDtypeStruct((2 * lines, width), f32),
        ],
        in_specs=[vmem] * 16,
        out_specs=[vmem] * 7,
        scratch_shapes=scratch,
        compiler_params=pltpu.CompilerParams(
            collective_id=3, has_side_effects=True, vmem_limit_bytes=VMEM_BYTES
        ),
    )(
        tokens,
        cotangent,
        norm1_gain,
        norm1_shift,
        qkv_weight,
        qv_bias,
        proj_weight,
        proj_bias,
        scale_attn,
        norm2_gain,
        norm2_shift,
        fc1_weight,
        fc1_bias,
        fc2_weight,
        fc2_bias,
        scale_mlp,
    )
    output, grad_in, small, grad_qkv, grad_proj, grad_fc1, grad_fc2 = results
    line = jax.ShapeDtypeStruct((width,), f32)
    large = [output, grad_in, grad_qkv, grad_proj, grad_fc1, grad_fc2]
    written = pl.pallas_call(
        functools.partial(emit_kernel, heads, hidden_width),
        out_shape=[jax.ShapeDtypeStruct(array.shape, f32) for array in large]
        + [
            jax.ShapeDtypeStruct((heads * 2 * HD,), f32),
            jax.ShapeDtypeStruct((hidden_width,), f32),
        ]
        + [line] * 8,
        in_specs=[vmem] * 7,
        out_specs=[vmem] * 16,
    )(small, *large)
    output, grad_in, grad_qkv, grad_proj, grad_fc1, grad_fc2, grad_qv, grad_fc1_bias = written[:8]
    lines_out = written[8:]
    return (
        output,
        grad_in,
        lines_out[0],
        lines_out[1],
        grad_qkv,
        grad_qv,
        grad_proj,
        lines_out[2],
        lines_out[3],
        lines_out[4],
        lines_out[5],
        grad_fc1,
        grad_fc1_bias,
        grad_fc2,
        lines_out[6],
        lines_out[7],
    )


def solution(mesh):
    return jax.shard_map(
        on_device,
        mesh=mesh,
        in_specs=(
            P("gx", "gy"),
            P("gx", "gy"),
            P("gy"),
            P("gy"),
            P("gx", "gy"),
            P("gy"),
            P("gx", "gy"),
            P("gy"),
            P("gy"),
            P("gy"),
            P("gy"),
            P("gx", "gy"),
            P("gy"),
            P("gx", "gy"),
            P("gy"),
            P("gy"),
        ),
        out_specs=(
            P("gx", "gy"),
            P("gx", "gy"),
            P("gy"),
            P("gy"),
            P("gx", "gy"),
            P("gy"),
            P("gx", "gy"),
            P("gy"),
            P("gy"),
            P("gy"),
            P("gy"),
            P("gx", "gy"),
            P("gy"),
            P("gx", "gy"),
            P("gy"),
            P("gy"),
        ),
        check_vma=False,
    )
```
